32 devices in a mesh: fsdp: 16 (over z, y, core), tp: 2 (over x).
Axes of the slice: x: 2, y: 2, z: 4, core: 2. Of those that a mesh axis runs over, the one named last changes fastest.
Arguments:
- tokens: bfloat16 [32768, 768], P(('fsdp', 'tp')), may hold values from -6 to 6
- lengths: int32 [64], P('fsdp'), may hold values from 32 to 512, as said below
- cotangent: bfloat16 [32768, 768], P(('fsdp', 'tp')), may hold values from -6 to 6
- w_query: float32 [768, 768], P('fsdp', 'tp'), may hold values from -0.21875 to 0.21875
- w_key: float32 [768, 768], P('fsdp', 'tp'), may hold values from -0.21875 to 0.21875
- w_value: float32 [768, 768], P('fsdp', 'tp'), may hold values from -0.21875 to 0.21875
- w_output: float32 [768, 768], P('tp', 'fsdp'), may hold values from -1.75 to 1.75
- w_inner: float32 [768, 3072], P('fsdp', 'tp'), may hold values from -0.21875 to 0.21875
- w_outer: float32 [3072, 768], P('tp', 'fsdp'), may hold values from -0.109375 to 0.109375
- bias_query: float32 [768], P('tp'), may hold values from -3 to 3
- bias_value: float32 [768], P('tp'), may hold values from -3 to 3
- bias_output: float32 [768], replicated, may hold values from -3 to 3
- norm1_gain: float32 [768], replicated, may hold values from 0.25 to 1.75
- norm1_bias: float32 [768], replicated, may hold values from -3 to 3
- bias_inner: float32 [3072], P('tp'), may hold values from -3 to 3
- bias_outer: float32 [768], replicated, may hold values from -3 to 3
- norm2_gain: float32 [768], replicated, may hold values from 0.25 to 1.75
- norm2_bias: float32 [768], replicated, may hold values from -3 to 3
Outputs:
- mixed_out: bfloat16 [32768, 768], P(('fsdp', 'tp'))
- grad_tokens: float32 [32768, 768], P(('fsdp', 'tp'))
- grad_w_query: float32 [768, 768], P('fsdp', 'tp')
- grad_w_key: float32 [768, 768], P('fsdp', 'tp')
- grad_w_value: float32 [768, 768], P('fsdp', 'tp')
- grad_w_output: float32 [768, 768], P('tp', 'fsdp')
- grad_w_inner: float32 [768, 3072], P('fsdp', 'tp')
- grad_w_outer: float32 [3072, 768], P('tp', 'fsdp')
- grad_bias_query: float32 [768], P('tp')
- grad_bias_value: float32 [768], P('tp')
- grad_bias_output: float32 [768], replicated
- grad_norm1_gain: float32 [768], replicated
- grad_norm1_bias: float32 [768], replicated
- grad_bias_inner: float32 [3072], P('tp')
- grad_bias_outer: float32 [768], replicated
- grad_norm2_gain: float32 [768], replicated
- grad_norm2_bias: float32 [768], replicated
The draws below stay inside these ranges and needn't reach their ends.
Inputs may be any that keep to these rules, and one draw needn't show every extreme that they name: `lengths`: the number of leading tokens of each sequence that are not padding; keys at later positions are masked for every query.
All inputs are finite; a program needn't handle non-finite values.
Results may differ from the reference program's by a relative error of at most 0.014.
The reference program's roundings to bfloat16 on the way count: a program that leaves them out, or rounds other values in their place, can miss the bound.
Values may be sent and summed in bfloat16 or wider, within the bound.
No kernel may reach another device: no remote copies, remote signals or barrier semaphores. Data moves between devices by JAX's collectives and lax.ppermute only.
A program may use at most 192 MiB of HBM per device.

```python
import jax
import jax.numpy as jnp
from jax import lax

D = 768
HEADS = 12
DH = 64
FF = 3072
SEQ = 512
SEQ_DEV = 4
SEQS = 64
TOKENS = 32768


def draw_lengths(key, part):
    raw = jax.random.randint(key, (SEQS,), 0, 3 * SEQ, dtype=jnp.int32) - SEQ // 2
    return jnp.clip(raw, SEQ // 16, SEQ).astype(jnp.int32)


def shard_levels(key, shape, split, smallest, largest):
    def one(position, blocks):
        heights = jax.random.uniform(jax.random.fold_in(jax.random.fold_in(key, 6), position), (blocks,), jnp.float32, smallest / len(split), largest / len(split))
        return jnp.repeat(jnp.exp(heights), shape[position] // blocks).reshape((-1,) + (1,) * (len(shape) - position - 1))

    level = one(*split[0])
    for cut in split[1:]:
        level = level * one(*cut)
    return level


def noise(own_key, shape, deviation, limit, cuts=(), kind=jnp.bfloat16):
    drawn = deviation * jax.random.normal(own_key, shape, jnp.float32)
    if cuts:
        drawn = drawn * shard_levels(own_key, shape, cuts, -0.22, 0.18)
    return jnp.clip(drawn, -limit, limit).astype(kind)


def setup_inputs(seed: int = 0) -> dict:
    arg_keys = jax.random.split(jax.random.key(seed), 19)
    return {
        "tokens": noise(arg_keys[0], (TOKENS, D), 1.0, 6.0, ((0, 32),)),
        "lengths": draw_lengths(jax.random.fold_in(arg_keys[18], 71), 0),
        "cotangent": noise(arg_keys[2], (TOKENS, D), 1.0, 6.0, ((0, 32),)),
        "w_query": noise(arg_keys[3], (D, D), D ** -0.5, 0.21875, ((0, 16), (1, 2)), jnp.float32),
        "w_key": noise(arg_keys[4], (D, D), D ** -0.5, 0.21875, ((0, 16), (1, 2)), jnp.float32),
        "w_value": noise(arg_keys[5], (D, D), D ** -0.5, 0.21875, ((0, 16), (1, 2)), jnp.float32),
        "w_output": noise(arg_keys[6], (D, D), (D // 64) ** -0.5, 1.75, ((0, 2), (1, 16)), jnp.float32),
        "w_inner": noise(arg_keys[7], (D, FF), D ** -0.5, 0.21875, ((0, 16), (1, 2)), jnp.float32),
        "w_outer": noise(arg_keys[8], (FF, D), FF ** -0.5, 0.109375, ((0, 2), (1, 16)), jnp.float32),
        "bias_query": noise(arg_keys[9], (D,), 0.5, 3.0, ((0, 2),), jnp.float32),
        "bias_value": noise(arg_keys[10], (D,), 0.5, 3.0, ((0, 2),), jnp.float32),
        "bias_output": noise(arg_keys[11], (D,), 0.3, 3.0, (), jnp.float32),
        "norm1_gain": jnp.clip(1.0 + 0.15 * jax.random.normal(arg_keys[12], (D,), jnp.float32), 0.25, 1.75),
        "norm1_bias": noise(arg_keys[13], (D,), 0.3, 3.0, (), jnp.float32),
        "bias_inner": noise(arg_keys[14], (FF,), 0.3, 3.0, ((0, 2),), jnp.float32),
        "bias_outer": noise(arg_keys[15], (D,), 0.3, 3.0, (), jnp.float32),
        "norm2_gain": jnp.clip(1.0 + 0.15 * jax.random.normal(arg_keys[16], (D,), jnp.float32), 0.25, 1.75),
        "norm2_bias": noise(arg_keys[17], (D,), 0.3, 3.0, (), jnp.float32),
    }


@jax.custom_vjp
def low(v):
    return lax.optimization_barrier(v.astype(jnp.bfloat16)).astype(jnp.float32)

@jax.custom_vjp
def low_back(v):
    return v

def low_keep(v):
    return (low(v), None)

def low_pass(kept, grad):
    return (grad,)

def back_keep(v):
    return (v, None)

def back_low(kept, grad):
    return (low(grad),)
low.defvjp(low_keep, low_pass)
low_back.defvjp(back_keep, back_low)
norm_eps = 1e-12

def matmul(left, right):
    return jnp.dot(left, right, precision=lax.Precision.HIGHEST, preferred_element_type=jnp.float32)

def norm_rows(values, gain, shift):
    row_mean = lax.optimization_barrier(jnp.mean(values, axis=-1, keepdims=True))
    centred = values - row_mean
    row_var = lax.optimization_barrier(jnp.mean(centred * centred, axis=-1, keepdims=True))
    return centred * lax.rsqrt(row_var + norm_eps) * gain + shift

def attend(pieces):
    query, key_rows, value, length = pieces
    scores = low_back(jnp.einsum('qhd,khd->hqk', query, key_rows, precision=lax.Precision.HIGHEST) * DH ** (-0.5))
    live = jnp.arange(SEQ) < length
    scores = jnp.where(live[None, None, :], scores, -1000000000.0)
    probs = low(jax.nn.softmax(scores, axis=-1))
    return jnp.einsum('hqk,khd->qhd', probs, value, precision=lax.Precision.HIGHEST)

def layer(params, inputs, group_lengths):
    w_query, w_key, w_value, w_output, w_inner, w_outer, bias_query, bias_value, bias_output, norm1_gain, norm1_bias, bias_inner, bias_outer, norm2_gain, norm2_bias = params
    row_total = inputs.shape[0]
    query = low(low_back(matmul(inputs, low(w_query)) + bias_query))
    key_rows = low(low_back(matmul(inputs, low(w_key))))
    value = low(low_back(matmul(inputs, low(w_value)) + bias_value))
    shape_four = (row_total // SEQ, SEQ, HEADS, DH)
    context = lax.map(jax.checkpoint(attend), (query.reshape(shape_four), key_rows.reshape(shape_four), value.reshape(shape_four), group_lengths))
    context = low(low_back(context.reshape(row_total, D)))
    attention = low_back(matmul(context, low(w_output)))
    summed = attention + bias_output + inputs
    normed = norm_rows(summed, norm1_gain, norm1_bias)
    inner = low_back(matmul(low(normed), low(w_inner)) + bias_inner)
    hidden = low(jax.nn.gelu(inner, approximate=False))
    ffn_out = low_back(matmul(hidden, low(w_outer)))
    before_norm = ffn_out + bias_outer + normed
    return norm_rows(before_norm, norm2_gain, norm2_bias)

def reference(tokens, lengths, cotangent, w_query, w_key, w_value, w_output, w_inner, w_outer, bias_query, bias_value, bias_output, norm1_gain, norm1_bias, bias_inner, bias_outer, norm2_gain, norm2_bias):
    params = (w_query, w_key, w_value, w_output, w_inner, w_outer, bias_query, bias_value, bias_output, norm1_gain, norm1_bias, bias_inner, bias_outer, norm2_gain, norm2_bias)
    params = tuple((param.astype(jnp.float32) for param in params))
    groups = SEQS // SEQ_DEV
    group_rows = SEQ_DEV * SEQ
    inputs_all = tokens.astype(jnp.float32).reshape(groups, group_rows, D)
    cotan_all = cotangent.astype(jnp.float32).reshape(groups, group_rows, D)
    lengths_all = lengths.astype(jnp.int32).reshape(groups, SEQ_DEV)

    def one_group(totals, pieces):
        inputs, cotan, group_lengths = pieces

        def forward(param_set, values):
            return layer(param_set, values, group_lengths)
        output, pull = jax.vjp(forward, params, inputs)
        grad_params, grad_inputs = pull(cotan)
        totals = jax.tree.map(lambda left, right: left + right, totals, grad_params)
        return (totals, (output, grad_inputs))
    zeros = tuple((jnp.zeros_like(param) for param in params))
    grads, (outputs, grad_inputs) = lax.scan(one_group, zeros, (inputs_all, cotan_all, lengths_all))
    mixed_out = outputs.reshape(TOKENS, D).astype(jnp.bfloat16)
    grad_tokens = grad_inputs.reshape(TOKENS, D)
    return (mixed_out, grad_tokens, grads[0], grads[1], grads[2], grads[3], grads[4], grads[5], grads[6], grads[7], grads[8], grads[9], grads[10], grads[11], grads[12], grads[13], grads[14])
```

```python
import functools

import jax
import jax.numpy as jnp
import numpy as np
from jax import lax
from jax.experimental import pallas as pl
from jax.experimental.pallas import tpu as pltpu
from jax.sharding import PartitionSpec as P

DH = 64
SEQ = 512
PAIR = 2 * DH
norm_eps = 1e-12
masked_score = -1000000000.0
bf16 = jnp.bfloat16
f32 = jnp.float32


def dot_nn(left, right):
    return lax.dot_general(left, right, (((1,), (0,)), ((), ())), preferred_element_type=f32)


def dot_nt(left, right):
    return lax.dot_general(left, right, (((1,), (1,)), ((), ())), preferred_element_type=f32)


def dot_tn(left, right):
    return lax.dot_general(left, right, (((0,), (0,)), ((), ())), preferred_element_type=f32)


def head_slice(block, head):
    return block[:, head * DH : (head + 1) * DH]


def live_rows(lengths_ref):
    rows = lax.broadcasted_iota(jnp.int32, (SEQ, 1), 0)
    return rows < lengths_ref[pl.program_id(0)]


def attend_forward_kernel(pairs, lengths_ref, qkv_ref, context_ref, lse_ref):
    live = live_rows(lengths_ref)
    width = pairs * PAIR

    def one_pair(index, carry):
        at = pl.multiple_of(index * PAIR, PAIR)
        query = qkv_ref[:, pl.ds(at, PAIR)] * jnp.asarray(DH ** (-0.5), bf16)
        keys = qkv_ref[:, pl.ds(width + at, PAIR)]
        values = qkv_ref[:, pl.ds(2 * width + at, PAIR)]
        turned = []
        for head in range(2):
            scores = dot_nt(head_slice(keys, head), head_slice(query, head))
            scores = jnp.where(live, scores, masked_score)
            top = jnp.max(scores, axis=0, keepdims=True)
            expo = jnp.exp(scores - top)
            total = jnp.sum(expo, axis=0, keepdims=True)
            probs = (expo * (1.0 / total)).astype(bf16)
            turned.append(dot_tn(head_slice(values, head), probs))
            lse_ref[0, pl.ds(index * 2 + head, 1), :] = top + jnp.log(total)
        context_ref[:, pl.ds(at, PAIR)] = jnp.concatenate(turned, axis=0).T.astype(bf16)
        return carry

    lax.fori_loop(0, pairs, one_pair, 0)


def attend_forward(qkv, lengths):
    rows, triple = qkv.shape
    width = triple // 3
    seqs, pairs = rows // SEQ, width // PAIR
    heads = 2 * pairs
    return pl.pallas_call(
        functools.partial(attend_forward_kernel, pairs),
        grid_spec=pltpu.PrefetchScalarGridSpec(
            num_scalar_prefetch=1,
            grid=(seqs,),
            in_specs=[pl.BlockSpec((SEQ, triple), lambda s, n: (s, 0))],
            out_specs=[
                pl.BlockSpec((SEQ, width), lambda s, n: (s, 0)),
                pl.BlockSpec((1, heads, SEQ), lambda s, n: (s, 0, 0)),
            ],
        ),
        out_shape=[
            jax.ShapeDtypeStruct((rows, width), bf16),
            jax.ShapeDtypeStruct((seqs, heads, SEQ), f32),
        ],
        compiler_params=pltpu.CompilerParams(vmem_limit_bytes=20 << 20),
        cost_estimate=pl.CostEstimate(
            flops=8 * rows * SEQ * width, bytes_accessed=rows * width * 8, transcendentals=rows * SEQ * heads
        ),
        name="attend_forward",
    )(lengths, qkv)


def attend_backward_kernel(pairs, lengths_ref, qkv_ref, context_ref, d_context_ref, lse_ref, out_ref):
    live = live_rows(lengths_ref)
    width = pairs * PAIR
    scale = DH ** (-0.5)

    def one_pair(index, carry):
        at = pl.multiple_of(index * PAIR, PAIR)
        query = qkv_ref[:, pl.ds(at, PAIR)] * jnp.asarray(scale, bf16)
        keys = qkv_ref[:, pl.ds(width + at, PAIR)]
        values = qkv_ref[:, pl.ds(2 * width + at, PAIR)]
        d_context = d_context_ref[:, pl.ds(at, PAIR)]
        weighed = (context_ref[:, pl.ds(at, PAIR)].astype(f32) * d_context.astype(f32)).T
        d_query, d_key, d_value = [], [], []
        for head in range(2):
            q_h, k_h, v_h = head_slice(query, head), head_slice(keys, head), head_slice(values, head)
            g_h = head_slice(d_context, head)
            row_dot = jnp.sum(weighed[head * DH : (head + 1) * DH], axis=0, keepdims=True)
            scores = jnp.where(live, dot_nt(k_h, q_h), masked_score)
            probs = jnp.exp(scores - lse_ref[0, pl.ds(index * 2 + head, 1), :])
            d_probs = dot_nt(v_h, g_h)
            d_scores = (probs * (d_probs - row_dot)).astype(bf16)
            d_value.append(dot_nn(probs.astype(bf16), g_h))
            d_key.append(dot_nn(d_scores, q_h))
            d_query.append(dot_tn(k_h, d_scores))
        turned = jnp.concatenate(d_query, axis=0).T * scale
        out_ref[:, pl.ds(at, PAIR)] = turned.astype(bf16)
        out_ref[:, pl.ds(width + at, PAIR)] = jnp.concatenate(d_key, axis=1).astype(bf16)
        out_ref[:, pl.ds(2 * width + at, PAIR)] = jnp.concatenate(d_value, axis=1).astype(bf16)
        return carry

    lax.fori_loop(0, pairs, one_pair, 0)


def attend_backward(qkv, context, d_context, lse, lengths):
    rows, triple = qkv.shape
    width = triple // 3
    seqs, pairs = rows // SEQ, width // PAIR
    heads = 2 * pairs
    return pl.pallas_call(
        functools.partial(attend_backward_kernel, pairs),
        grid_spec=pltpu.PrefetchScalarGridSpec(
            num_scalar_prefetch=1,
            grid=(seqs,),
            in_specs=[
                pl.BlockSpec((SEQ, triple), lambda s, n: (s, 0)),
                pl.BlockSpec((SEQ, width), lambda s, n: (s, 0)),
                pl.BlockSpec((SEQ, width), lambda s, n: (s, 0)),
                pl.BlockSpec((1, heads, SEQ), lambda s, n: (s, 0, 0)),
            ],
            out_specs=pl.BlockSpec((SEQ, triple), lambda s, n: (s, 0)),
        ),
        out_shape=jax.ShapeDtypeStruct((rows, triple), bf16),
        compiler_params=pltpu.CompilerParams(vmem_limit_bytes=24 << 20),
        cost_estimate=pl.CostEstimate(
            flops=20 * rows * SEQ * width, bytes_accessed=rows * width * 16, transcendentals=rows * SEQ * heads
        ),
        name="attend_backward",
    )(lengths, qkv, context, d_context, lse)


class Exchange:
    def __init__(self, fsdp):
        self.fsdp = fsdp
        bits = [1 << i for i in range(fsdp.bit_length() - 1)]
        self.far = [bit for bit in bits if bit > 2]
        self.stages = self.far + [bit for bit in (2, 1) if bit in bits]
        self.masks = [0]
        for bit in self.stages:
            self.masks = self.masks + [mask ^ bit for mask in self.masks]

    def flip(self, array, bit):
        return lax.ppermute(array, "fsdp", [(i, i ^ bit) for i in range(self.fsdp)])

    def cross(self, array):
        return lax.ppermute(array, "tp", [(0, 1), (1, 0)])

    def gather(self, shard, cross_first):
        own = shard
        for bit in self.far:
            own = jnp.concatenate([own, self.flip(own, bit)], axis=0)
        if cross_first:
            other = self.cross(own)
            own = jnp.concatenate([own, self.flip(own, 2)], axis=0)
            other = jnp.concatenate([other, self.flip(other, 2)], axis=0)
        else:
            own = jnp.concatenate([own, self.flip(own, 2)], axis=0)
            other = self.cross(own)
        own = jnp.concatenate([own, self.flip(own, 1)], axis=0)
        other = jnp.concatenate([other, self.flip(other, 1)], axis=0)
        return own, other

    def halves(self, array):
        half = array.shape[0] // 2
        return array[:half], array[half:]

    def merge(self, keep, send, bit):
        return keep + self.flip(send.astype(bf16), bit).astype(f32)

    def scatter(self, own_keep, own_send, other_keep, other_send, cross_first):
        own = self.merge(own_keep, own_send, 1)
        other = self.merge(other_keep, other_send, 1)
        if cross_first:
            own = own + self.cross(other.astype(bf16)).astype(f32)
            own = self.merge(*self.halves(own), 2)
        else:
            own = self.merge(*self.halves(own), 2)
            other = self.merge(*self.halves(other), 2)
            own = own + self.cross(other.astype(bf16)).astype(f32)
        for bit in reversed(self.far):
            own = self.merge(*self.halves(own), bit)
        return own

    def total(self, array):
        for bit in reversed(self.stages):
            array = array + self.flip(array, bit)
        return array


ERF_P = 0.3275911
ERF_A = (0.254829592, -0.284496736, 1.421413741, -1.453152027, 1.061405429)


def gelu_parts(values):
    size = jnp.abs(values)
    t = 1.0 / (1.0 + (ERF_P * 2**-0.5) * size)
    expo = jnp.exp(-0.5 * values * values)
    poly = ERF_A[4]
    for coefficient in ERF_A[3::-1]:
        poly = poly * t + coefficient
    tail = (0.5 * poly) * (t * expo)
    phi = jnp.where(values < 0, tail, 1.0 - tail)
    return values * phi, phi + values * (expo * (2 * np.pi) ** -0.5)


def norm_parts(values):
    centred = values - jnp.mean(values, axis=-1, keepdims=True)
    scale = lax.rsqrt(jnp.mean(centred * centred, axis=-1, keepdims=True) + norm_eps)
    return centred * scale, scale


def norm_pull(grads, gain, normal, scale):
    inner = grads * gain
    return scale * (
        inner
        - jnp.mean(inner, axis=-1, keepdims=True)
        - normal * jnp.mean(inner * normal, axis=-1, keepdims=True)
    )


def shards(
    tokens,
    lengths,
    cotangent,
    w_query,
    w_key,
    w_value,
    w_output,
    w_inner,
    w_outer,
    bias_query,
    bias_value,
    bias_output,
    norm1_gain,
    norm1_bias,
    bias_inner,
    bias_outer,
    norm2_gain,
    norm2_bias,
):
    fsdp = lax.axis_size("fsdp")
    exchange = Exchange(fsdp)
    rows, model = tokens.shape
    seqs = rows // SEQ
    block = w_query.shape[0]
    width = w_query.shape[1]
    half = model // 2

    here = lax.axis_index("fsdp")
    masks = jnp.repeat(jnp.asarray(exchange.masks, jnp.int32), block)
    inside = jnp.tile(jnp.arange(block, dtype=jnp.int32), fsdp)
    source = (here ^ masks) * block + inside
    place = jnp.arange(model, dtype=jnp.int32)[:, None] == source[None, :]
    place16 = place.astype(bf16)
    place32 = place.astype(f32)

    shard_qkv = jnp.concatenate([w_query, w_key, w_value], axis=1).astype(bf16)
    qkv_own, qkv_other = exchange.gather(shard_qkv, False)
    out_own, out_other = exchange.gather(w_output.T.astype(bf16), True)
    inner_own, inner_other = exchange.gather(w_inner.astype(bf16), False)
    outer_own, outer_other = exchange.gather(w_outer.T.astype(bf16), True)

    biases_own = jnp.concatenate([bias_query, bias_value, bias_inner])
    biases_other = exchange.cross(biases_own)
    zero = jnp.zeros((width,), f32)

    def qkv_bias(biases):
        return jnp.concatenate([biases[:width], zero, biases[width : 2 * width]])

    def inner_bias(biases):
        return biases[2 * width :]

    vectors = jnp.stack([bias_output, norm1_gain, norm1_bias, bias_outer, norm2_gain, norm2_bias])
    vectors = lax.dot_general(
        vectors, place32, (((1,), (0,)), ((), ())), precision=lax.Precision.HIGHEST, preferred_element_type=f32
    )
    output_shift, gain_one, shift_one, outer_shift, gain_two, shift_two = [vectors[i] for i in range(6)]

    lengths_here = lax.dynamic_slice_in_dim(lengths, lax.axis_index("tp") * seqs, seqs, 0)

    inputs = dot_nn(tokens, place16).astype(bf16)
    cotan = dot_nn(cotangent, place16)
    proj_own = (dot_nn(inputs, qkv_own) + qkv_bias(biases_own)).astype(bf16)
    context_own, lse_own = attend_forward(proj_own, lengths_here)
    proj_other = (dot_nn(inputs, qkv_other) + qkv_bias(biases_other)).astype(bf16)
    context_other, lse_other = attend_forward(proj_other, lengths_here)
    attention = dot_nt(context_own, out_own) + dot_nt(context_other, out_other)
    normal_one, scale_one = norm_parts(attention + output_shift + inputs.astype(f32))
    normed = normal_one * gain_one + shift_one
    normed16 = normed.astype(bf16)
    hidden_own, slope_own = gelu_parts(dot_nn(normed16, inner_own) + inner_bias(biases_own))
    hidden_other, slope_other = gelu_parts(dot_nn(normed16, inner_other) + inner_bias(biases_other))
    hidden_own, hidden_other = hidden_own.astype(bf16), hidden_other.astype(bf16)
    ffn = dot_nt(hidden_own, outer_own) + dot_nt(hidden_other, outer_other)
    normal_two, scale_two = norm_parts(ffn + outer_shift + normed)
    mixed = dot_nt((normal_two * gain_two + shift_two).astype(bf16), place16).astype(bf16)

    d_before = norm_pull(cotan, gain_two, normal_two, scale_two)
    grad_gain_two = jnp.sum(cotan * normal_two, axis=0)
    grad_shift_two = jnp.sum(cotan, axis=0)
    grad_outer_bias = jnp.sum(d_before, axis=0)
    d_ffn = d_before.astype(bf16)

    def weight_grads(left, own, other):
        own_send = dot_tn(left[:, half:], own).astype(bf16)
        other_send = dot_tn(left[:, half:], other).astype(bf16)
        own_keep = dot_tn(left[:, :half], own)
        other_keep = dot_tn(left[:, :half], other)
        return own_keep, own_send, other_keep, other_send

    sum_outer = exchange.scatter(*weight_grads(d_ffn, hidden_own, hidden_other), True)
    d_inner_own = (dot_nn(d_ffn, outer_own) * slope_own).astype(bf16)
    d_inner_other = (dot_nn(d_ffn, outer_other) * slope_other).astype(bf16)
    grad_inner_bias_own = jnp.sum(d_inner_own.astype(f32), axis=0)
    grad_inner_bias_other = jnp.sum(d_inner_other.astype(f32), axis=0)
    sum_inner = exchange.scatter(*weight_grads(normed16, d_inner_own, d_inner_other), False)
    d_normed = d_before + dot_nt(d_inner_own, inner_own) + dot_nt(d_inner_other, inner_other)
    d_summed = norm_pull(d_normed, gain_one, normal_one, scale_one)
    grad_gain_one = jnp.sum(d_normed * normal_one, axis=0)
    grad_shift_one = jnp.sum(d_normed, axis=0)
    grad_output_bias = jnp.sum(d_summed, axis=0)
    d_attn = d_summed.astype(bf16)
    sum_output = exchange.scatter(*weight_grads(d_attn, context_own, context_other), True)
    d_context_own = dot_nn(d_attn, out_own).astype(bf16)
    d_context_other = dot_nn(d_attn, out_other).astype(bf16)
    d_proj_own = attend_backward(proj_own, context_own, d_context_own, lse_own, lengths_here)
    d_proj_other = attend_backward(proj_other, context_other, d_context_other, lse_other, lengths_here)
    sum_qkv = exchange.scatter(*weight_grads(inputs, d_proj_own, d_proj_other), False)
    grad_inputs = d_summed + dot_nt(d_proj_own, qkv_own) + dot_nt(d_proj_other, qkv_other)
    high = lax.reduce_precision(grad_inputs, 8, 7)
    grad_tokens = dot_nt(high.astype(bf16), place16) + dot_nt((grad_inputs - high).astype(bf16), place16)

    def sliced(d_proj, inner_part):
        summed = jnp.sum(d_proj.astype(f32), axis=0)
        return jnp.concatenate([summed[:width], summed[2 * width :], inner_part])

    whole = jnp.stack(
        [grad_output_bias, grad_gain_one, grad_shift_one, grad_outer_bias, grad_gain_two, grad_shift_two]
    )
    whole = lax.dot_general(
        whole, place32, (((1,), (1,)), ((), ())), precision=lax.Precision.HIGHEST, preferred_element_type=f32
    ).reshape(-1)
    small_own = jnp.concatenate([sliced(d_proj_own, grad_inner_bias_own), whole])
    small_other = jnp.concatenate([sliced(d_proj_other, grad_inner_bias_other), whole])
    small = exchange.total(small_own + exchange.cross(small_other))
    inner_width = bias_inner.shape[0]
    cuts = np.cumsum([width, width, inner_width] + [model] * 6)
    query_bias, value_bias, inner_bias_sum, *rest = jnp.split(small, cuts[:-1])

    return (
        mixed,
        grad_tokens,
        sum_qkv[:, :width],
        sum_qkv[:, width : 2 * width],
        sum_qkv[:, 2 * width :],
        sum_output.T,
        sum_inner,
        sum_outer.T,
        query_bias,
        value_bias,
        rest[0],
        rest[1],
        rest[2],
        inner_bias_sum,
        rest[3],
        rest[4],
        rest[5],
    )


def solution(mesh):
    both = P(("fsdp", "tp"), None)
    cols, rows = P("fsdp", "tp"), P("tp", "fsdp")
    return jax.shard_map(
        shards,
        mesh=mesh,
        in_specs=(both, P("fsdp"), both, cols, cols, cols, rows, cols, rows)
        + (P("tp"), P("tp"), P(), P(), P(), P("tp"), P(), P(), P()),
        out_specs=(both, both, cols, cols, cols, rows, cols, rows)
        + (P("tp"), P("tp"), P(), P(), P(), P("tp"), P(), P(), P()),
        check_vma=False,
    )
```

```python
import functools

import jax
import jax.numpy as jnp
import numpy as np
from jax import lax
from jax.experimental import pallas as pl
from jax.experimental.pallas import tpu as pltpu
from jax.sharding import PartitionSpec as P

DH = 64
SEQ = 512
PAIR = 2 * DH
norm_eps = 1e-12
masked_score = -1000000000.0
bf16 = jnp.bfloat16
f32 = jnp.float32
TILE = 256
COST = dict.fromkeys(
    (
        "attend_forward",
        "attend_backward",
        "attention_out",
        "hidden",
        "turn",
        "d_hidden",
        "d_attention",
        "d_inputs",
        "send_grads",
        "keep_grads",
    ),
    0.02,
)


def cost(micros):
    return pl.CostEstimate(flops=int(micros * 9e8), bytes_accessed=1024, transcendentals=0)


def dot_nn(left, right):
    return lax.dot_general(left, right, (((1,), (0,)), ((), ())), preferred_element_type=f32)


def dot_nt(left, right):
    return lax.dot_general(left, right, (((1,), (1,)), ((), ())), preferred_element_type=f32)


def dot_tn(left, right):
    return lax.dot_general(left, right, (((0,), (0,)), ((), ())), preferred_element_type=f32)


ERF_P = 0.3275911
ERF_A = (0.254829592, -0.284496736, 1.421413741, -1.453152027, 1.061405429)


def gelu_parts(values):
    size = jnp.abs(values)
    t = 1.0 / (1.0 + (ERF_P * 2**-0.5) * size)
    expo = jnp.exp(-0.5 * values * values)
    poly = ERF_A[4]
    for coefficient in ERF_A[3::-1]:
        poly = poly * t + coefficient
    tail = (0.5 * poly) * (t * expo)
    phi = jnp.where(values < 0, tail, 1.0 - tail)
    return values * phi, phi + values * (expo * (2 * np.pi) ** -0.5)


def norm_parts(values):
    centred = values - jnp.mean(values, axis=-1, keepdims=True)
    scale = lax.rsqrt(jnp.mean(centred * centred, axis=-1, keepdims=True) + norm_eps)
    return centred * scale, scale


def norm_pull(grads, gain, normal, scale):
    inner = grads * gain
    return scale * (
        inner
        - jnp.mean(inner, axis=-1, keepdims=True)
        - normal * jnp.mean(inner * normal, axis=-1, keepdims=True)
    )


def head_slice(block, head):
    return block[:, head * DH : (head + 1) * DH]


def live_rows(lengths_ref):
    rows = lax.broadcasted_iota(jnp.int32, (SEQ, 1), 0)
    return rows < lengths_ref[pl.program_id(0)]


def attend_forward_kernel(
    pairs, lengths_ref, inputs_ref, first_ref, second_ref, shift_ref, qkv_ref, context_ref, lse_ref
):
    live = live_rows(lengths_ref)
    width = pairs * PAIR
    half = first_ref.shape[0]
    qkv_ref[...] = (
        dot_nn(inputs_ref[:, :half], first_ref[...])
        + dot_nn(inputs_ref[:, half:], second_ref[...])
        + shift_ref[...]
    ).astype(bf16)

    def one_pair(index, carry):
        at = pl.multiple_of(index * PAIR, PAIR)
        query = qkv_ref[:, pl.ds(at, PAIR)] * jnp.asarray(DH ** (-0.5), bf16)
        keys = qkv_ref[:, pl.ds(width + at, PAIR)]
        values = qkv_ref[:, pl.ds(2 * width + at, PAIR)]
        turned = []
        for head in range(2):
            scores = dot_nt(head_slice(keys, head), head_slice(query, head))
            scores = jnp.where(live, scores, masked_score)
            top = jnp.max(scores, axis=0, keepdims=True)
            expo = jnp.exp(scores - top)
            total = jnp.sum(expo, axis=0, keepdims=True)
            probs = (expo * (1.0 / total)).astype(bf16)
            turned.append(dot_tn(head_slice(values, head), probs))
            lse_ref[0, pl.ds(index * 2 + head, 1), :] = top + jnp.log(total)
        context_ref[:, pl.ds(at, PAIR)] = jnp.concatenate(turned, axis=0).T.astype(bf16)
        return carry

    lax.fori_loop(0, pairs, one_pair, 0)


def attend_forward(inputs, weight, shift, lengths):
    rows, model = inputs.shape
    half, triple = weight[0].shape
    width = triple // 3
    seqs, pairs = rows // SEQ, width // PAIR
    heads = 2 * pairs
    return pl.pallas_call(
        functools.partial(attend_forward_kernel, pairs),
        grid_spec=pltpu.PrefetchScalarGridSpec(
            num_scalar_prefetch=1,
            grid=(seqs,),
            in_specs=[
                pl.BlockSpec((SEQ, model), lambda s, n: (s, 0)),
                pl.BlockSpec((half, triple), lambda s, n: (0, 0), pipeline_mode=pl.Buffered(1)),
                pl.BlockSpec((half, triple), lambda s, n: (0, 0), pipeline_mode=pl.Buffered(1)),
                pl.BlockSpec((1, triple), lambda s, n: (0, 0)),
            ],
            out_specs=[
                pl.BlockSpec((SEQ, triple), lambda s, n: (s, 0)),
                pl.BlockSpec((SEQ, width), lambda s, n: (s, 0)),
                pl.BlockSpec((1, heads, SEQ), lambda s, n: (s, 0, 0)),
            ],
        ),
        out_shape=[
            jax.ShapeDtypeStruct((rows, triple), bf16),
            jax.ShapeDtypeStruct((rows, width), bf16),
            jax.ShapeDtypeStruct((seqs, heads, SEQ), f32),
        ],
        compiler_params=pltpu.CompilerParams(vmem_limit_bytes=24 << 20),
        cost_estimate=cost(COST["attend_forward"]),
        name="attend_forward",
    )(lengths, inputs, *weight, shift[None, :])


def attend_backward_kernel(pairs, lengths_ref, qkv_ref, context_ref, d_context_ref, lse_ref, out_ref, sums_ref):
    live = live_rows(lengths_ref)

    @pl.when(pl.program_id(0) == 0)
    def _():
        sums_ref[...] = jnp.zeros_like(sums_ref)

    width = pairs * PAIR
    scale = DH ** (-0.5)

    def one_pair(index, carry):
        at = pl.multiple_of(index * PAIR, PAIR)
        query = qkv_ref[:, pl.ds(at, PAIR)] * jnp.asarray(scale, bf16)
        keys = qkv_ref[:, pl.ds(width + at, PAIR)]
        values = qkv_ref[:, pl.ds(2 * width + at, PAIR)]
        d_context = d_context_ref[:, pl.ds(at, PAIR)]
        weighed = (context_ref[:, pl.ds(at, PAIR)].astype(f32) * d_context.astype(f32)).T
        d_query, d_key, d_value = [], [], []
        for head in range(2):
            q_h, k_h, v_h = head_slice(query, head), head_slice(keys, head), head_slice(values, head)
            g_h = head_slice(d_context, head)
            row_dot = jnp.sum(weighed[head * DH : (head + 1) * DH], axis=0, keepdims=True)
            scores = jnp.where(live, dot_nt(k_h, q_h), masked_score)
            probs = jnp.exp(scores - lse_ref[0, pl.ds(index * 2 + head, 1), :])
            d_probs = dot_nt(v_h, g_h)
            d_scores = (probs * (d_probs - row_dot)).astype(bf16)
            d_value.append(dot_nn(probs.astype(bf16), g_h))
            d_key.append(dot_nn(d_scores, q_h))
            d_query.append(dot_tn(k_h, d_scores))
        turned = (jnp.concatenate(d_query, axis=0).T * scale).astype(bf16)
        d_value = jnp.concatenate(d_value, axis=1).astype(bf16)
        out_ref[:, pl.ds(at, PAIR)] = turned
        out_ref[:, pl.ds(width + at, PAIR)] = jnp.concatenate(d_key, axis=1).astype(bf16)
        out_ref[:, pl.ds(2 * width + at, PAIR)] = d_value
        sums_ref[0:1, pl.ds(at, PAIR)] += jnp.sum(turned.astype(f32), axis=0, keepdims=True)
        sums_ref[1:2, pl.ds(at, PAIR)] += jnp.sum(d_value.astype(f32), axis=0, keepdims=True)
        return carry

    lax.fori_loop(0, pairs, one_pair, 0)


def attend_backward(qkv, context, d_context, lse, lengths):
    rows, triple = qkv.shape
    width = triple // 3
    seqs, pairs = rows // SEQ, width // PAIR
    heads = 2 * pairs
    return pl.pallas_call(
        functools.partial(attend_backward_kernel, pairs),
        grid_spec=pltpu.PrefetchScalarGridSpec(
            num_scalar_prefetch=1,
            grid=(seqs,),
            in_specs=[
                pl.BlockSpec((SEQ, triple), lambda s, n: (s, 0)),
                pl.BlockSpec((SEQ, width), lambda s, n: (s, 0)),
                pl.BlockSpec((SEQ, width), lambda s, n: (s, 0)),
                pl.BlockSpec((1, heads, SEQ), lambda s, n: (s, 0, 0)),
            ],
            out_specs=[
                pl.BlockSpec((SEQ, triple), lambda s, n: (s, 0)),
                pl.BlockSpec((8, width), lambda s, n: (0, 0)),
            ],
        ),
        out_shape=[jax.ShapeDtypeStruct((rows, triple), bf16), jax.ShapeDtypeStruct((8, width), f32)],
        compiler_params=pltpu.CompilerParams(vmem_limit_bytes=24 << 20),
        cost_estimate=cost(COST["attend_backward"]),
        name="attend_backward",
    )(lengths, qkv, context, d_context, lse)


def in_vmem(kernel, name, limit, outs, *args):
    return pl.pallas_call(
        kernel,
        in_specs=[pl.BlockSpec(memory_space=pltpu.VMEM)] * len(args),
        out_specs=[pl.BlockSpec(memory_space=pltpu.VMEM)] * len(outs),
        out_shape=[jax.ShapeDtypeStruct(*out) for out in outs],
        compiler_params=pltpu.CompilerParams(vmem_limit_bytes=limit << 20),
        cost_estimate=cost(COST[name]),
        name=name,
    )(*args)


def tiles_of(ref, body):
    def one(index, carry):
        body(pl.ds(pl.multiple_of(index * TILE, TILE), TILE))
        return carry

    lax.fori_loop(0, ref.shape[0] // TILE, one, 0)


def add_sums(ref, row, values):
    ref[row : row + 1, :] += jnp.sum(values, axis=0, keepdims=True)


def nn_rows(left, pieces):
    total, start = None, 0
    for piece in pieces:
        part = dot_nn(left[:, start : start + piece.shape[0]], piece[...])
        total = part if total is None else total + part
        start += piece.shape[0]
    return total


def nt_rows(lefts, pieces):
    parts = []
    for index in range(len(pieces[0])):
        parts.append(sum(dot_nt(left, piece[index][...]) for left, piece in zip(lefts, pieces)))
    return jnp.concatenate(parts, axis=1)


def attention_out_kernel(
    own_ref, other_ref, own_a, own_b, other_a, other_b, inputs_ref, vectors_ref, normal_ref, scale_ref, normed_ref
):
    def body(at):
        mixed = nt_rows((own_ref[at], other_ref[at]), ((own_a, own_b), (other_a, other_b)))
        normal, scale = norm_parts(mixed + vectors_ref[0:1] + inputs_ref[at].astype(f32))
        normal_ref[at] = normal
        scale_ref[at] = scale
        normed_ref[at] = (normal * vectors_ref[1:2] + vectors_ref[2:3]).astype(bf16)

    tiles_of(own_ref, body)


def attention_out(own, other, w_own, w_other, inputs, vectors):
    shape = inputs.shape
    outs = [(shape, f32), ((shape[0], 1), f32), (shape, bf16)]
    return in_vmem(attention_out_kernel, "attention_out", 16, outs, own, other, *w_own, *w_other, inputs, vectors)


def hidden_kernel(normed_ref, w_a, w_b, shift_ref, hidden_ref, slope_ref):
    def body(at):
        hidden, slope = gelu_parts(nn_rows(normed_ref[at], (w_a, w_b)) + shift_ref[...])
        hidden_ref[at] = hidden.astype(bf16)
        slope_ref[at] = slope.astype(bf16)

    tiles_of(normed_ref, body)


def hidden_parts(normed, w, shift):
    shape = (normed.shape[0], w[0].shape[1])
    return in_vmem(hidden_kernel, "hidden", 24, [(shape, bf16), (shape, bf16)], normed, *w, shift[None, :])


def turn_kernel(
    own_ref,
    other_ref,
    own_a,
    own_b,
    other_a,
    other_b,
    normal_one_ref,
    cotan_ref,
    vectors_ref,
    place_ref,
    mixed_ref,
    d_before_ref,
    d_ffn_ref,
    sums_ref,
):
    sums_ref[...] = jnp.zeros_like(sums_ref)

    def body(at):
        ffn = nt_rows((own_ref[at], other_ref[at]), ((own_a, own_b), (other_a, other_b)))
        normed = normal_one_ref[at] * vectors_ref[1:2] + vectors_ref[2:3]
        normal, scale = norm_parts(ffn + vectors_ref[3:4] + normed)
        result = (normal * vectors_ref[4:5] + vectors_ref[5:6]).astype(bf16)
        mixed_ref[at] = dot_nt(result, place_ref[...]).astype(bf16)
        cotan = cotan_ref[at].astype(f32)
        d_before = norm_pull(cotan, vectors_ref[4:5], normal, scale)
        d_before_ref[at] = d_before
        d_ffn_ref[at] = d_before.astype(bf16)
        add_sums(sums_ref, 0, d_before)
        add_sums(sums_ref, 1, cotan * normal)
        add_sums(sums_ref, 2, cotan)

    tiles_of(own_ref, body)


def turn(own, other, w_own, w_other, normal_one, cotan, vectors, place):
    shape = normal_one.shape
    outs = [(shape, bf16), (shape, f32), (shape, bf16), ((8, shape[1]), f32)]
    args = (own, other, *w_own, *w_other, normal_one, cotan, vectors, place)
    return in_vmem(turn_kernel, "turn", 20, outs, *args)


def d_hidden_kernel(d_ffn_ref, w_a, w_b, slope_ref, d_inner_ref, sums_ref):
    sums_ref[...] = jnp.zeros_like(sums_ref)

    def body(at):
        d_inner = (nn_rows(d_ffn_ref[at], (w_a, w_b)) * slope_ref[at].astype(f32)).astype(bf16)
        d_inner_ref[at] = d_inner
        add_sums(sums_ref, 0, d_inner.astype(f32))

    tiles_of(d_ffn_ref, body)


def d_hidden(d_ffn, w, slope):
    outs = [(slope.shape, bf16), ((8, slope.shape[1]), f32)]
    return in_vmem(d_hidden_kernel, "d_hidden", 20, outs, d_ffn, *w, slope)


def d_attention_kernel(
    own_ref,
    other_ref,
    own_a,
    own_b,
    other_a,
    other_b,
    d_before_ref,
    normal_ref,
    scale_ref,
    vectors_ref,
    out_own_a,
    out_own_b,
    out_other_a,
    out_other_b,
    d_summed_ref,
    d_attn_ref,
    d_own_ref,
    d_other_ref,
    sums_ref,
):
    sums_ref[...] = jnp.zeros_like(sums_ref)

    def body(at):
        d_normed = d_before_ref[at] + nt_rows(
            (own_ref[at], other_ref[at]), ((own_a, own_b), (other_a, other_b))
        )
        normal = normal_ref[at]
        d_summed = norm_pull(d_normed, vectors_ref[1:2], normal, scale_ref[at])
        d_summed_ref[at] = d_summed
        d_attn = d_summed.astype(bf16)
        d_attn_ref[at] = d_attn
        d_own_ref[at] = nn_rows(d_attn, (out_own_a, out_own_b)).astype(bf16)
        d_other_ref[at] = nn_rows(d_attn, (out_other_a, out_other_b)).astype(bf16)
        add_sums(sums_ref, 0, d_summed)
        add_sums(sums_ref, 1, d_normed * normal)
        add_sums(sums_ref, 2, d_normed)

    tiles_of(own_ref, body)


def d_attention(own, other, w_own, w_other, d_before, normal, scale, vectors, out_own, out_other):
    shape = d_before.shape
    part = (shape[0], out_own[0].shape[1])
    outs = [(shape, f32), (shape, bf16), (part, bf16), (part, bf16), ((8, shape[1]), f32)]
    args = (own, other, *w_own, *w_other, d_before, normal, scale, vectors, *out_own, *out_other)
    return in_vmem(d_attention_kernel, "d_attention", 20, outs, *args)


def d_inputs_kernel(d_summed_ref, own_ref, other_ref, own_a, own_b, other_a, other_b, place_ref, out_ref):
    def body(at):
        grads = d_summed_ref[at] + nt_rows((own_ref[at], other_ref[at]), ((own_a, own_b), (other_a, other_b)))
        high = grads.astype(bf16)
        low = (grads - high.astype(f32)).astype(bf16)
        out_ref[at] = dot_nt(high, place_ref[...]) + dot_nt(low, place_ref[...])

    tiles_of(d_summed_ref, body)


def d_inputs(d_summed, own, other, w_own, w_other, place):
    outs = [(d_summed.shape, f32)]
    args = (d_summed, own, other, *w_own, *w_other, place)
    return in_vmem(d_inputs_kernel, "d_inputs", 16, outs, *args)[0]


def column_chunks(width):
    step = next(step for step in (512, 384, 256, 128) if width % step == 0)
    return [(start, step) for start in range(0, width, step)]


def send_kernel(count, left_ref, *refs):
    half = left_ref.shape[1] // 2
    left = left_ref[:, half:]
    for right_ref, out_ref in zip(refs[:count], refs[count:]):
        for start, step in column_chunks(right_ref.shape[1]):
            out_ref[:, start : start + step] = dot_tn(left, right_ref[:, start : start + step]).astype(bf16)


def send_grads(left, *rights):
    outs = [((left.shape[1] // 2, right.shape[1]), bf16) for right in rights]
    return in_vmem(functools.partial(send_kernel, len(rights)), "send_grads", 16, outs, left, *rights)


def keep_kernel(count, left_ref, *refs):
    half = left_ref.shape[1] // 2
    left = left_ref[:, :half]
    rights, others, outs = refs[:count], refs[count : 2 * count], refs[2 * count :]
    for index, (right_ref, other_ref) in enumerate(zip(rights, others)):
        upper_ref, lower_ref = outs[2 * index : 2 * index + 2]
        for start, step in column_chunks(right_ref.shape[1]):
            at = slice(start, start + step)
            total = dot_tn(left, right_ref[:, at]) + other_ref[:, at].astype(f32)
            upper_ref[:, at] = total[: half // 2].astype(upper_ref.dtype)
            lower_ref[:, at] = total[half // 2 :].astype(bf16)


def keep_grads(left, rights, others, kinds):
    quarter = left.shape[1] // 4
    outs = []
    for right, kind in zip(rights, kinds):
        outs += [((quarter, right.shape[1]), kind), ((quarter, right.shape[1]), bf16)]
    return in_vmem(functools.partial(keep_kernel, len(rights)), "keep_grads", 16, outs, left, *rights, *others)


class Exchange:
    def __init__(self, fsdp):
        self.fsdp = fsdp
        bits = [1 << i for i in range(2, fsdp.bit_length() - 1)]
        self.far = []
        for i in range(0, len(bits), 2):
            steps = [0]
            for bit in bits[i : i + 2]:
                steps = steps + [step ^ bit for step in steps]
            self.far.append(steps)
        self.masks = [0]
        for steps in self.far + [[0, 2], [0, 1]]:
            self.masks = [step ^ mask for step in steps for mask in self.masks]

    def flip(self, array, bit):
        return lax.ppermute(array, "fsdp", [(i, i ^ bit) for i in range(self.fsdp)])

    def cross(self, array):
        return lax.ppermute(array, "tp", [(0, 1), (1, 0)])

    def flip_cross(self, array, bit):
        pairs = [(2 * i + j, 2 * (i ^ bit) + 1 - j) for i in range(self.fsdp) for j in range(2)]
        return lax.ppermute(array, ("fsdp", "tp"), pairs)

    def gather_far(self, array):
        for steps in self.far[:-1]:
            array = join([array] + [self.flip(array, step) for step in steps[1:]])
        return [array] + [self.flip(array, step) for step in self.far[-1][1:]]

    def scatter_far(self, array):
        for steps in reversed(self.far):
            size = array.shape[0] // len(steps)
            parts = [array[i * size : (i + 1) * size] for i in range(len(steps))]
            array = parts[0]
            for part, step in zip(parts[1:], steps[1:]):
                array = array + self.flip(part.astype(bf16), step).astype(f32)
        return array

    def total_far(self, array):
        for steps in reversed(self.far):
            parts = [array] + [self.flip(array, step) for step in steps[1:]]
            while len(parts) > 1:
                parts = [parts[i] + parts[i + 1] for i in range(0, len(parts), 2)]
            array = parts[0]
        return array


def join(arrays):
    return jnp.concatenate(arrays, axis=0)


def top(array):
    return array[: array.shape[0] // 2]


def bottom(array):
    return array[array.shape[0] // 2 :]


def gate(values, *others):
    return lax.optimization_barrier((values, others))[0]


def shards(
    tokens,
    lengths,
    cotangent,
    w_query,
    w_key,
    w_value,
    w_output,
    w_inner,
    w_outer,
    bias_query,
    bias_value,
    bias_output,
    norm1_gain,
    norm1_bias,
    bias_inner,
    bias_outer,
    norm2_gain,
    norm2_bias,
):
    fsdp = lax.axis_size("fsdp")
    exchange = Exchange(fsdp)
    rows, model = tokens.shape
    seqs = rows // SEQ
    block = w_query.shape[0]
    width = w_query.shape[1]
    half = model // 2

    here = lax.axis_index("fsdp")
    masks = jnp.repeat(jnp.asarray(exchange.masks, jnp.int32), block)
    inside = jnp.tile(jnp.arange(block, dtype=jnp.int32), fsdp)
    source = (here ^ masks) * block + inside
    place = jnp.arange(model, dtype=jnp.int32)[:, None] == source[None, :]
    place16 = place.astype(bf16)
    place32 = place.astype(f32)
    lengths_here = lax.dynamic_slice_in_dim(lengths, lax.axis_index("tp") * seqs, seqs, 0)

    def permuted(vectors, dims):
        return lax.dot_general(
            vectors, place32, ((dims), ((), ())), precision=lax.Precision.HIGHEST, preferred_element_type=f32
        )

    zero = jnp.zeros((width,), f32)

    def qkv_bias(biases):
        return jnp.concatenate([biases[:width], zero, biases[width : 2 * width]])

    def inner_bias(biases):
        return biases[2 * width :]

    def merge(keep, received):
        return keep + received.astype(f32)

    flip, cross, flip_cross = exchange.flip, exchange.cross, exchange.flip_cross

    def ring(array):
        return flip(array, 2), cross(array), flip_cross(array, 2)

    shard_qkv = jnp.concatenate([w_query, w_key, w_value], axis=1).astype(bf16)
    biases_own = jnp.concatenate([bias_query, bias_value, bias_inner])
    biases_other = cross(biases_own)
    far_qkv = exchange.gather_far(shard_qkv)
    inputs = dot_nn(tokens, place16).astype(bf16)
    vectors = jnp.stack([bias_output, norm1_gain, norm1_bias, bias_outer, norm2_gain, norm2_bias])

    far_qkv, shard_mid, shard_outer, cotangent, vectors = gate(
        (
            far_qkv,
            jnp.concatenate([w_output.T.astype(bf16), w_inner.astype(bf16)], axis=1),
            w_outer.T.astype(bf16),
            cotangent,
            vectors,
        ),
        inputs,
        biases_other,
    )
    far_qkv = join(far_qkv)
    near_qkv, across_qkv, corner_qkv = ring(far_qkv)
    far_mid = exchange.gather_far(shard_mid)
    cotan = dot_nn(cotangent, place16).astype(bf16)
    vectors = permuted(vectors, ((1,), (0,)))

    half_qkv_own, half_qkv_other, far_mid, shard_outer = gate(
        ((far_qkv, near_qkv), (across_qkv, corner_qkv), far_mid, shard_outer), cotan, vectors
    )
    half_qkv_own, half_qkv_other, far_mid = join(half_qkv_own), join(half_qkv_other), join(far_mid)
    pair_qkv_own, pair_qkv_other = flip(half_qkv_own, 1), flip(half_qkv_other, 1)
    near_mid, across_mid, corner_mid = ring(far_mid)
    far_outer = exchange.gather_far(shard_outer)
    qkv_own = (half_qkv_own, pair_qkv_own)
    proj_own, context_own, lse_own = attend_forward(inputs, qkv_own, qkv_bias(biases_own), lengths_here)
    qkv_other = gate((half_qkv_other, pair_qkv_other), context_own)
    proj_other, context_other, lse_other = attend_forward(inputs, qkv_other, qkv_bias(biases_other), lengths_here)

    half_mid_own, half_mid_other, far_outer, context_other = gate(
        ((far_mid, near_mid), (across_mid, corner_mid), far_outer, context_other)
    )
    half_mid_own, half_mid_other, far_outer = join(half_mid_own), join(half_mid_other), join(far_outer)
    pair_mid_own, pair_mid_other = flip(half_mid_own, 1), flip(half_mid_other, 1)
    near_outer, across_outer, corner_outer = ring(far_outer)
    mid_own, mid_other = (half_mid_own, pair_mid_own), (half_mid_other, pair_mid_other)
    out_own, out_other = [[piece[:, :width] for piece in mid] for mid in (mid_own, mid_other)]
    inner_own, inner_other = [[piece[:, width:] for piece in mid] for mid in (mid_own, mid_other)]
    normal_one, scale_one, normed16 = attention_out(context_own, context_other, out_own, out_other, inputs, vectors)
    hidden_own, slope_own = hidden_parts(normed16, inner_own, inner_bias(biases_own))
    left = gate(normed16, hidden_own)
    hidden_other, slope_other = hidden_parts(left, inner_other, inner_bias(biases_other))

    half_outer_own, half_outer_other, hidden_other = gate(
        ((far_outer, near_outer), (across_outer, corner_outer), hidden_other)
    )
    half_outer_own, half_outer_other = join(half_outer_own), join(half_outer_other)
    outer_own = (half_outer_own, flip(half_outer_own, 1))
    outer_other = (half_outer_other, flip(half_outer_other, 1))

    mixed, d_before, d_ffn, sums_two = turn(
        hidden_own, hidden_other, outer_own, outer_other, normal_one, cotan, vectors, place16
    )

    def swap(arrays):
        return [flip(array, 1) for array in arrays]

    def spread(own_lower, other_upper, other_lower):
        return flip(own_lower, 2), cross(other_upper), flip_cross(other_lower, 2)

    def add_all(keep, parts):
        for part in parts:
            keep = merge(keep, part)
        return keep

    send_outer = send_grads(d_ffn, hidden_own, hidden_other)

    send_outer, d_ffn = gate((send_outer, d_ffn))
    pair_outer = swap(send_outer)
    d_inner_own, inner_sums_own = d_hidden(d_ffn, outer_own, slope_own)

    pair_outer, d_ffn, d_inner_own = gate((pair_outer, d_ffn, d_inner_own))
    keep_outer, *away_outer = keep_grads(d_ffn, (hidden_own, hidden_other), pair_outer, (f32, bf16))

    keep_outer, away_outer, d_ffn = gate((keep_outer, away_outer, d_ffn))
    ring_outer = spread(*away_outer)
    d_inner_other, inner_sums_other = d_hidden(d_ffn, outer_other, slope_other)
    send_inner = send_grads(normed16, d_inner_own, d_inner_other)

    send_inner, d_inner_other, normed16 = gate((send_inner, d_inner_other, normed16))
    pair_inner = swap(send_inner)
    d_summed, d_attn, d_context_own, d_context_other, sums_one = d_attention(
        d_inner_own, d_inner_other, inner_own, inner_other, d_before, normal_one, scale_one, vectors, out_own, out_other
    )

    pair_inner, d_attn, normed16 = gate((pair_inner, d_attn, normed16))
    keep_inner, *away_inner = keep_grads(normed16, (d_inner_own, d_inner_other), pair_inner, (f32, bf16))

    keep_inner, away_inner, d_attn = gate((keep_inner, away_inner, d_attn))
    ring_inner = spread(*away_inner)
    send_output = send_grads(d_attn, context_own, context_other)

    send_output, keep_outer, ring_outer, d_context_other = gate((send_output, keep_outer, ring_outer, d_context_other))
    pair_output = swap(send_output)
    sum_outer = exchange.scatter_far(add_all(keep_outer, ring_outer))
    d_proj_other, qkv_sums_other = attend_backward(
        proj_other, context_other, d_context_other, lse_other, lengths_here
    )
    send_qkv_other = send_grads(inputs, d_proj_other)

    send_qkv_other, pair_output, d_attn = gate((send_qkv_other, pair_output, d_attn))
    pair_qkv_other = swap(send_qkv_other)
    keep_output, *away_output = keep_grads(d_attn, (context_own, context_other), pair_output, (f32, bf16))

    pair_qkv_other, keep_output, d_proj_other = gate((pair_qkv_other, keep_output, d_proj_other))
    upper_qkv_other, lower_qkv_other = keep_grads(inputs, (d_proj_other,), pair_qkv_other, (bf16,))

    upper_qkv_other, lower_qkv_other, away_output, d_context_own = gate(
        (upper_qkv_other, lower_qkv_other, away_output, d_context_own)
    )
    ring_output = spread(*away_output)
    ring_qkv = (cross(upper_qkv_other), flip_cross(lower_qkv_other, 2))
    d_proj_own, qkv_sums_own = attend_backward(proj_own, context_own, d_context_own, lse_own, lengths_here)
    send_qkv_own = send_grads(inputs, d_proj_own)

    send_qkv_own, keep_inner, ring_inner, keep_output, ring_output, d_proj_own, qkv_sums_own = gate(
        (send_qkv_own, keep_inner, ring_inner, keep_output, ring_output, d_proj_own, qkv_sums_own), sum_outer
    )
    pair_qkv_own = swap(send_qkv_own)
    whole = permuted(jnp.concatenate([sums_one[:3], sums_two[:3]]), ((1,), (1,))).reshape(-1)
    small_own = jnp.concatenate([qkv_sums_own[0], qkv_sums_own[1], inner_sums_own[0], whole])
    small_other = jnp.concatenate([qkv_sums_other[0], qkv_sums_other[1], inner_sums_other[0], whole])
    across_small = cross(small_other)
    sum_inner = exchange.scatter_far(add_all(keep_inner, ring_inner))
    sum_output = exchange.scatter_far(add_all(keep_output, ring_output))

    pair_qkv_own, d_proj_own, across_small, small_own = gate((pair_qkv_own, d_proj_own, across_small, small_own))
    keep_qkv, away_qkv = keep_grads(inputs, (d_proj_own,), pair_qkv_own, (f32,))

    keep_qkv, away_qkv, d_proj_own = gate((keep_qkv, away_qkv, d_proj_own))
    near_qkv = flip(away_qkv, 2)
    small = small_own + across_small
    near_small = flip(small, 2)
    grad_tokens = d_inputs(d_summed, d_proj_own, d_proj_other, qkv_own, qkv_other, place16)

    keep_qkv, near_qkv, ring_qkv, small, near_small, grad_tokens = gate(
        (keep_qkv, near_qkv, ring_qkv, small, near_small, grad_tokens), sum_output, sum_inner
    )
    sum_qkv = exchange.scatter_far(add_all(keep_qkv, (near_qkv,) + tuple(ring_qkv)))
    small = small + near_small
    small = small + flip(small, 1)
    small = exchange.total_far(small)

    inner_width = bias_inner.shape[0]
    cuts = np.cumsum([width, width, inner_width] + [model] * 6)
    query_bias, value_bias, inner_bias_sum, *rest = jnp.split(small, cuts[:-1])

    return (
        mixed,
        grad_tokens,
        sum_qkv[:, :width],
        sum_qkv[:, width : 2 * width],
        sum_qkv[:, 2 * width :],
        sum_output.T,
        sum_inner,
        sum_outer.T,
        query_bias,
        value_bias,
        rest[0],
        rest[1],
        rest[2],
        inner_bias_sum,
        rest[3],
        rest[4],
        rest[5],
    )


def solution(mesh):
    both = P(("fsdp", "tp"), None)
    cols, rows = P("fsdp", "tp"), P("tp", "fsdp")
    return jax.shard_map(
        shards,
        mesh=mesh,
        in_specs=(both, P("fsdp"), both, cols, cols, cols, rows, cols, rows)
        + (P("tp"), P("tp"), P(), P(), P(), P("tp"), P(), P(), P()),
        out_specs=(both, both, cols, cols, cols, rows, cols, rows)
        + (P("tp"), P("tp"), P(), P(), P(), P("tp"), P(), P(), P()),
        check_vma=False,
    )
```

```python
import functools

import jax
import jax.numpy as jnp
import numpy as np
from jax import lax
from jax.experimental import pallas as pl
from jax.experimental.pallas import tpu as pltpu
from jax.sharding import PartitionSpec as P

DH = 64
SEQ = 512
PAIR = 2 * DH
norm_eps = 1e-12
masked_score = -1000000000.0
bf16 = jnp.bfloat16
f32 = jnp.float32
TILE = 256
COST = dict(
    attend_forward=39,
    attend_backward=0.02,
    attention_out=12,
    hidden=25.5,
    turn=39,
    d_hidden=10.8,
    d_attention=30,
    d_context=6,
    d_inputs=0.02,
    join=3,
    send_grads=0.02,
    keep_grads=10.5,
)


def cost(micros):
    return pl.CostEstimate(flops=int(micros * 9e8), bytes_accessed=1024, transcendentals=0)


def dot_nn(left, right):
    return lax.dot_general(left, right, (((1,), (0,)), ((), ())), preferred_element_type=f32)


def dot_nt(left, right):
    return lax.dot_general(left, right, (((1,), (1,)), ((), ())), preferred_element_type=f32)


def dot_tn(left, right):
    return lax.dot_general(left, right, (((0,), (0,)), ((), ())), preferred_element_type=f32)


ERF_P = 0.3275911
ERF_A = (0.254829592, -0.284496736, 1.421413741, -1.453152027, 1.061405429)


def gelu_parts(values):
    size = jnp.abs(values)
    t = 1.0 / (1.0 + (ERF_P * 2**-0.5) * size)
    expo = jnp.exp(-0.5 * values * values)
    poly = ERF_A[4]
    for coefficient in ERF_A[3::-1]:
        poly = poly * t + coefficient
    tail = (0.5 * poly) * (t * expo)
    phi = jnp.where(values < 0, tail, 1.0 - tail)
    return values * phi, phi + values * (expo * (2 * np.pi) ** -0.5)


def norm_parts(values):
    centred = values - jnp.mean(values, axis=-1, keepdims=True)
    scale = lax.rsqrt(jnp.mean(centred * centred, axis=-1, keepdims=True) + norm_eps)
    return centred * scale, scale


def norm_pull(grads, gain, normal, scale):
    inner = grads * gain
    return scale * (
        inner
        - jnp.mean(inner, axis=-1, keepdims=True)
        - normal * jnp.mean(inner * normal, axis=-1, keepdims=True)
    )


def fill(ref, column, pieces, start, width):
    part = pieces[0].shape[0]
    step = 32 if part % 32 == 0 else part
    for index, piece in enumerate(pieces):

        def one(at, carry, piece=piece, base=index * part):
            rows = pl.ds(pl.multiple_of(at * step, step), step)
            to = pl.ds(pl.multiple_of(base + at * step, step), step)
            ref[to, column : column + width] = piece[rows, start : start + width]
            return carry

        lax.fori_loop(0, part // step, one, 0)


def head_slice(block, head):
    return block[:, head * DH : (head + 1) * DH]


def live_rows(lengths_ref):
    rows = lax.broadcasted_iota(jnp.int32, (SEQ, 1), 0)
    return rows < lengths_ref[pl.program_id(0)]


def attend_forward_kernel(
    pairs, lengths_ref, inputs_ref, a_ref, b_ref, c_ref, d_ref, shift_ref, qkv_ref, context_ref, lse_ref, weight_ref
):
    live = live_rows(lengths_ref)
    width = pairs * PAIR

    @pl.when(pl.program_id(0) == 0)
    def _():
        fill(weight_ref, 0, (a_ref, b_ref, c_ref, d_ref), 0, 3 * width)

    qkv_ref[...] = (dot_nn(inputs_ref[...], weight_ref[...]) + shift_ref[...]).astype(bf16)

    def one_pair(index, carry):
        at = pl.multiple_of(index * PAIR, PAIR)
        query = qkv_ref[:, pl.ds(at, PAIR)] * jnp.asarray(DH ** (-0.5), bf16)
        keys = qkv_ref[:, pl.ds(width + at, PAIR)]
        values = qkv_ref[:, pl.ds(2 * width + at, PAIR)]
        turned = []
        for head in range(2):
            scores = dot_nt(head_slice(keys, head), head_slice(query, head))
            scores = jnp.where(live, scores, masked_score)
            top = jnp.max(scores, axis=0, keepdims=True)
            expo = jnp.exp(scores - top)
            total = jnp.sum(expo, axis=0, keepdims=True)
            probs = (expo * (1.0 / total)).astype(bf16)
            turned.append(dot_tn(head_slice(values, head), probs))
            lse_ref[0, pl.ds(index * 2 + head, 1), :] = top + jnp.log(total)
        context_ref[:, pl.ds(at, PAIR)] = jnp.concatenate(turned, axis=0).T.astype(bf16)
        return carry

    lax.fori_loop(0, pairs, one_pair, 0)


def attend_forward(inputs, pieces, shift, lengths):
    rows, model = inputs.shape
    part, _ = pieces[0].shape
    triple = shift.shape[0]
    width = triple // 3
    seqs, pairs = rows // SEQ, width // PAIR
    heads = 2 * pairs
    piece_spec = pl.BlockSpec((part, triple), lambda s, n: (0, 0), pipeline_mode=pl.Buffered(1))
    return pl.pallas_call(
        functools.partial(attend_forward_kernel, pairs),
        grid_spec=pltpu.PrefetchScalarGridSpec(
            num_scalar_prefetch=1,
            grid=(seqs,),
            in_specs=[pl.BlockSpec((SEQ, model), lambda s, n: (s, 0))]
            + [piece_spec] * 4
            + [pl.BlockSpec((1, triple), lambda s, n: (0, 0))],
            out_specs=[
                pl.BlockSpec((SEQ, triple), lambda s, n: (s, 0)),
                pl.BlockSpec((SEQ, width), lambda s, n: (s, 0)),
                pl.BlockSpec((1, heads, SEQ), lambda s, n: (s, 0, 0)),
            ],
            scratch_shapes=[pltpu.VMEM((model, triple), bf16)],
        ),
        out_shape=[
            jax.ShapeDtypeStruct((rows, triple), bf16),
            jax.ShapeDtypeStruct((rows, width), bf16),
            jax.ShapeDtypeStruct((seqs, heads, SEQ), f32),
        ],
        compiler_params=pltpu.CompilerParams(vmem_limit_bytes=18 << 20),
        cost_estimate=cost(COST["attend_forward"]),
        name="attend_forward",
    )(lengths, inputs, *pieces, shift[None, :])


def attend_backward_kernel(pairs, lengths_ref, qkv_ref, context_ref, d_context_ref, lse_ref, out_ref, sums_ref):
    live = live_rows(lengths_ref)

    @pl.when(pl.program_id(0) == 0)
    def _():
        sums_ref[...] = jnp.zeros_like(sums_ref)

    width = pairs * PAIR
    scale = DH ** (-0.5)

    def one_pair(index, carry):
        at = pl.multiple_of(index * PAIR, PAIR)
        query = qkv_ref[:, pl.ds(at, PAIR)] * jnp.asarray(scale, bf16)
        keys = qkv_ref[:, pl.ds(width + at, PAIR)]
        values = qkv_ref[:, pl.ds(2 * width + at, PAIR)]
        d_context = d_context_ref[:, pl.ds(at, PAIR)]
        weighed = (context_ref[:, pl.ds(at, PAIR)].astype(f32) * d_context.astype(f32)).T
        d_query, d_key, d_value = [], [], []
        for head in range(2):
            q_h, k_h, v_h = head_slice(query, head), head_slice(keys, head), head_slice(values, head)
            g_h = head_slice(d_context, head)
            row_dot = jnp.sum(weighed[head * DH : (head + 1) * DH], axis=0, keepdims=True)
            scores = jnp.where(live, dot_nt(k_h, q_h), masked_score)
            probs = jnp.exp(scores - lse_ref[0, pl.ds(index * 2 + head, 1), :])
            d_probs = dot_nt(v_h, g_h)
            d_scores = (probs * (d_probs - row_dot)).astype(bf16)
            d_value.append(dot_nn(probs.astype(bf16), g_h))
            d_key.append(dot_nn(d_scores, q_h))
            d_query.append(dot_tn(k_h, d_scores))
        turned = (jnp.concatenate(d_query, axis=0).T * scale).astype(bf16)
        d_value = jnp.concatenate(d_value, axis=1).astype(bf16)
        out_ref[:, pl.ds(at, PAIR)] = turned
        out_ref[:, pl.ds(width + at, PAIR)] = jnp.concatenate(d_key, axis=1).astype(bf16)
        out_ref[:, pl.ds(2 * width + at, PAIR)] = d_value
        sums_ref[0:1, pl.ds(at, PAIR)] += jnp.sum(turned.astype(f32), axis=0, keepdims=True)
        sums_ref[1:2, pl.ds(at, PAIR)] += jnp.sum(d_value.astype(f32), axis=0, keepdims=True)
        return carry

    lax.fori_loop(0, pairs, one_pair, 0)


def attend_backward(qkv, context, d_context, lse, lengths):
    rows, triple = qkv.shape
    width = triple // 3
    seqs, pairs = rows // SEQ, width // PAIR
    heads = 2 * pairs
    return pl.pallas_call(
        functools.partial(attend_backward_kernel, pairs),
        grid_spec=pltpu.PrefetchScalarGridSpec(
            num_scalar_prefetch=1,
            grid=(seqs,),
            in_specs=[
                pl.BlockSpec((SEQ, triple), lambda s, n: (s, 0)),
                pl.BlockSpec((SEQ, width), lambda s, n: (s, 0)),
                pl.BlockSpec((SEQ, width), lambda s, n: (s, 0)),
                pl.BlockSpec((1, heads, SEQ), lambda s, n: (s, 0, 0)),
            ],
            out_specs=[
                pl.BlockSpec((SEQ, triple), lambda s, n: (s, 0)),
                pl.BlockSpec((8, width), lambda s, n: (0, 0)),
            ],
        ),
        out_shape=[jax.ShapeDtypeStruct((rows, triple), bf16), jax.ShapeDtypeStruct((8, width), f32)],
        compiler_params=pltpu.CompilerParams(vmem_limit_bytes=14 << 20),
        cost_estimate=cost(COST["attend_backward"]),
        name="attend_backward",
    )(lengths, qkv, context, d_context, lse)


def in_vmem(kernel, name, limit, outs, *args, scratch=()):
    return pl.pallas_call(
        kernel,
        in_specs=[pl.BlockSpec(memory_space=pltpu.VMEM)] * len(args),
        out_specs=[pl.BlockSpec(memory_space=pltpu.VMEM)] * len(outs),
        out_shape=[jax.ShapeDtypeStruct(*out) for out in outs],
        scratch_shapes=[pltpu.VMEM(shape, bf16) for shape in scratch],
        compiler_params=pltpu.CompilerParams(vmem_limit_bytes=limit << 20),
        cost_estimate=cost(COST[name]),
        name=name,
    )(*args)


def tiles_of(ref, body):
    def one(index, carry):
        body(pl.ds(pl.multiple_of(index * TILE, TILE), TILE))
        return carry

    lax.fori_loop(0, ref.shape[0] // TILE, one, 0)


def add_sums(ref, row, values):
    ref[row : row + 1, :] += jnp.sum(values, axis=0, keepdims=True)


def side(one, other):
    return jnp.concatenate([one, other], axis=1)


def join_kernel(*refs):
    *pieces, out_ref = refs
    fill(out_ref, 0, pieces, 0, out_ref.shape[1])


def join(arrays):
    if len(arrays) == 1:
        return arrays[0]
    rows, width = arrays[0].shape
    if rows % 16:
        return jnp.concatenate(arrays, axis=0)
    return in_vmem(join_kernel, "join", 8, [((len(arrays) * rows, width), arrays[0].dtype)], *arrays)[0]


def attention_out_kernel(own_ref, other_ref, *refs):
    pieces, (inputs_ref, vectors_ref, normal_ref, scale_ref, normed_ref, weight_ref) = refs[:8], refs[8:]
    width = own_ref.shape[1]
    fill(weight_ref, 0, pieces[:4], 3 * width, width)
    fill(weight_ref, width, pieces[4:], 3 * width, width)

    def body(at):
        mixed = dot_nt(side(own_ref[at], other_ref[at]), weight_ref[...])
        normal, scale = norm_parts(mixed + vectors_ref[0:1] + inputs_ref[at].astype(f32))
        normal_ref[at] = normal
        scale_ref[at] = scale
        normed_ref[at] = (normal * vectors_ref[1:2] + vectors_ref[2:3]).astype(bf16)

    tiles_of(own_ref, body)


def attention_out(own, other, w_own, w_other, inputs, vectors):
    shape = inputs.shape
    outs = [(shape, f32), ((shape[0], 1), f32), (shape, bf16)]
    args = (own, other, *w_own, *w_other, inputs, vectors)
    return in_vmem(attention_out_kernel, "attention_out", 6, outs, *args, scratch=[(shape[1], shape[1])])


def hidden_kernel(normed_ref, *refs):
    pieces, (shift_ref, hidden_ref, slope_ref, weight_ref) = refs[:4], refs[4:]
    fill(weight_ref, 0, pieces, 0, weight_ref.shape[1])

    def body(at):
        hidden, slope = gelu_parts(dot_nn(normed_ref[at], weight_ref[...]) + shift_ref[...])
        hidden_ref[at] = hidden.astype(bf16)
        slope_ref[at] = slope.astype(bf16)

    tiles_of(normed_ref, body)


def hidden_parts(normed, w, shift):
    rows, model = normed.shape
    shape = (rows, w[0].shape[1])
    outs = [(shape, bf16), (shape, bf16)]
    args = (normed, *w, shift[None, :])
    return in_vmem(hidden_kernel, "hidden", 8, outs, *args, scratch=[(model, shape[1])])


def turn_kernel(own_ref, other_ref, *refs):
    pieces, (normal_one_ref, cotan_ref, vectors_ref, place_ref) = refs[:8], refs[8:12]
    mixed_ref, d_before_ref, d_ffn_ref, sums_ref, w_own_ref, w_other_ref = refs[12:]
    sums_ref[...] = jnp.zeros_like(sums_ref)
    fill(w_own_ref, 0, pieces[:4], 0, w_own_ref.shape[1])
    fill(w_other_ref, 0, pieces[4:], 0, w_other_ref.shape[1])

    def body(at):
        ffn = dot_nt(own_ref[at], w_own_ref[...]) + dot_nt(other_ref[at], w_other_ref[...])
        normed = normal_one_ref[at] * vectors_ref[1:2] + vectors_ref[2:3]
        normal, scale = norm_parts(ffn + vectors_ref[3:4] + normed)
        result = (normal * vectors_ref[4:5] + vectors_ref[5:6]).astype(bf16)
        mixed_ref[at] = dot_nt(result, place_ref[...]).astype(bf16)
        cotan = cotan_ref[at].astype(f32)
        d_before = norm_pull(cotan, vectors_ref[4:5], normal, scale)
        d_before_ref[at] = d_before
        d_ffn_ref[at] = d_before.astype(bf16)
        add_sums(sums_ref, 0, d_before)
        add_sums(sums_ref, 1, cotan * normal)
        add_sums(sums_ref, 2, cotan)

    tiles_of(own_ref, body)


def turn(own, other, w_own, w_other, normal_one, cotan, vectors, place):
    shape = normal_one.shape
    outs = [(shape, bf16), (shape, f32), (shape, bf16), ((8, shape[1]), f32)]
    args = (own, other, *w_own, *w_other, normal_one, cotan, vectors, place)
    return in_vmem(turn_kernel, "turn", 10, outs, *args, scratch=[(shape[1], own.shape[1])] * 2)


def d_hidden_kernel(d_ffn_ref, *refs):
    pieces, (slope_ref, d_inner_ref, sums_ref, weight_ref) = refs[:4], refs[4:]
    sums_ref[...] = jnp.zeros_like(sums_ref)
    fill(weight_ref, 0, pieces, 0, weight_ref.shape[1])

    def body(at):
        d_inner = (dot_nn(d_ffn_ref[at], weight_ref[...]) * slope_ref[at].astype(f32)).astype(bf16)
        d_inner_ref[at] = d_inner
        add_sums(sums_ref, 0, d_inner.astype(f32))

    tiles_of(d_ffn_ref, body)


def d_hidden(d_ffn, w, slope):
    outs = [(slope.shape, bf16), ((8, slope.shape[1]), f32)]
    return in_vmem(d_hidden_kernel, "d_hidden", 8, outs, d_ffn, *w, slope, scratch=[(d_ffn.shape[1], slope.shape[1])])


def d_attention_kernel(own_ref, other_ref, *refs):
    pieces, (d_before_ref, normal_ref, scale_ref, vectors_ref) = refs[:8], refs[8:12]
    d_summed_ref, d_attn_ref, sums_ref, w_own_ref, w_other_ref = refs[12:]
    sums_ref[...] = jnp.zeros_like(sums_ref)
    fill(w_own_ref, 0, pieces[:4], 0, w_own_ref.shape[1])
    fill(w_other_ref, 0, pieces[4:], 0, w_other_ref.shape[1])

    def body(at):
        d_normed = d_before_ref[at] + dot_nt(own_ref[at], w_own_ref[...]) + dot_nt(other_ref[at], w_other_ref[...])
        normal = normal_ref[at]
        d_summed = norm_pull(d_normed, vectors_ref[1:2], normal, scale_ref[at])
        d_summed_ref[at] = d_summed
        d_attn_ref[at] = d_summed.astype(bf16)
        add_sums(sums_ref, 0, d_summed)
        add_sums(sums_ref, 1, d_normed * normal)
        add_sums(sums_ref, 2, d_normed)

    tiles_of(own_ref, body)


def d_attention(own, other, w_own, w_other, d_before, normal, scale, vectors):
    shape = d_before.shape
    outs = [(shape, f32), (shape, bf16), ((8, shape[1]), f32)]
    args = (own, other, *w_own, *w_other, d_before, normal, scale, vectors)
    return in_vmem(d_attention_kernel, "d_attention", 10, outs, *args, scratch=[(shape[1], own.shape[1])] * 2)


def d_context_kernel(d_attn_ref, *refs):
    pieces, (own_ref, other_ref, weight_ref) = refs[:8], refs[8:]
    width = own_ref.shape[1]
    fill(weight_ref, 0, pieces[:4], 3 * width, width)
    fill(weight_ref, width, pieces[4:], 3 * width, width)

    def body(at):
        result = dot_nn(d_attn_ref[at], weight_ref[...]).astype(bf16)
        own_ref[at] = result[:, :width]
        other_ref[at] = result[:, width:]

    tiles_of(d_attn_ref, body)


def d_context(d_attn, w_own, w_other):
    rows, model = d_attn.shape
    outs = [((rows, model // 2), bf16)] * 2
    return in_vmem(d_context_kernel, "d_context", 5, outs, d_attn, *w_own, *w_other, scratch=[(model, model)])


def d_inputs_kernel(d_summed_ref, own_ref, other_ref, *refs):
    pieces, place_ref, (out_ref, weight_ref) = refs[:8], refs[8], refs[-2:]
    triple = own_ref.shape[1]

    @pl.when(pl.program_id(0) == 0)
    def _():
        fill(weight_ref, 0, pieces[:4], 0, triple)
        fill(weight_ref, triple, pieces[4:], 0, triple)

    grads = d_summed_ref[...] + dot_nt(side(own_ref[...], other_ref[...]), weight_ref[...])
    high = grads.astype(bf16)
    low = (grads - high.astype(f32)).astype(bf16)
    out_ref[...] = dot_nt(high, place_ref[...]) + dot_nt(low, place_ref[...])


def d_inputs(d_summed, own, other, w_own, w_other, place, half, earlier=()):
    rows, model = d_summed.shape
    part, triple = w_own[0].shape[0], own.shape[1]
    steps = rows // 2 // TILE

    def tile(width):
        return pl.BlockSpec((TILE, width), lambda i: (i + half * steps, 0))

    def fixed(shape):
        return pl.BlockSpec(shape, lambda i: (0, 0), pipeline_mode=pl.Buffered(1))

    args = (d_summed, own, other, *w_own, *w_other, place)
    return pl.pallas_call(
        d_inputs_kernel,
        grid=(steps,),
        in_specs=[tile(model), tile(triple), tile(triple)]
        + [fixed((part, triple))] * 8
        + [fixed(place.shape)]
        + [pl.BlockSpec(memory_space=pl.ANY)] * len(earlier),
        out_specs=tile(model),
        out_shape=jax.ShapeDtypeStruct((rows, model), f32),
        scratch_shapes=[pltpu.VMEM((model, 2 * triple), bf16)],
        input_output_aliases={len(args): 0} if earlier else {},
        compiler_params=pltpu.CompilerParams(vmem_limit_bytes=18 << 20),
        cost_estimate=cost(COST["d_inputs"]),
        name="d_inputs",
    )(*args, *earlier)


def chunks(width):
    step = next(step for step in (512, 384, 256, 128) if width % step == 0)
    return [(start, step) for start in range(0, width, step)]


def send_kernel(left_ref, *refs):
    *rights, out_ref = refs
    half = left_ref.shape[1] // 2
    left = left_ref[:, half:]
    base = 0
    for right_ref in rights:
        for start, step in chunks(right_ref.shape[1]):
            part = dot_tn(left, right_ref[:, start : start + step])
            out_ref[:, base + start : base + start + step] = part.astype(bf16)
        base += right_ref.shape[1]


def send_grads(left, *rights):
    outs = [((left.shape[1] // 2, sum(right.shape[1] for right in rights)), bf16)]
    return in_vmem(send_kernel, "send_grads", 5, outs, left, *rights)[0]


def keep_kernel(terms, *refs):
    for left_at, right_at, adds, upper, lower in terms:
        left_ref, right_ref = refs[left_at], refs[right_at]
        half = left_ref.shape[1] // 2
        left = left_ref[:, :half]
        for start, step in chunks(right_ref.shape[1]):
            total = dot_tn(left, right_ref[:, start : start + step])
            for add_at, column in adds:
                total = total + refs[add_at][:, column + start : column + start + step].astype(f32)
            for part, places in ((total[: half // 2], upper), (total[half // 2 :], lower)):
                for first, last, out_at, row, column in places:
                    if first <= start < last:
                        out_ref = refs[out_at]
                        to = column + start - first
                        out_ref[row : row + half // 2, to : to + step] = part.astype(out_ref.dtype)


def keep_grads(args, terms, outs):
    return in_vmem(functools.partial(keep_kernel, terms), "keep_grads", 8, outs, *args)


class Exchange:
    def __init__(self, fsdp):
        self.fsdp = fsdp
        bits = [1 << i for i in range(2, fsdp.bit_length() - 1)]
        self.bits, self.far = bits, []
        for i in range(0, len(bits), 2):
            steps = [0]
            for bit in bits[i : i + 2]:
                steps = steps + [step ^ bit for step in steps]
            self.far.append(steps)
        self.masks = [0]
        for steps in self.far + [[0, 2], [0, 1]]:
            self.masks = [step ^ mask for step in steps for mask in self.masks]

    def flip(self, array, bit):
        return lax.ppermute(array, "fsdp", [(i, i ^ bit) for i in range(self.fsdp)])

    def cross(self, array):
        return lax.ppermute(array, "tp", [(0, 1), (1, 0)])

    def flip_cross(self, array, bit):
        pairs = [(2 * i + j, 2 * (i ^ bit) + 1 - j) for i in range(self.fsdp) for j in range(2)]
        return lax.ppermute(array, ("fsdp", "tp"), pairs)

    def gather_far(self, array):
        for steps in self.far[:-1]:
            array = join([array] + [self.flip(array, step) for step in steps[1:]])
        return [array] + [self.flip(array, step) for step in self.far[-1][1:]]

    def scatter_far(self, array):
        for steps in reversed(self.far):
            size = array.shape[0] // len(steps)
            parts = [array[i * size : (i + 1) * size] for i in range(len(steps))]
            array = parts[0]
            for part, step in zip(parts[1:], steps[1:]):
                array = array + self.flip(part.astype(bf16), step).astype(f32)
        return array

    def halve(self, parts, bit):
        away = self.flip(jnp.concatenate(parts[1::2], axis=0).astype(bf16), bit)
        size = parts[0].shape[0]
        return parts[::2], [away[at : at + size] for at in range(0, away.shape[0], size)]

    def halve_first(self, array):
        size = array.shape[0] >> len(self.bits)
        return self.halve([array[at : at + size] for at in range(0, array.shape[0], size)], self.bits[0])

    def halve_rest(self, keep, away):
        for bit in self.bits[1:]:
            keep, away = self.halve([mine + theirs.astype(f32) for mine, theirs in zip(keep, away)], bit)
        return keep[0] + away[0].astype(f32)

    def total_far(self, array):
        for steps in reversed(self.far):
            parts = [array] + [self.flip(array, step) for step in steps[1:]]
            while len(parts) > 1:
                parts = [parts[i] + parts[i + 1] for i in range(0, len(parts), 2)]
            array = parts[0]
        return array


def gate(values, *others):
    return lax.optimization_barrier((values, others))[0]


def shards(
    tokens,
    lengths,
    cotangent,
    w_query,
    w_key,
    w_value,
    w_output,
    w_inner,
    w_outer,
    bias_query,
    bias_value,
    bias_output,
    norm1_gain,
    norm1_bias,
    bias_inner,
    bias_outer,
    norm2_gain,
    norm2_bias,
):
    fsdp = lax.axis_size("fsdp")
    exchange = Exchange(fsdp)
    rows, model = tokens.shape
    seqs = rows // SEQ
    block = w_query.shape[0]
    width = w_query.shape[1]
    half = model // 2

    here = lax.axis_index("fsdp")
    masks = jnp.repeat(jnp.asarray(exchange.masks, jnp.int32), block)
    inside = jnp.tile(jnp.arange(block, dtype=jnp.int32), fsdp)
    source = (here ^ masks) * block + inside
    place = jnp.arange(model, dtype=jnp.int32)[:, None] == source[None, :]
    place16 = place.astype(bf16)
    place32 = place.astype(f32)
    lengths_here = lax.dynamic_slice_in_dim(lengths, lax.axis_index("tp") * seqs, seqs, 0)

    def permuted(vectors, dims):
        return lax.dot_general(
            vectors, place32, ((dims), ((), ())), precision=lax.Precision.HIGHEST, preferred_element_type=f32
        )

    zero = jnp.zeros((width,), f32)

    def qkv_bias(biases):
        return jnp.concatenate([biases[:width], zero, biases[width : 2 * width]])

    def inner_bias(biases):
        return biases[2 * width :]

    flip, cross, flip_cross = exchange.flip, exchange.cross, exchange.flip_cross

    shard_attn = jnp.concatenate([w_query, w_key, w_value, w_output.T], axis=1).astype(bf16)
    biases_own = jnp.concatenate([bias_query, bias_value, bias_inner])
    far_attn = exchange.gather_far(shard_attn)
    biases_other = cross(biases_own)
    inputs = dot_nn(tokens, place16).astype(bf16)
    shard_inner, shard_outer = w_inner.astype(bf16), w_outer.T.astype(bf16)
    vectors = jnp.stack([bias_output, norm1_gain, norm1_bias, bias_outer, norm2_gain, norm2_bias])

    far_attn, shard_inner, shard_outer, biases_other, cotangent, vectors, inputs = gate(
        (far_attn, shard_inner, shard_outer, biases_other, cotangent, vectors, inputs)
    )
    far_attn = join(far_attn)
    near_attn, across_attn = flip(far_attn, 2), cross(far_attn)
    far_inner = exchange.gather_far(shard_inner)
    cotan = dot_nn(cotangent, place16).astype(bf16)
    vectors = permuted(vectors, ((1,), (0,)))

    far_attn, near_attn, across_attn, far_inner, shard_outer, inputs = gate(
        (far_attn, near_attn, across_attn, far_inner, shard_outer, inputs), cotan, vectors
    )
    pair_far_attn, pair_near_attn, corner_attn = flip(far_attn, 1), flip(near_attn, 1), cross(near_attn)
    far_inner = join(far_inner)
    near_inner = flip(far_inner, 2)
    far_outer = exchange.gather_far(shard_outer)
    attn_own = (far_attn, near_attn, pair_far_attn, pair_near_attn)
    proj_own, context_own, lse_own = attend_forward(inputs, attn_own, qkv_bias(biases_own), lengths_here)

    across_attn, corner_attn, far_inner, near_inner, far_outer, context_own = gate(
        (across_attn, corner_attn, far_inner, near_inner, far_outer, context_own)
    )
    pair_across_attn, pair_corner_attn = flip(across_attn, 1), flip(corner_attn, 1)
    across_inner = cross(far_inner)
    far_outer = join(far_outer)
    near_outer = flip(far_outer, 2)
    attn_other = (across_attn, corner_attn, pair_across_attn, pair_corner_attn)
    proj_other, context_other, lse_other = attend_forward(inputs, attn_other, qkv_bias(biases_other), lengths_here)

    far_inner, near_inner, across_inner, far_outer, near_outer, context_other = gate(
        (far_inner, near_inner, across_inner, far_outer, near_outer, context_other)
    )
    pair_far_inner, pair_near_inner = flip(far_inner, 1), flip(near_inner, 1)
    corner_inner = flip(across_inner, 2)
    across_outer = cross(far_outer)
    normal_one, scale_one, normed16 = attention_out(context_own, context_other, attn_own, attn_other, inputs, vectors)
    inner_own = (far_inner, near_inner, pair_far_inner, pair_near_inner)
    hidden_own, slope_own = hidden_parts(normed16, inner_own, inner_bias(biases_own))

    across_inner, corner_inner, far_outer, near_outer, across_outer, normed16, hidden_own = gate(
        (across_inner, corner_inner, far_outer, near_outer, across_outer, normed16, hidden_own)
    )
    corner_outer = cross(near_outer)
    pair_across_inner, pair_corner_inner = flip(across_inner, 1), flip(corner_inner, 1)
    pair_far_outer, pair_near_outer = flip(far_outer, 1), flip(near_outer, 1)
    inner_other = (across_inner, corner_inner, pair_across_inner, pair_corner_inner)
    hidden_other, slope_other = hidden_parts(normed16, inner_other, inner_bias(biases_other))

    across_outer, corner_outer, hidden_other = gate((across_outer, corner_outer, hidden_other))
    pair_across_outer, pair_corner_outer = flip(across_outer, 1), flip(corner_outer, 1)
    outer_own = (far_outer, near_outer, pair_far_outer, pair_near_outer)
    outer_other = (across_outer, corner_outer, pair_across_outer, pair_corner_outer)

    mixed, d_before, d_ffn, sums_two = turn(
        hidden_own, hidden_other, outer_own, outer_other, normal_one, cotan, vectors, place16
    )
    upper = model // 4
    inner_width = bias_inner.shape[0]

    def received(array):
        return array.astype(f32)

    send_outer = send_grads(d_ffn, hidden_own, hidden_other)

    send_outer, d_ffn = gate((send_outer, d_ffn))
    pair_outer = flip(send_outer, 1)
    d_inner_own, inner_sums_own = d_hidden(d_ffn, outer_own, slope_own)

    pair_outer, d_ffn, d_inner_own = gate((pair_outer, d_ffn, d_inner_own))
    part = (upper, inner_width)
    keep_outer, *away_outer = keep_grads(
        (d_ffn, hidden_own, hidden_other, pair_outer),
        (
            (0, 1, ((3, 0),), ((0, inner_width, 4, 0, 0),), ((0, inner_width, 5, 0, 0),)),
            (0, 2, ((3, inner_width),), ((0, inner_width, 6, 0, 0),), ((0, inner_width, 7, 0, 0),)),
        ),
        [(part, f32), (part, bf16), (part, bf16), (part, bf16)],
    )

    keep_outer, away_outer, d_ffn = gate((keep_outer, away_outer, d_ffn))
    ring_outer = (flip(away_outer[0], 2), cross(away_outer[1]), flip_cross(away_outer[2], 2))
    d_inner_other, inner_sums_other = d_hidden(d_ffn, outer_other, slope_other)
    send_inner = send_grads(normed16, d_inner_own, d_inner_other)

    send_inner, d_inner_other, normed16 = gate((send_inner, d_inner_other, normed16))
    pair_inner = flip(send_inner, 1)
    d_summed, d_attn, sums_one = d_attention(
        d_inner_own, d_inner_other, inner_own, inner_other, d_before, normal_one, scale_one, vectors
    )
    send_output = send_grads(d_attn, context_own, context_other)

    send_output, d_attn = gate((send_output, d_attn))
    pair_output = flip(send_output, 1)
    d_context_own, d_context_other = d_context(d_attn, attn_own, attn_other)

    pair_output, pair_inner, d_attn, normed16, d_context_other = gate(
        (pair_output, pair_inner, d_attn, normed16, d_context_other)
    )
    cut = 2 * inner_width // 3
    late = inner_width - cut
    rest = late + width
    args = (normed16, d_attn, d_inner_own, d_inner_other, context_own, context_other, pair_inner, pair_output)
    own_cut, own_low, other_cut, own_rest, other_rest, near_rest = range(8, 14)
    first_keep, first_low, first_away, last_keep, last_cross, last_away = keep_grads(
        args,
        (
            (
                0,
                2,
                ((6, 0),),
                ((0, cut, own_cut, 0, 0), (cut, inner_width, own_rest, 0, 0)),
                ((0, cut, own_low, 0, 0), (cut, inner_width, near_rest, 0, 0)),
            ),
            (
                0,
                3,
                ((6, inner_width),),
                ((0, cut, other_cut, 0, 0), (cut, inner_width, other_rest, 0, 0)),
                ((0, cut, other_cut, upper, 0), (cut, inner_width, near_rest, 0, rest)),
            ),
            (1, 4, ((7, 0),), ((0, width, own_rest, 0, late),), ((0, width, near_rest, 0, late),)),
            (1, 5, ((7, width),), ((0, width, other_rest, 0, late),), ((0, width, near_rest, 0, rest + late),)),
        ),
        [
            ((upper, cut), f32),
            ((upper, cut), f32),
            ((2 * upper, cut), bf16),
            ((upper, rest), f32),
            ((upper, rest), f32),
            ((upper, 2 * rest), bf16),
        ],
    )

    first_keep, first_low, first_away, last_keep, last_cross, last_away, d_context_other, keep_outer, ring_outer = gate(
        (first_keep, first_low, first_away, last_keep, last_cross, last_away, d_context_other, keep_outer, ring_outer)
    )
    first_across, last_near = cross(first_away), flip(last_away, 2)
    for piece in ring_outer:
        keep_outer = keep_outer + received(piece)
    keep_outer, lower_outer = exchange.halve_first(keep_outer)
    d_proj_other, qkv_sums_other = attend_backward(
        proj_other, context_other, d_context_other, lse_other, lengths_here
    )
    send_other = send_grads(inputs, d_proj_other)

    send_other, d_proj_other, first_across, last_near, keep_outer, lower_outer = gate(
        (send_other, d_proj_other, first_across, last_near, keep_outer, lower_outer)
    )
    pair_other = flip(send_other, 1)
    first_near = flip((first_low + received(first_across[upper:])).astype(bf16), 2)
    last_across = cross((last_cross + received(last_near[:, rest:])).astype(bf16))
    sum_outer = exchange.halve_rest(keep_outer, lower_outer)

    pair_other, d_proj_other = gate((pair_other, d_proj_other))
    triple = 3 * width
    (away_other,) = keep_grads(
        (inputs, d_proj_other, pair_other),
        ((0, 1, ((2, 0),), ((0, triple, 3, 0, 0),), ((0, triple, 3, upper, 0),)),),
        [((2 * upper, triple), bf16)],
    )

    away_other, d_context_own, qkv_sums_other, first_near, last_across, sum_outer = gate(
        (away_other, d_context_own, qkv_sums_other, first_near, last_across, sum_outer)
    )
    across_qkv = cross(away_other)
    whole = permuted(jnp.concatenate([sums_one[:3], sums_two[:3]]), ((1,), (1,))).reshape(-1)
    across_small = cross(jnp.concatenate([qkv_sums_other[0], qkv_sums_other[1], inner_sums_other[0], whole]))
    first_keep = first_keep + received(first_across[:upper]) + received(first_near)
    last_keep = last_keep + received(last_near[:, :rest]) + received(last_across)
    keep_mid, lower_mid = exchange.halve_first(jnp.concatenate([first_keep, last_keep], axis=1))
    d_proj_own, qkv_sums_own = attend_backward(proj_own, context_own, d_context_own, lse_own, lengths_here)
    send_own = send_grads(inputs, d_proj_own)
    early = d_inputs(d_summed, d_proj_own, d_proj_other, attn_own, attn_other, place16, 0)

    send_own, d_proj_own, qkv_sums_own, across_small, across_qkv, early, keep_mid, lower_mid = gate(
        (send_own, d_proj_own, qkv_sums_own, across_small, across_qkv, early, keep_mid, lower_mid)
    )
    pair_own = flip(send_own, 1)
    small = jnp.concatenate([qkv_sums_own[0], qkv_sums_own[1], inner_sums_own[0], whole]) + across_small
    pair_small = flip(small, 1)
    sum_mid = exchange.halve_rest(keep_mid, lower_mid)

    pair_own, d_proj_own, small, pair_small = gate((pair_own, d_proj_own, small, pair_small))
    small = small + pair_small
    near_small = flip(small, 2)
    keep_qkv, away_qkv = keep_grads(
        (inputs, d_proj_own, pair_own, across_qkv),
        ((0, 1, ((2, 0), (3, 0)), ((0, triple, 4, 0, 0),), ((0, triple, 5, 0, 0),)),),
        [((upper, triple), f32), ((upper, triple), bf16)],
    )

    keep_qkv, away_qkv, small, near_small, early = gate((keep_qkv, away_qkv, small, near_small, early))
    near_qkv = flip(away_qkv, 2)
    small = exchange.total_far(small + near_small)
    grad_tokens = d_inputs(d_summed, d_proj_own, d_proj_other, attn_own, attn_other, place16, 1, (early,))

    keep_qkv, near_qkv, small, grad_tokens, sum_mid = gate((keep_qkv, near_qkv, small, grad_tokens, sum_mid))
    sum_qkv = exchange.scatter_far(keep_qkv + received(near_qkv))

    inner_width = bias_inner.shape[0]
    cuts = np.cumsum([width, width, inner_width] + [model] * 6)
    query_bias, value_bias, inner_bias_sum, *rest = jnp.split(small, cuts[:-1])

    return (
        mixed,
        grad_tokens,
        sum_qkv[:, :width],
        sum_qkv[:, width : 2 * width],
        sum_qkv[:, 2 * width :],
        sum_mid[:, inner_width:].T,
        sum_mid[:, :inner_width],
        sum_outer.T,
        query_bias,
        value_bias,
        rest[0],
        rest[1],
        rest[2],
        inner_bias_sum,
        rest[3],
        rest[4],
        rest[5],
    )


def solution(mesh):
    both = P(("fsdp", "tp"), None)
    cols, rows = P("fsdp", "tp"), P("tp", "fsdp")
    return jax.shard_map(
        shards,
        mesh=mesh,
        in_specs=(both, P("fsdp"), both, cols, cols, cols, rows, cols, rows)
        + (P("tp"), P("tp"), P(), P(), P(), P("tp"), P(), P(), P()),
        out_specs=(both, both, cols, cols, cols, rows, cols, rows)
        + (P("tp"), P("tp"), P(), P(), P(), P("tp"), P(), P(), P()),
        check_vma=False,
    )
```

```python
import functools

import jax
import jax.numpy as jnp
import numpy as np
from jax import lax
from jax.experimental import pallas as pl
from jax.experimental.pallas import tpu as pltpu
from jax.sharding import PartitionSpec as P

DH = 64
SEQ = 512
PAIR = 2 * DH
norm_eps = 1e-12
masked_score = -1000000000.0
bf16 = jnp.bfloat16
f32 = jnp.float32
TILE = 256
COST = dict(
    attend_forward=39,
    attend_backward=0.02,
    attention_out=12,
    hidden=25.5,
    turn=39,
    d_hidden=10.8,
    d_attention=30,
    d_context=6,
    d_inputs=0.02,
    join=3,
    send_grads=0.02,
    keep_grads=10.5,
)


def cost(micros):
    return pl.CostEstimate(flops=int(micros * 9e8), bytes_accessed=1024, transcendentals=0)


def dot_nn(left, right):
    return lax.dot_general(left, right, (((1,), (0,)), ((), ())), preferred_element_type=f32)


def dot_nt(left, right):
    return lax.dot_general(left, right, (((1,), (1,)), ((), ())), preferred_element_type=f32)


def dot_tn(left, right):
    return lax.dot_general(left, right, (((0,), (0,)), ((), ())), preferred_element_type=f32)


ERF_P = 0.3275911
ERF_A = (0.254829592, -0.284496736, 1.421413741, -1.453152027, 1.061405429)


def gelu_parts(values):
    size = jnp.abs(values)
    t = 1.0 / (1.0 + (ERF_P * 2**-0.5) * size)
    expo = jnp.exp(-0.5 * values * values)
    poly = ERF_A[4]
    for coefficient in ERF_A[3::-1]:
        poly = poly * t + coefficient
    tail = (0.5 * poly) * (t * expo)
    phi = jnp.where(values < 0, tail, 1.0 - tail)
    return values * phi, phi + values * (expo * (2 * np.pi) ** -0.5)


def norm_parts(values):
    centred = values - jnp.mean(values, axis=-1, keepdims=True)
    scale = lax.rsqrt(jnp.mean(centred * centred, axis=-1, keepdims=True) + norm_eps)
    return centred * scale, scale


def norm_pull(grads, gain, normal, scale):
    inner = grads * gain
    return scale * (
        inner
        - jnp.mean(inner, axis=-1, keepdims=True)
        - normal * jnp.mean(inner * normal, axis=-1, keepdims=True)
    )


def fill(ref, column, pieces, start, width):
    part = pieces[0].shape[0]
    step = 32 if part % 32 == 0 else part
    for index, piece in enumerate(pieces):

        def one(at, carry, piece=piece, base=index * part):
            rows = pl.ds(pl.multiple_of(at * step, step), step)
            to = pl.ds(pl.multiple_of(base + at * step, step), step)
            ref[to, column : column + width] = piece[rows, start : start + width]
            return carry

        lax.fori_loop(0, part // step, one, 0)


def head_slice(block, head):
    return block[:, head * DH : (head + 1) * DH]


def live_rows(lengths_ref):
    rows = lax.broadcasted_iota(jnp.int32, (SEQ, 1), 0)
    return rows < lengths_ref[pl.program_id(0)]


def attend_forward_kernel(
    pairs, lengths_ref, inputs_ref, a_ref, b_ref, c_ref, d_ref, shift_ref, qkv_ref, context_ref, lse_ref, weight_ref
):
    live = live_rows(lengths_ref)
    width = pairs * PAIR

    @pl.when(pl.program_id(0) == 0)
    def _():
        fill(weight_ref, 0, (a_ref, b_ref, c_ref, d_ref), 0, 3 * width)

    qkv_ref[...] = (dot_nn(inputs_ref[...], weight_ref[...]) + shift_ref[...]).astype(bf16)

    def one_pair(index, carry):
        at = pl.multiple_of(index * PAIR, PAIR)
        query = qkv_ref[:, pl.ds(at, PAIR)] * jnp.asarray(DH ** (-0.5), bf16)
        keys = qkv_ref[:, pl.ds(width + at, PAIR)]
        values = qkv_ref[:, pl.ds(2 * width + at, PAIR)]
        turned = []
        for head in range(2):
            scores = dot_nt(head_slice(keys, head), head_slice(query, head))
            scores = jnp.where(live, scores, masked_score)
            top = jnp.max(scores, axis=0, keepdims=True)
            expo = jnp.exp(scores - top)
            total = jnp.sum(expo, axis=0, keepdims=True)
            probs = (expo * (1.0 / total)).astype(bf16)
            turned.append(dot_tn(head_slice(values, head), probs))
            lse_ref[0, pl.ds(index * 2 + head, 1), :] = top + jnp.log(total)
        context_ref[:, pl.ds(at, PAIR)] = jnp.concatenate(turned, axis=0).T.astype(bf16)
        return carry

    lax.fori_loop(0, pairs, one_pair, 0)


def attend_forward(inputs, pieces, shift, lengths):
    rows, model = inputs.shape
    part, _ = pieces[0].shape
    triple = shift.shape[0]
    width = triple // 3
    seqs, pairs = rows // SEQ, width // PAIR
    heads = 2 * pairs
    piece_spec = pl.BlockSpec((part, triple), lambda s, n: (0, 0), pipeline_mode=pl.Buffered(1))
    return pl.pallas_call(
        functools.partial(attend_forward_kernel, pairs),
        grid_spec=pltpu.PrefetchScalarGridSpec(
            num_scalar_prefetch=1,
            grid=(seqs,),
            in_specs=[pl.BlockSpec((SEQ, model), lambda s, n: (s, 0))]
            + [piece_spec] * 4
            + [pl.BlockSpec((1, triple), lambda s, n: (0, 0))],
            out_specs=[
                pl.BlockSpec((SEQ, triple), lambda s, n: (s, 0)),
                pl.BlockSpec((SEQ, width), lambda s, n: (s, 0)),
                pl.BlockSpec((1, heads, SEQ), lambda s, n: (s, 0, 0)),
            ],
            scratch_shapes=[pltpu.VMEM((model, triple), bf16)],
        ),
        out_shape=[
            jax.ShapeDtypeStruct((rows, triple), bf16),
            jax.ShapeDtypeStruct((rows, width), bf16),
            jax.ShapeDtypeStruct((seqs, heads, SEQ), f32),
        ],
        compiler_params=pltpu.CompilerParams(vmem_limit_bytes=18 << 20),
        cost_estimate=cost(COST["attend_forward"]),
        name="attend_forward",
    )(lengths, inputs, *pieces, shift[None, :])


def attend_backward_kernel(pairs, lengths_ref, qkv_ref, context_ref, d_context_ref, lse_ref, out_ref, sums_ref):
    live = live_rows(lengths_ref)

    @pl.when(pl.program_id(0) == 0)
    def _():
        sums_ref[...] = jnp.zeros_like(sums_ref)

    width = pairs * PAIR
    scale = DH ** (-0.5)

    def one_pair(index, carry):
        at = pl.multiple_of(index * PAIR, PAIR)
        query = qkv_ref[:, pl.ds(at, PAIR)] * jnp.asarray(scale, bf16)
        keys = qkv_ref[:, pl.ds(width + at, PAIR)]
        values = qkv_ref[:, pl.ds(2 * width + at, PAIR)]
        d_context = d_context_ref[:, pl.ds(at, PAIR)]
        weighed = (context_ref[:, pl.ds(at, PAIR)].astype(f32) * d_context.astype(f32)).T
        d_query, d_key, d_value = [], [], []
        for head in range(2):
            q_h, k_h, v_h = head_slice(query, head), head_slice(keys, head), head_slice(values, head)
            g_h = head_slice(d_context, head)
            row_dot = jnp.sum(weighed[head * DH : (head + 1) * DH], axis=0, keepdims=True)
            scores = jnp.where(live, dot_nt(k_h, q_h), masked_score)
            probs = jnp.exp(scores - lse_ref[0, pl.ds(index * 2 + head, 1), :])
            d_probs = dot_nt(v_h, g_h)
            d_scores = (probs * (d_probs - row_dot)).astype(bf16)
            d_value.append(dot_nn(probs.astype(bf16), g_h))
            d_key.append(dot_nn(d_scores, q_h))
            d_query.append(dot_tn(k_h, d_scores))
        turned = (jnp.concatenate(d_query, axis=0).T * scale).astype(bf16)
        d_value = jnp.concatenate(d_value, axis=1).astype(bf16)
        out_ref[:, pl.ds(at, PAIR)] = turned
        out_ref[:, pl.ds(width + at, PAIR)] = jnp.concatenate(d_key, axis=1).astype(bf16)
        out_ref[:, pl.ds(2 * width + at, PAIR)] = d_value
        sums_ref[0:1, pl.ds(at, PAIR)] += jnp.sum(turned.astype(f32), axis=0, keepdims=True)
        sums_ref[1:2, pl.ds(at, PAIR)] += jnp.sum(d_value.astype(f32), axis=0, keepdims=True)
        return carry

    lax.fori_loop(0, pairs, one_pair, 0)


def attend_backward(qkv, context, d_context, lse, lengths):
    rows, triple = qkv.shape
    width = triple // 3
    seqs, pairs = rows // SEQ, width // PAIR
    heads = 2 * pairs
    return pl.pallas_call(
        functools.partial(attend_backward_kernel, pairs),
        grid_spec=pltpu.PrefetchScalarGridSpec(
            num_scalar_prefetch=1,
            grid=(seqs,),
            in_specs=[
                pl.BlockSpec((SEQ, triple), lambda s, n: (s, 0)),
                pl.BlockSpec((SEQ, width), lambda s, n: (s, 0)),
                pl.BlockSpec((SEQ, width), lambda s, n: (s, 0)),
                pl.BlockSpec((1, heads, SEQ), lambda s, n: (s, 0, 0)),
            ],
            out_specs=[
                pl.BlockSpec((SEQ, triple), lambda s, n: (s, 0)),
                pl.BlockSpec((8, width), lambda s, n: (0, 0)),
            ],
        ),
        out_shape=[jax.ShapeDtypeStruct((rows, triple), bf16), jax.ShapeDtypeStruct((8, width), f32)],
        compiler_params=pltpu.CompilerParams(vmem_limit_bytes=14 << 20),
        cost_estimate=cost(COST["attend_backward"]),
        name="attend_backward",
    )(lengths, qkv, context, d_context, lse)


def in_vmem(kernel, name, limit, outs, *args, scratch=(), aliases=None):
    return pl.pallas_call(
        kernel,
        in_specs=[pl.BlockSpec(memory_space=pltpu.VMEM)] * len(args),
        out_specs=[pl.BlockSpec(memory_space=pltpu.VMEM)] * len(outs),
        out_shape=[jax.ShapeDtypeStruct(*out) for out in outs],
        scratch_shapes=[pltpu.VMEM(shape, bf16) for shape in scratch],
        input_output_aliases=aliases or {},
        compiler_params=pltpu.CompilerParams(vmem_limit_bytes=limit << 20),
        cost_estimate=cost(COST[name]),
        name=name,
    )(*args)


def tiles_of(ref, body):
    def one(index, carry):
        body(pl.ds(pl.multiple_of(index * TILE, TILE), TILE))
        return carry

    lax.fori_loop(0, ref.shape[0] // TILE, one, 0)


def add_sums(ref, row, values):
    ref[row : row + 1, :] += jnp.sum(values, axis=0, keepdims=True)


def side(one, other):
    return jnp.concatenate([one, other], axis=1)


def join_kernel(*refs):
    *pieces, out_ref = refs
    fill(out_ref, 0, pieces, 0, out_ref.shape[1])


def join(arrays):
    if len(arrays) == 1:
        return arrays[0]
    rows, width = arrays[0].shape
    if rows % 16:
        return jnp.concatenate(arrays, axis=0)
    return in_vmem(join_kernel, "join", 8, [((len(arrays) * rows, width), arrays[0].dtype)], *arrays)[0]


def attention_out_kernel(own_ref, other_ref, *refs):
    pieces, (inputs_ref, vectors_ref, normal_ref, scale_ref, normed_ref, weight_ref) = refs[:8], refs[8:]
    width = own_ref.shape[1]
    fill(weight_ref, 0, pieces[:4], 3 * width, width)
    fill(weight_ref, width, pieces[4:], 3 * width, width)

    def body(at):
        mixed = dot_nt(side(own_ref[at], other_ref[at]), weight_ref[...])
        normal, scale = norm_parts(mixed + vectors_ref[0:1] + inputs_ref[at].astype(f32))
        normal_ref[at] = normal
        scale_ref[at] = scale
        normed_ref[at] = (normal * vectors_ref[1:2] + vectors_ref[2:3]).astype(bf16)

    tiles_of(own_ref, body)


def attention_out(own, other, w_own, w_other, inputs, vectors):
    shape = inputs.shape
    outs = [(shape, f32), ((shape[0], 1), f32), (shape, bf16)]
    args = (own, other, *w_own, *w_other, inputs, vectors)
    return in_vmem(attention_out_kernel, "attention_out", 6, outs, *args, scratch=[(shape[1], shape[1])])


def hidden_kernel(normed_ref, *refs):
    pieces, (shift_ref, hidden_ref, slope_ref, weight_ref) = refs[:4], refs[4:]
    fill(weight_ref, 0, pieces, 0, weight_ref.shape[1])

    def body(at):
        hidden, slope = gelu_parts(dot_nn(normed_ref[at], weight_ref[...]) + shift_ref[...])
        hidden_ref[at] = hidden.astype(bf16)
        slope_ref[at] = slope.astype(bf16)

    tiles_of(normed_ref, body)


def hidden_parts(normed, w, shift):
    rows, model = normed.shape
    shape = (rows, w[0].shape[1])
    outs = [(shape, bf16), (shape, bf16)]
    args = (normed, *w, shift[None, :])
    return in_vmem(hidden_kernel, "hidden", 8, outs, *args, scratch=[(model, shape[1])])


def turn_kernel(own_ref, other_ref, *refs):
    pieces, (normal_one_ref, cotan_ref, vectors_ref, place_ref) = refs[:8], refs[8:12]
    mixed_ref, d_before_ref, d_ffn_ref, sums_ref, w_own_ref, w_other_ref = refs[12:]
    sums_ref[...] = jnp.zeros_like(sums_ref)
    fill(w_own_ref, 0, pieces[:4], 0, w_own_ref.shape[1])
    fill(w_other_ref, 0, pieces[4:], 0, w_other_ref.shape[1])

    def body(at):
        ffn = dot_nt(own_ref[at], w_own_ref[...]) + dot_nt(other_ref[at], w_other_ref[...])
        normed = normal_one_ref[at] * vectors_ref[1:2] + vectors_ref[2:3]
        normal, scale = norm_parts(ffn + vectors_ref[3:4] + normed)
        result = (normal * vectors_ref[4:5] + vectors_ref[5:6]).astype(bf16)
        mixed_ref[at] = dot_nt(result, place_ref[...]).astype(bf16)
        cotan = cotan_ref[at].astype(f32)
        d_before = norm_pull(cotan, vectors_ref[4:5], normal, scale)
        d_before_ref[at] = d_before
        d_ffn_ref[at] = d_before.astype(bf16)
        add_sums(sums_ref, 0, d_before)
        add_sums(sums_ref, 1, cotan * normal)
        add_sums(sums_ref, 2, cotan)

    tiles_of(own_ref, body)


def turn(own, other, w_own, w_other, normal_one, cotan, vectors, place):
    shape = normal_one.shape
    outs = [(shape, bf16), (shape, f32), (shape, bf16), ((8, shape[1]), f32)]
    args = (own, other, *w_own, *w_other, normal_one, cotan, vectors, place)
    scratch = [(shape[1], own.shape[1])] * 2
    return in_vmem(turn_kernel, "turn", 10, outs, *args, scratch=scratch, aliases={11: 2})


def d_hidden_kernel(d_ffn_ref, *refs):
    pieces, (slope_ref, d_inner_ref, sums_ref, weight_ref) = refs[:4], refs[4:]
    sums_ref[...] = jnp.zeros_like(sums_ref)
    fill(weight_ref, 0, pieces, 0, weight_ref.shape[1])

    def body(at):
        d_inner = (dot_nn(d_ffn_ref[at], weight_ref[...]) * slope_ref[at].astype(f32)).astype(bf16)
        d_inner_ref[at] = d_inner
        add_sums(sums_ref, 0, d_inner.astype(f32))

    tiles_of(d_ffn_ref, body)


def d_hidden(d_ffn, w, slope):
    outs = [(slope.shape, bf16), ((8, slope.shape[1]), f32)]
    args = (d_ffn, *w, slope)
    scratch = [(d_ffn.shape[1], slope.shape[1])]
    return in_vmem(d_hidden_kernel, "d_hidden", 8, outs, *args, scratch=scratch, aliases={5: 0})


def d_attention_kernel(own_ref, other_ref, *refs):
    pieces, (d_before_ref, normal_ref, scale_ref, vectors_ref) = refs[:8], refs[8:12]
    d_summed_ref, d_attn_ref, sums_ref, w_own_ref, w_other_ref = refs[12:]
    sums_ref[...] = jnp.zeros_like(sums_ref)
    fill(w_own_ref, 0, pieces[:4], 0, w_own_ref.shape[1])
    fill(w_other_ref, 0, pieces[4:], 0, w_other_ref.shape[1])

    def body(at):
        d_normed = d_before_ref[at] + dot_nt(own_ref[at], w_own_ref[...]) + dot_nt(other_ref[at], w_other_ref[...])
        normal = normal_ref[at]
        d_summed = norm_pull(d_normed, vectors_ref[1:2], normal, scale_ref[at])
        d_summed_ref[at] = d_summed
        d_attn_ref[at] = d_summed.astype(bf16)
        add_sums(sums_ref, 0, d_summed)
        add_sums(sums_ref, 1, d_normed * normal)
        add_sums(sums_ref, 2, d_normed)

    tiles_of(own_ref, body)


def d_attention(own, other, w_own, w_other, d_before, normal, scale, vectors):
    shape = d_before.shape
    outs = [(shape, f32), (shape, bf16), ((8, shape[1]), f32)]
    args = (own, other, *w_own, *w_other, d_before, normal, scale, vectors)
    scratch = [(shape[1], own.shape[1])] * 2
    return in_vmem(d_attention_kernel, "d_attention", 10, outs, *args, scratch=scratch, aliases={10: 0})


def d_context_kernel(d_attn_ref, *refs):
    pieces, (own_ref, other_ref, weight_ref) = refs[:8], refs[8:]
    width = own_ref.shape[1]
    fill(weight_ref, 0, pieces[:4], 3 * width, width)
    fill(weight_ref, width, pieces[4:], 3 * width, width)

    def body(at):
        result = dot_nn(d_attn_ref[at], weight_ref[...]).astype(bf16)
        own_ref[at] = result[:, :width]
        other_ref[at] = result[:, width:]

    tiles_of(d_attn_ref, body)


def d_context(d_attn, w_own, w_other):
    rows, model = d_attn.shape
    outs = [((rows, model // 2), bf16)] * 2
    return in_vmem(d_context_kernel, "d_context", 5, outs, d_attn, *w_own, *w_other, scratch=[(model, model)])


def d_inputs_kernel(d_summed_ref, own_ref, other_ref, *refs):
    pieces, place_ref, (out_ref, weight_ref) = refs[:8], refs[8], refs[-2:]
    triple = own_ref.shape[1]

    @pl.when(pl.program_id(0) == 0)
    def _():
        fill(weight_ref, 0, pieces[:4], 0, triple)
        fill(weight_ref, triple, pieces[4:], 0, triple)

    grads = d_summed_ref[...] + dot_nt(side(own_ref[...], other_ref[...]), weight_ref[...])
    high = grads.astype(bf16)
    low = (grads - high.astype(f32)).astype(bf16)
    out_ref[...] = dot_nt(high, place_ref[...]) + dot_nt(low, place_ref[...])


def d_inputs(d_summed, own, other, w_own, w_other, place, half, earlier=()):
    rows, model = d_summed.shape
    part, triple = w_own[0].shape[0], own.shape[1]
    steps = rows // 2 // TILE

    def tile(width):
        return pl.BlockSpec((TILE, width), lambda i: (i + half * steps, 0))

    def fixed(shape):
        return pl.BlockSpec(shape, lambda i: (0, 0), pipeline_mode=pl.Buffered(1))

    args = (d_summed, own, other, *w_own, *w_other, place)
    return pl.pallas_call(
        d_inputs_kernel,
        grid=(steps,),
        in_specs=[tile(model), tile(triple), tile(triple)]
        + [fixed((part, triple))] * 8
        + [fixed(place.shape)]
        + [pl.BlockSpec(memory_space=pl.ANY)] * len(earlier),
        out_specs=tile(model),
        out_shape=jax.ShapeDtypeStruct((rows, model), f32),
        scratch_shapes=[pltpu.VMEM((model, 2 * triple), bf16)],
        input_output_aliases={len(args): 0} if earlier else {},
        compiler_params=pltpu.CompilerParams(vmem_limit_bytes=18 << 20),
        cost_estimate=cost(COST["d_inputs"]),
        name="d_inputs",
    )(*args, *earlier)


def chunks(width):
    step = next(step for step in (512, 384, 256, 128) if width % step == 0)
    return [(start, step) for start in range(0, width, step)]


def send_kernel(left_ref, *refs):
    *rights, out_ref = refs
    half = left_ref.shape[1] // 2
    left = left_ref[:, half:]
    base = 0
    for right_ref in rights:
        for start, step in chunks(right_ref.shape[1]):
            part = dot_tn(left, right_ref[:, start : start + step])
            out_ref[:, base + start : base + start + step] = part.astype(bf16)
        base += right_ref.shape[1]


def send_grads(left, *rights):
    outs = [((left.shape[1] // 2, sum(right.shape[1] for right in rights)), bf16)]
    return in_vmem(send_kernel, "send_grads", 5, outs, left, *rights)[0]


def keep_kernel(terms, *refs):
    for left_at, right_at, adds, upper, lower in terms:
        left_ref, right_ref = refs[left_at], refs[right_at]
        half = left_ref.shape[1] // 2
        left = left_ref[:, :half]
        for start, step in chunks(right_ref.shape[1]):
            total = dot_tn(left, right_ref[:, start : start + step])
            for add_at, column in adds:
                total = total + refs[add_at][:, column + start : column + start + step].astype(f32)
            for part, places in ((total[: half // 2], upper), (total[half // 2 :], lower)):
                for first, last, out_at, row, column in places:
                    if first <= start < last:
                        out_ref = refs[out_at]
                        to = column + start - first
                        out_ref[row : row + half // 2, to : to + step] = part.astype(out_ref.dtype)


def keep_grads(args, terms, outs):
    return in_vmem(functools.partial(keep_kernel, terms), "keep_grads", 8, outs, *args)


class Exchange:
    def __init__(self, fsdp):
        self.fsdp = fsdp
        bits = [1 << i for i in range(2, fsdp.bit_length() - 1)]
        self.bits, self.far = bits, []
        for i in range(0, len(bits), 2):
            steps = [0]
            for bit in bits[i : i + 2]:
                steps = steps + [step ^ bit for step in steps]
            self.far.append(steps)
        self.masks = [0]
        for steps in self.far + [[0, 2], [0, 1]]:
            self.masks = [step ^ mask for step in steps for mask in self.masks]

    def flip(self, array, bit):
        return lax.ppermute(array, "fsdp", [(i, i ^ bit) for i in range(self.fsdp)])

    def cross(self, array):
        return lax.ppermute(array, "tp", [(0, 1), (1, 0)])

    def flip_cross(self, array, bit):
        pairs = [(2 * i + j, 2 * (i ^ bit) + 1 - j) for i in range(self.fsdp) for j in range(2)]
        return lax.ppermute(array, ("fsdp", "tp"), pairs)

    def gather_far(self, array):
        for steps in self.far[:-1]:
            array = join([array] + [self.flip(array, step) for step in steps[1:]])
        return [array] + [self.flip(array, step) for step in self.far[-1][1:]]

    def scatter_far(self, array):
        for steps in reversed(self.far):
            size = array.shape[0] // len(steps)
            parts = [array[i * size : (i + 1) * size] for i in range(len(steps))]
            array = parts[0]
            for part, step in zip(parts[1:], steps[1:]):
                array = array + self.flip(part.astype(bf16), step).astype(f32)
        return array

    def halve(self, parts, bit):
        away = self.flip(jnp.concatenate(parts[1::2], axis=0).astype(bf16), bit)
        size = parts[0].shape[0]
        return parts[::2], [away[at : at + size] for at in range(0, away.shape[0], size)]

    def halve_first(self, array):
        size = array.shape[0] >> len(self.bits)
        return self.halve([array[at : at + size] for at in range(0, array.shape[0], size)], self.bits[0])

    def halve_rest(self, keep, away):
        for bit in self.bits[1:]:
            keep, away = self.halve([mine + theirs.astype(f32) for mine, theirs in zip(keep, away)], bit)
        return keep[0], away[0]

    def total_rest(self, array):
        for bit in self.bits[1:]:
            array = array + self.flip(array, bit)
        return array


def gate(values, *others):
    return lax.optimization_barrier((values, others))[0]


def shards(
    tokens,
    lengths,
    cotangent,
    w_query,
    w_key,
    w_value,
    w_output,
    w_inner,
    w_outer,
    bias_query,
    bias_value,
    bias_output,
    norm1_gain,
    norm1_bias,
    bias_inner,
    bias_outer,
    norm2_gain,
    norm2_bias,
):
    fsdp = lax.axis_size("fsdp")
    exchange = Exchange(fsdp)
    rows, model = tokens.shape
    seqs = rows // SEQ
    block = w_query.shape[0]
    width = w_query.shape[1]
    half = model // 2

    here = lax.axis_index("fsdp")
    masks = jnp.repeat(jnp.asarray(exchange.masks, jnp.int32), block)
    inside = jnp.tile(jnp.arange(block, dtype=jnp.int32), fsdp)
    source = (here ^ masks) * block + inside
    place = jnp.arange(model, dtype=jnp.int32)[:, None] == source[None, :]
    place16 = place.astype(bf16)
    place32 = place.astype(f32)
    lengths_here = lax.dynamic_slice_in_dim(lengths, lax.axis_index("tp") * seqs, seqs, 0)

    def permuted(vectors, dims):
        return lax.dot_general(
            vectors, place32, ((dims), ((), ())), precision=lax.Precision.HIGHEST, preferred_element_type=f32
        )

    zero = jnp.zeros((width,), f32)

    def qkv_bias(biases):
        return jnp.concatenate([biases[:width], zero, biases[width : 2 * width]])

    def inner_bias(biases):
        return biases[2 * width :]

    flip, cross, flip_cross = exchange.flip, exchange.cross, exchange.flip_cross

    shard_attn = jnp.concatenate([w_query, w_key, w_value, w_output.T], axis=1).astype(bf16)
    biases_own = jnp.concatenate([bias_query, bias_value, bias_inner])
    far_attn = exchange.gather_far(shard_attn)
    biases_other = cross(biases_own)
    inputs = dot_nn(tokens, place16).astype(bf16)
    shard_inner, shard_outer = w_inner.astype(bf16), w_outer.T.astype(bf16)
    vectors = jnp.stack([bias_output, norm1_gain, norm1_bias, bias_outer, norm2_gain, norm2_bias])

    far_attn, shard_inner, shard_outer, biases_other, cotangent, vectors, inputs = gate(
        (far_attn, shard_inner, shard_outer, biases_other, cotangent, vectors, inputs)
    )
    far_attn = join(far_attn)
    near_attn, across_attn = flip(far_attn, 2), cross(far_attn)
    far_inner = exchange.gather_far(shard_inner)
    cotan = dot_nn(cotangent, place16).astype(bf16)
    vectors = permuted(vectors, ((1,), (0,)))

    far_attn, near_attn, across_attn, far_inner, shard_outer, inputs = gate(
        (far_attn, near_attn, across_attn, far_inner, shard_outer, inputs), cotan, vectors
    )
    pair_far_attn, pair_near_attn, corner_attn = flip(far_attn, 1), flip(near_attn, 1), cross(near_attn)
    far_inner = join(far_inner)
    near_inner = flip(far_inner, 2)
    far_outer = exchange.gather_far(shard_outer)
    attn_own = (far_attn, near_attn, pair_far_attn, pair_near_attn)
    proj_own, context_own, lse_own = attend_forward(inputs, attn_own, qkv_bias(biases_own), lengths_here)

    across_attn, corner_attn, far_inner, near_inner, far_outer, context_own = gate(
        (across_attn, corner_attn, far_inner, near_inner, far_outer, context_own)
    )
    pair_across_attn, pair_corner_attn = flip(across_attn, 1), flip(corner_attn, 1)
    across_inner = cross(far_inner)
    far_outer = join(far_outer)
    near_outer = flip(far_outer, 2)
    attn_other = (across_attn, corner_attn, pair_across_attn, pair_corner_attn)
    proj_other, context_other, lse_other = attend_forward(inputs, attn_other, qkv_bias(biases_other), lengths_here)

    far_inner, near_inner, across_inner, far_outer, near_outer, context_other = gate(
        (far_inner, near_inner, across_inner, far_outer, near_outer, context_other)
    )
    pair_far_inner, pair_near_inner = flip(far_inner, 1), flip(near_inner, 1)
    corner_inner = flip(across_inner, 2)
    across_outer = cross(far_outer)
    normal_one, scale_one, normed16 = attention_out(context_own, context_other, attn_own, attn_other, inputs, vectors)
    inner_own = (far_inner, near_inner, pair_far_inner, pair_near_inner)
    hidden_own, slope_own = hidden_parts(normed16, inner_own, inner_bias(biases_own))

    across_inner, corner_inner, far_outer, near_outer, across_outer, normed16, hidden_own = gate(
        (across_inner, corner_inner, far_outer, near_outer, across_outer, normed16, hidden_own)
    )
    corner_outer = cross(near_outer)
    pair_across_inner, pair_corner_inner = flip(across_inner, 1), flip(corner_inner, 1)
    pair_far_outer, pair_near_outer = flip(far_outer, 1), flip(near_outer, 1)
    inner_other = (across_inner, corner_inner, pair_across_inner, pair_corner_inner)
    hidden_other, slope_other = hidden_parts(normed16, inner_other, inner_bias(biases_other))

    across_outer, corner_outer, hidden_other = gate((across_outer, corner_outer, hidden_other))
    pair_across_outer, pair_corner_outer = flip(across_outer, 1), flip(corner_outer, 1)
    outer_own = (far_outer, near_outer, pair_far_outer, pair_near_outer)
    outer_other = (across_outer, corner_outer, pair_across_outer, pair_corner_outer)

    mixed, d_before, d_ffn, sums_two = turn(
        hidden_own, hidden_other, outer_own, outer_other, normal_one, cotan, vectors, place16
    )
    upper = model // 4
    inner_width = bias_inner.shape[0]

    def received(array):
        return array.astype(f32)

    send_outer = send_grads(d_ffn, hidden_own, hidden_other)

    send_outer, d_ffn = gate((send_outer, d_ffn))
    pair_outer = flip(send_outer, 1)
    d_inner_own, inner_sums_own = d_hidden(d_ffn, outer_own, slope_own)

    pair_outer, d_ffn, d_inner_own = gate((pair_outer, d_ffn, d_inner_own))
    part = (upper, inner_width)
    keep_outer, *away_outer = keep_grads(
        (d_ffn, hidden_own, hidden_other, pair_outer),
        (
            (0, 1, ((3, 0),), ((0, inner_width, 4, 0, 0),), ((0, inner_width, 5, 0, 0),)),
            (0, 2, ((3, inner_width),), ((0, inner_width, 6, 0, 0),), ((0, inner_width, 7, 0, 0),)),
        ),
        [(part, f32), (part, bf16), (part, bf16), (part, bf16)],
    )

    keep_outer, away_outer, d_ffn = gate((keep_outer, away_outer, d_ffn))
    ring_outer = (flip(away_outer[0], 2), cross(away_outer[1]), flip_cross(away_outer[2], 2))
    d_inner_other, inner_sums_other = d_hidden(d_ffn, outer_other, slope_other)
    send_inner = send_grads(normed16, d_inner_own, d_inner_other)

    send_inner, d_inner_other, normed16 = gate((send_inner, d_inner_other, normed16))
    pair_inner = flip(send_inner, 1)
    d_summed, d_attn, sums_one = d_attention(
        d_inner_own, d_inner_other, inner_own, inner_other, d_before, normal_one, scale_one, vectors
    )
    send_output = send_grads(d_attn, context_own, context_other)

    send_output, d_attn = gate((send_output, d_attn))
    pair_output = flip(send_output, 1)
    d_context_own, d_context_other = d_context(d_attn, attn_own, attn_other)

    pair_output, pair_inner, d_attn, normed16, d_context_other = gate(
        (pair_output, pair_inner, d_attn, normed16, d_context_other)
    )
    cut = 2 * inner_width // 3
    late = inner_width - cut
    rest = late + width
    args = (normed16, d_attn, d_inner_own, d_inner_other, context_own, context_other, pair_inner, pair_output)
    own_cut, own_low, other_cut, own_rest, other_rest, near_rest = range(8, 14)
    first_keep, first_low, first_away, last_keep, last_cross, last_away = keep_grads(
        args,
        (
            (
                0,
                2,
                ((6, 0),),
                ((0, cut, own_cut, 0, 0), (cut, inner_width, own_rest, 0, 0)),
                ((0, cut, own_low, 0, 0), (cut, inner_width, near_rest, 0, 0)),
            ),
            (
                0,
                3,
                ((6, inner_width),),
                ((0, cut, other_cut, 0, 0), (cut, inner_width, other_rest, 0, 0)),
                ((0, cut, other_cut, upper, 0), (cut, inner_width, near_rest, 0, rest)),
            ),
            (1, 4, ((7, 0),), ((0, width, own_rest, 0, late),), ((0, width, near_rest, 0, late),)),
            (1, 5, ((7, width),), ((0, width, other_rest, 0, late),), ((0, width, near_rest, 0, rest + late),)),
        ),
        [
            ((upper, cut), f32),
            ((upper, cut), f32),
            ((2 * upper, cut), bf16),
            ((upper, rest), f32),
            ((upper, rest), f32),
            ((upper, 2 * rest), bf16),
        ],
    )

    first_keep, first_low, first_away, last_keep, last_cross, last_away, d_context_other, keep_outer, ring_outer = gate(
        (first_keep, first_low, first_away, last_keep, last_cross, last_away, d_context_other, keep_outer, ring_outer)
    )
    first_across, last_near = cross(first_away), flip(last_away, 2)
    for piece in ring_outer:
        keep_outer = keep_outer + received(piece)
    keep_outer, lower_outer = exchange.halve_first(keep_outer)
    d_proj_other, qkv_sums_other = attend_backward(
        proj_other, context_other, d_context_other, lse_other, lengths_here
    )
    send_other = send_grads(inputs, d_proj_other)

    send_other, d_proj_other, first_across, last_near, keep_outer, lower_outer = gate(
        (send_other, d_proj_other, first_across, last_near, keep_outer, lower_outer)
    )
    pair_other = flip(send_other, 1)
    first_near = flip((first_low + received(first_across[upper:])).astype(bf16), 2)
    last_across = cross((last_cross + received(last_near[:, rest:])).astype(bf16))
    keep_outer, lower_outer = exchange.halve_rest(keep_outer, lower_outer)

    pair_other, d_proj_other = gate((pair_other, d_proj_other))
    triple = 3 * width
    (away_other,) = keep_grads(
        (inputs, d_proj_other, pair_other),
        ((0, 1, ((2, 0),), ((0, triple, 3, 0, 0),), ((0, triple, 3, upper, 0),)),),
        [((2 * upper, triple), bf16)],
    )

    away_other, d_context_own, qkv_sums_other, first_near, last_across, keep_outer, lower_outer = gate(
        (away_other, d_context_own, qkv_sums_other, first_near, last_across, keep_outer, lower_outer)
    )
    sum_outer = keep_outer + received(lower_outer)
    across_qkv = cross(away_other)
    whole = permuted(jnp.concatenate([sums_one[:3], sums_two[:3]]), ((1,), (1,))).reshape(-1)
    across_small = cross(jnp.concatenate([qkv_sums_other[0], qkv_sums_other[1], inner_sums_other[0], whole]))
    first_keep = first_keep + received(first_across[:upper]) + received(first_near)
    last_keep = last_keep + received(last_near[:, :rest]) + received(last_across)
    keep_mid, lower_mid = exchange.halve_first(jnp.concatenate([first_keep, last_keep], axis=1))
    d_proj_own, qkv_sums_own = attend_backward(proj_own, context_own, d_context_own, lse_own, lengths_here)
    send_own = send_grads(inputs, d_proj_own)
    early = d_inputs(d_summed, d_proj_own, d_proj_other, attn_own, attn_other, place16, 0)

    send_own, d_proj_own, qkv_sums_own, across_small, across_qkv, early, keep_mid, lower_mid = gate(
        (send_own, d_proj_own, qkv_sums_own, across_small, across_qkv, early, keep_mid, lower_mid)
    )
    pair_own = flip(send_own, 1)
    small = jnp.concatenate([qkv_sums_own[0], qkv_sums_own[1], inner_sums_own[0], whole]) + across_small
    pair_small = flip(small, 1)
    keep_mid, lower_mid = exchange.halve_rest(keep_mid, lower_mid)

    pair_own, d_proj_own, small, pair_small = gate((pair_own, d_proj_own, small, pair_small))
    small = small + pair_small
    near_small = flip(small, 2)
    keep_qkv, away_qkv = keep_grads(
        (inputs, d_proj_own, pair_own, across_qkv),
        ((0, 1, ((2, 0), (3, 0)), ((0, triple, 4, 0, 0),), ((0, triple, 5, 0, 0),)),),
        [((upper, triple), f32), ((upper, triple), bf16)],
    )

    keep_qkv, away_qkv, small, near_small, early = gate((keep_qkv, away_qkv, small, near_small, early))
    near_qkv = flip(away_qkv, 2)
    small = small + near_small
    pair_small = exchange.flip(small, exchange.bits[0])
    grad_tokens = d_inputs(d_summed, d_proj_own, d_proj_other, attn_own, attn_other, place16, 1, (early,))

    keep_qkv, near_qkv, small, pair_small, grad_tokens, keep_mid, lower_mid = gate(
        (keep_qkv, near_qkv, small, pair_small, grad_tokens, keep_mid, lower_mid)
    )
    sum_mid = keep_mid + received(lower_mid)
    sum_qkv = exchange.scatter_far(keep_qkv + received(near_qkv))
    small = exchange.total_rest(small + pair_small)

    inner_width = bias_inner.shape[0]
    cuts = np.cumsum([width, width, inner_width] + [model] * 6)
    query_bias, value_bias, inner_bias_sum, *rest = jnp.split(small, cuts[:-1])

    return (
        mixed,
        grad_tokens,
        sum_qkv[:, :width],
        sum_qkv[:, width : 2 * width],
        sum_qkv[:, 2 * width :],
        sum_mid[:, inner_width:].T,
        sum_mid[:, :inner_width],
        sum_outer.T,
        query_bias,
        value_bias,
        rest[0],
        rest[1],
        rest[2],
        inner_bias_sum,
        rest[3],
        rest[4],
        rest[5],
    )


def solution(mesh):
    both = P(("fsdp", "tp"), None)
    cols, rows = P("fsdp", "tp"), P("tp", "fsdp")
    return jax.shard_map(
        shards,
        mesh=mesh,
        in_specs=(both, P("fsdp"), both, cols, cols, cols, rows, cols, rows)
        + (P("tp"), P("tp"), P(), P(), P(), P("tp"), P(), P(), P()),
        out_specs=(both, both, cols, cols, cols, rows, cols, rows)
        + (P("tp"), P("tp"), P(), P(), P(), P("tp"), P(), P(), P()),
        check_vma=False,
    )
```

```python
import functools

import jax
import jax.numpy as jnp
import numpy as np
from jax import lax
from jax.experimental import pallas as pl
from jax.experimental.pallas import tpu as pltpu
from jax.sharding import PartitionSpec as P

DH = 64
SEQ = 512
PAIR = 2 * DH
norm_eps = 1e-12
masked_score = -1000000000.0
bf16 = jnp.bfloat16
f32 = jnp.float32
TILE = 256
COST = dict(
    attend_forward=39,
    attend_backward=0.02,
    attention_out=12,
    hidden=25.5,
    turn=39,
    d_hidden=10.8,
    d_attention=30,
    d_context=20,
    d_inputs=0.02,
    join=3,
    order=3,
    send_grads=0.02,
    keep_grads=10.5,
)


def cost(micros):
    return pl.CostEstimate(flops=int(micros * 9e8), bytes_accessed=1024, transcendentals=0)


def dot_nn(left, right):
    return lax.dot_general(left, right, (((1,), (0,)), ((), ())), preferred_element_type=f32)


def dot_nt(left, right):
    return lax.dot_general(left, right, (((1,), (1,)), ((), ())), preferred_element_type=f32)


def dot_tn(left, right):
    return lax.dot_general(left, right, (((0,), (0,)), ((), ())), preferred_element_type=f32)


ERF_P = 0.3275911
ERF_A = (0.254829592, -0.284496736, 1.421413741, -1.453152027, 1.061405429)


def gelu_parts(values):
    size = jnp.abs(values)
    t = 1.0 / (1.0 + (ERF_P * 2**-0.5) * size)
    expo = jnp.exp(-0.5 * values * values)
    poly = ERF_A[4]
    for coefficient in ERF_A[3::-1]:
        poly = poly * t + coefficient
    tail = (0.5 * poly) * (t * expo)
    phi = jnp.where(values < 0, tail, 1.0 - tail)
    return values * phi, phi + values * (expo * (2 * np.pi) ** -0.5)


def norm_parts(values):
    centred = values - jnp.mean(values, axis=-1, keepdims=True)
    scale = lax.rsqrt(jnp.mean(centred * centred, axis=-1, keepdims=True) + norm_eps)
    return centred * scale, scale


def norm_pull(grads, gain, normal, scale):
    inner = grads * gain
    return scale * (
        inner
        - jnp.mean(inner, axis=-1, keepdims=True)
        - normal * jnp.mean(inner * normal, axis=-1, keepdims=True)
    )


def fill(ref, column, pieces, start, width):
    part = pieces[0].shape[0]
    step = 32 if part % 32 == 0 else part
    for index, piece in enumerate(pieces):

        def one(at, carry, piece=piece, base=index * part):
            rows = pl.ds(pl.multiple_of(at * step, step), step)
            to = pl.ds(pl.multiple_of(base + at * step, step), step)
            ref[to, column : column + width] = piece[rows, start : start + width]
            return carry

        lax.fori_loop(0, part // step, one, 0)


def head_slice(block, head):
    return block[:, head * DH : (head + 1) * DH]


def live_rows(lengths_ref):
    rows = lax.broadcasted_iota(jnp.int32, (SEQ, 1), 0)
    return rows < lengths_ref[pl.program_id(0)]


def attend_forward_kernel(
    pairs, lengths_ref, inputs_ref, a_ref, b_ref, c_ref, d_ref, shift_ref, qkv_ref, context_ref, lse_ref, weight_ref
):
    live = live_rows(lengths_ref)
    width = pairs * PAIR

    @pl.when(pl.program_id(0) == 0)
    def _():
        fill(weight_ref, 0, (a_ref, b_ref, c_ref, d_ref), 0, 3 * width)

    qkv_ref[...] = (dot_nn(inputs_ref[...], weight_ref[...]) + shift_ref[...]).astype(bf16)

    def one_pair(index, carry):
        at = pl.multiple_of(index * PAIR, PAIR)
        query = qkv_ref[:, pl.ds(at, PAIR)] * jnp.asarray(DH ** (-0.5), bf16)
        keys = qkv_ref[:, pl.ds(width + at, PAIR)]
        values = qkv_ref[:, pl.ds(2 * width + at, PAIR)]
        turned = []
        for head in range(2):
            scores = dot_nt(head_slice(keys, head), head_slice(query, head))
            scores = jnp.where(live, scores, masked_score)
            top = jnp.max(scores, axis=0, keepdims=True)
            expo = jnp.exp(scores - top)
            total = jnp.sum(expo, axis=0, keepdims=True)
            probs = (expo * (1.0 / total)).astype(bf16)
            turned.append(dot_tn(head_slice(values, head), probs))
            lse_ref[0, pl.ds(index * 2 + head, 1), :] = top + jnp.log(total)
        context_ref[:, pl.ds(at, PAIR)] = jnp.concatenate(turned, axis=0).T.astype(bf16)
        return carry

    lax.fori_loop(0, pairs, one_pair, 0)


def attend_forward(inputs, pieces, shift, lengths):
    rows, model = inputs.shape
    part, _ = pieces[0].shape
    triple = shift.shape[0]
    width = triple // 3
    seqs, pairs = rows // SEQ, width // PAIR
    heads = 2 * pairs
    piece_spec = pl.BlockSpec((part, triple), lambda s, n: (0, 0), pipeline_mode=pl.Buffered(1))
    return pl.pallas_call(
        functools.partial(attend_forward_kernel, pairs),
        grid_spec=pltpu.PrefetchScalarGridSpec(
            num_scalar_prefetch=1,
            grid=(seqs,),
            in_specs=[pl.BlockSpec((SEQ, model), lambda s, n: (s, 0))]
            + [piece_spec] * 4
            + [pl.BlockSpec((1, triple), lambda s, n: (0, 0))],
            out_specs=[
                pl.BlockSpec((SEQ, triple), lambda s, n: (s, 0)),
                pl.BlockSpec((SEQ, width), lambda s, n: (s, 0)),
                pl.BlockSpec((1, heads, SEQ), lambda s, n: (s, 0, 0)),
            ],
            scratch_shapes=[pltpu.VMEM((model, triple), bf16)],
        ),
        out_shape=[
            jax.ShapeDtypeStruct((rows, triple), bf16),
            jax.ShapeDtypeStruct((rows, width), bf16),
            jax.ShapeDtypeStruct((seqs, heads, SEQ), f32),
        ],
        compiler_params=pltpu.CompilerParams(vmem_limit_bytes=18 << 20),
        cost_estimate=cost(COST["attend_forward"]),
        name="attend_forward",
    )(lengths, inputs, *pieces, shift[None, :])


def attend_backward_kernel(pairs, lengths_ref, qkv_ref, context_ref, d_context_ref, lse_ref, out_ref, sums_ref):
    live = live_rows(lengths_ref)

    @pl.when(pl.program_id(0) == 0)
    def _():
        sums_ref[...] = jnp.zeros_like(sums_ref)

    width = pairs * PAIR
    scale = DH ** (-0.5)

    def one_pair(index, carry):
        at = pl.multiple_of(index * PAIR, PAIR)
        query = qkv_ref[:, pl.ds(at, PAIR)] * jnp.asarray(scale, bf16)
        keys = qkv_ref[:, pl.ds(width + at, PAIR)]
        values = qkv_ref[:, pl.ds(2 * width + at, PAIR)]
        d_context = d_context_ref[:, pl.ds(at, PAIR)]
        weighed = (context_ref[:, pl.ds(at, PAIR)].astype(f32) * d_context.astype(f32)).T
        d_query, d_key, d_value = [], [], []
        for head in range(2):
            q_h, k_h, v_h = head_slice(query, head), head_slice(keys, head), head_slice(values, head)
            g_h = head_slice(d_context, head)
            row_dot = jnp.sum(weighed[head * DH : (head + 1) * DH], axis=0, keepdims=True)
            scores = jnp.where(live, dot_nt(k_h, q_h), masked_score)
            probs = jnp.exp(scores - lse_ref[0, pl.ds(index * 2 + head, 1), :])
            d_probs = dot_nt(v_h, g_h)
            d_scores = (probs * (d_probs - row_dot)).astype(bf16)
            d_value.append(dot_nn(probs.astype(bf16), g_h))
            d_key.append(dot_nn(d_scores, q_h))
            d_query.append(dot_tn(k_h, d_scores))
        turned = (jnp.concatenate(d_query, axis=0).T * scale).astype(bf16)
        d_value = jnp.concatenate(d_value, axis=1).astype(bf16)
        out_ref[:, pl.ds(at, PAIR)] = turned
        out_ref[:, pl.ds(width + at, PAIR)] = jnp.concatenate(d_key, axis=1).astype(bf16)
        out_ref[:, pl.ds(2 * width + at, PAIR)] = d_value
        sums_ref[0:1, pl.ds(at, PAIR)] += jnp.sum(turned.astype(f32), axis=0, keepdims=True)
        sums_ref[1:2, pl.ds(at, PAIR)] += jnp.sum(d_value.astype(f32), axis=0, keepdims=True)
        return carry

    lax.fori_loop(0, pairs, one_pair, 0)


def attend_backward(qkv, context, d_context, lse, lengths):
    rows, triple = qkv.shape
    width = triple // 3
    seqs, pairs = rows // SEQ, width // PAIR
    heads = 2 * pairs
    return pl.pallas_call(
        functools.partial(attend_backward_kernel, pairs),
        grid_spec=pltpu.PrefetchScalarGridSpec(
            num_scalar_prefetch=1,
            grid=(seqs,),
            in_specs=[
                pl.BlockSpec((SEQ, triple), lambda s, n: (s, 0)),
                pl.BlockSpec((SEQ, width), lambda s, n: (s, 0)),
                pl.BlockSpec((SEQ, width), lambda s, n: (s, 0)),
                pl.BlockSpec((1, heads, SEQ), lambda s, n: (s, 0, 0)),
            ],
            out_specs=[
                pl.BlockSpec((SEQ, triple), lambda s, n: (s, 0)),
                pl.BlockSpec((8, width), lambda s, n: (0, 0)),
            ],
        ),
        out_shape=[jax.ShapeDtypeStruct((rows, triple), bf16), jax.ShapeDtypeStruct((8, width), f32)],
        compiler_params=pltpu.CompilerParams(vmem_limit_bytes=14 << 20),
        cost_estimate=cost(COST["attend_backward"]),
        name="attend_backward",
    )(lengths, qkv, context, d_context, lse)


def in_vmem(kernel, name, limit, outs, *args, scratch=(), aliases=None):
    return pl.pallas_call(
        kernel,
        in_specs=[pl.BlockSpec(memory_space=pltpu.VMEM)] * len(args),
        out_specs=[pl.BlockSpec(memory_space=pltpu.VMEM)] * len(outs),
        out_shape=[jax.ShapeDtypeStruct(*out) for out in outs],
        scratch_shapes=[pltpu.VMEM(shape, bf16) for shape in scratch],
        input_output_aliases=aliases or {},
        compiler_params=pltpu.CompilerParams(vmem_limit_bytes=limit << 20),
        cost_estimate=cost(COST[name]),
        name=name,
    )(*args)


def tiles_of(ref, body):
    def one(index, carry):
        body(pl.ds(pl.multiple_of(index * TILE, TILE), TILE))
        return carry

    lax.fori_loop(0, ref.shape[0] // TILE, one, 0)


def add_sums(ref, row, values):
    ref[row : row + 1, :] += jnp.sum(values, axis=0, keepdims=True)


def side(one, other):
    return jnp.concatenate([one, other], axis=1)


def join_kernel(*refs):
    *pieces, out_ref = refs
    fill(out_ref, 0, pieces, 0, out_ref.shape[1])


def join(arrays):
    if len(arrays) == 1:
        return arrays[0]
    rows, width = arrays[0].shape
    if rows % 16:
        return jnp.concatenate(arrays, axis=0)
    return in_vmem(join_kernel, "join", 8, [((len(arrays) * rows, width), arrays[0].dtype)], *arrays)[0]


def exact_dot(dot, vectors, place):
    parts, left = [], vectors
    for _ in range(3):
        part = left.astype(bf16).astype(f32)
        parts.append(part)
        left = left - part
    count = vectors.shape[0]
    result = dot(jnp.concatenate(parts, axis=0).astype(bf16), place)
    return result[:count] + result[count : 2 * count] + result[2 * count :]


def order_kernel(rows_ref, vectors_ref, place_ref, out_ref, ordered_ref):
    ordered_ref[...] = exact_dot(dot_nn, vectors_ref[...], place_ref[...])

    def body(at):
        out_ref[at] = dot_nn(rows_ref[at], place_ref[...]).astype(bf16)

    tiles_of(rows_ref, body)


def order(rows, vectors, place):
    outs = [(rows.shape, bf16), (vectors.shape, f32)]
    return in_vmem(order_kernel, "order", 8, outs, rows, vectors, place)


def small_kernel(one_ref, two_ref, qkv_ref, inner_ref, place_ref, out_ref):
    whole = exact_dot(dot_nt, jnp.concatenate([one_ref[...], two_ref[...]], axis=0), place_ref[...])
    model = out_ref.shape[1]
    rows = inner_ref.shape[1] // model
    out_ref[...] = jnp.zeros_like(out_ref)
    out_ref[0:1] = side(qkv_ref[0:1], qkv_ref[1:2])
    for index in range(rows):
        out_ref[1 + index : 2 + index] = inner_ref[0:1, index * model : (index + 1) * model]
    out_ref[1 + rows : 4 + rows] = whole[:3]
    out_ref[4 + rows : 7 + rows] = whole[8:11]


def small_sums(one, two, qkv, inner, place):
    return in_vmem(small_kernel, "order", 8, [((16, place.shape[0]), f32)], one, two, qkv, inner, place)[0]


def attention_out_kernel(own_ref, other_ref, *refs):
    pieces, (inputs_ref, vectors_ref, normal_ref, scale_ref, normed_ref, weight_ref) = refs[:8], refs[8:]
    width = own_ref.shape[1]
    fill(weight_ref, 0, pieces[:4], 3 * width, width)
    fill(weight_ref, width, pieces[4:], 3 * width, width)

    def body(at):
        mixed = dot_nt(side(own_ref[at], other_ref[at]), weight_ref[...])
        normal, scale = norm_parts(mixed + vectors_ref[0:1] + inputs_ref[at].astype(f32))
        normal_ref[at] = normal
        scale_ref[at] = scale
        normed_ref[at] = (normal * vectors_ref[1:2] + vectors_ref[2:3]).astype(bf16)

    tiles_of(own_ref, body)


def attention_out(own, other, w_own, w_other, inputs, vectors):
    shape = inputs.shape
    outs = [(shape, f32), ((shape[0], 1), f32), (shape, bf16)]
    args = (own, other, *w_own, *w_other, inputs, vectors)
    return in_vmem(attention_out_kernel, "attention_out", 6, outs, *args, scratch=[(shape[1], shape[1])])


def hidden_kernel(normed_ref, *refs):
    pieces, (shift_ref, hidden_ref, slope_ref, weight_ref) = refs[:4], refs[4:]
    fill(weight_ref, 0, pieces, 0, weight_ref.shape[1])

    def body(at):
        hidden, slope = gelu_parts(dot_nn(normed_ref[at], weight_ref[...]) + shift_ref[...])
        hidden_ref[at] = hidden.astype(bf16)
        slope_ref[at] = slope.astype(bf16)

    tiles_of(normed_ref, body)


def hidden_parts(normed, w, shift):
    rows, model = normed.shape
    shape = (rows, w[0].shape[1])
    outs = [(shape, bf16), (shape, bf16)]
    args = (normed, *w, shift[None, :])
    return in_vmem(hidden_kernel, "hidden", 8, outs, *args, scratch=[(model, shape[1])])


def turn_kernel(own_ref, other_ref, *refs):
    pieces, (normal_one_ref, cotan_ref, vectors_ref, place_ref) = refs[:8], refs[8:12]
    mixed_ref, d_before_ref, d_ffn_ref, sums_ref, w_own_ref, w_other_ref = refs[12:]
    sums_ref[...] = jnp.zeros_like(sums_ref)
    fill(w_own_ref, 0, pieces[:4], 0, w_own_ref.shape[1])
    fill(w_other_ref, 0, pieces[4:], 0, w_other_ref.shape[1])

    def body(at):
        ffn = dot_nt(own_ref[at], w_own_ref[...]) + dot_nt(other_ref[at], w_other_ref[...])
        normed = normal_one_ref[at] * vectors_ref[1:2] + vectors_ref[2:3]
        normal, scale = norm_parts(ffn + vectors_ref[3:4] + normed)
        result = (normal * vectors_ref[4:5] + vectors_ref[5:6]).astype(bf16)
        mixed_ref[at] = dot_nt(result, place_ref[...]).astype(bf16)
        cotan = cotan_ref[at].astype(f32)
        d_before = norm_pull(cotan, vectors_ref[4:5], normal, scale)
        d_before_ref[at] = d_before
        d_ffn_ref[at] = d_before.astype(bf16)
        add_sums(sums_ref, 0, d_before)
        add_sums(sums_ref, 1, cotan * normal)
        add_sums(sums_ref, 2, cotan)

    tiles_of(own_ref, body)


def turn(own, other, w_own, w_other, normal_one, cotan, vectors, place):
    shape = normal_one.shape
    outs = [(shape, bf16), (shape, f32), (shape, bf16), ((8, shape[1]), f32)]
    args = (own, other, *w_own, *w_other, normal_one, cotan, vectors, place)
    scratch = [(shape[1], own.shape[1])] * 2
    return in_vmem(turn_kernel, "turn", 10, outs, *args, scratch=scratch, aliases={11: 2})


def d_hidden_kernel(d_ffn_ref, *refs):
    pieces, (slope_ref, d_inner_ref, sums_ref, weight_ref) = refs[:4], refs[4:]
    sums_ref[...] = jnp.zeros_like(sums_ref)
    fill(weight_ref, 0, pieces, 0, weight_ref.shape[1])

    def body(at):
        d_inner = (dot_nn(d_ffn_ref[at], weight_ref[...]) * slope_ref[at].astype(f32)).astype(bf16)
        d_inner_ref[at] = d_inner
        add_sums(sums_ref, 0, d_inner.astype(f32))

    tiles_of(d_ffn_ref, body)


def d_hidden(d_ffn, w, slope):
    outs = [(slope.shape, bf16), ((8, slope.shape[1]), f32)]
    args = (d_ffn, *w, slope)
    scratch = [(d_ffn.shape[1], slope.shape[1])]
    return in_vmem(d_hidden_kernel, "d_hidden", 8, outs, *args, scratch=scratch, aliases={5: 0})


def d_attention_kernel(own_ref, other_ref, *refs):
    pieces, (d_before_ref, normal_ref, scale_ref, vectors_ref) = refs[:8], refs[8:12]
    d_summed_ref, d_attn_ref, sums_ref, w_own_ref, w_other_ref = refs[12:]
    sums_ref[...] = jnp.zeros_like(sums_ref)
    fill(w_own_ref, 0, pieces[:4], 0, w_own_ref.shape[1])
    fill(w_other_ref, 0, pieces[4:], 0, w_other_ref.shape[1])

    def body(at):
        d_normed = d_before_ref[at] + dot_nt(own_ref[at], w_own_ref[...]) + dot_nt(other_ref[at], w_other_ref[...])
        normal = normal_ref[at]
        d_summed = norm_pull(d_normed, vectors_ref[1:2], normal, scale_ref[at])
        d_summed_ref[at] = d_summed
        d_attn_ref[at] = d_summed.astype(bf16)
        add_sums(sums_ref, 0, d_summed)
        add_sums(sums_ref, 1, d_normed * normal)
        add_sums(sums_ref, 2, d_normed)

    tiles_of(own_ref, body)


def d_attention(own, other, w_own, w_other, d_before, normal, scale, vectors):
    shape = d_before.shape
    outs = [(shape, f32), (shape, bf16), ((8, shape[1]), f32)]
    args = (own, other, *w_own, *w_other, d_before, normal, scale, vectors)
    scratch = [(shape[1], own.shape[1])] * 2
    return in_vmem(d_attention_kernel, "d_attention", 10, outs, *args, scratch=scratch, aliases={10: 0})


def d_context_kernel(d_attn_ref, *refs):
    pieces, (own_ref, other_ref, weight_ref) = refs[:8], refs[8:]
    width = own_ref.shape[1]
    fill(weight_ref, 0, pieces[:4], 3 * width, width)
    fill(weight_ref, width, pieces[4:], 3 * width, width)

    def body(at):
        result = dot_nn(d_attn_ref[at], weight_ref[...]).astype(bf16)
        own_ref[at] = result[:, :width]
        other_ref[at] = result[:, width:]

    tiles_of(d_attn_ref, body)


def d_context(d_attn, w_own, w_other):
    rows, model = d_attn.shape
    outs = [((rows, model // 2), bf16)] * 2
    return in_vmem(d_context_kernel, "d_context", 5, outs, d_attn, *w_own, *w_other, scratch=[(model, model)])


def d_inputs_kernel(d_summed_ref, own_ref, other_ref, *refs):
    pieces, place_ref, (out_ref, weight_ref) = refs[:8], refs[8], refs[-2:]
    triple = own_ref.shape[1]

    @pl.when(pl.program_id(0) == 0)
    def _():
        fill(weight_ref, 0, pieces[:4], 0, triple)
        fill(weight_ref, triple, pieces[4:], 0, triple)

    grads = d_summed_ref[...] + dot_nt(side(own_ref[...], other_ref[...]), weight_ref[...])
    high = grads.astype(bf16)
    low = (grads - high.astype(f32)).astype(bf16)
    out_ref[...] = dot_nt(high, place_ref[...]) + dot_nt(low, place_ref[...])


def d_inputs(d_summed, own, other, w_own, w_other, place, half, earlier=()):
    rows, model = d_summed.shape
    part, triple = w_own[0].shape[0], own.shape[1]
    steps = rows // 2 // TILE

    def tile(width):
        return pl.BlockSpec((TILE, width), lambda i: (i + half * steps, 0))

    def fixed(shape):
        return pl.BlockSpec(shape, lambda i: (0, 0), pipeline_mode=pl.Buffered(1))

    args = (d_summed, own, other, *w_own, *w_other, place)
    return pl.pallas_call(
        d_inputs_kernel,
        grid=(steps,),
        in_specs=[tile(model), tile(triple), tile(triple)]
        + [fixed((part, triple))] * 8
        + [fixed(place.shape)]
        + [pl.BlockSpec(memory_space=pl.ANY)] * len(earlier),
        out_specs=tile(model),
        out_shape=jax.ShapeDtypeStruct((rows, model), f32),
        scratch_shapes=[pltpu.VMEM((model, 2 * triple), bf16)],
        input_output_aliases={len(args): 0} if earlier else {},
        compiler_params=pltpu.CompilerParams(vmem_limit_bytes=18 << 20),
        cost_estimate=cost(COST["d_inputs"]),
        name="d_inputs",
    )(*args, *earlier)


def chunks(width):
    step = next(step for step in (512, 384, 256, 128) if width % step == 0)
    return [(start, step) for start in range(0, width, step)]


def send_kernel(left_ref, *refs):
    *rights, out_ref = refs
    half = left_ref.shape[1] // 2
    left = left_ref[:, half:]
    base = 0
    for right_ref in rights:
        for start, step in chunks(right_ref.shape[1]):
            part = dot_tn(left, right_ref[:, start : start + step])
            out_ref[:, base + start : base + start + step] = part.astype(bf16)
        base += right_ref.shape[1]


def send_grads(left, *rights):
    outs = [((left.shape[1] // 2, sum(right.shape[1] for right in rights)), bf16)]
    return in_vmem(send_kernel, "send_grads", 5, outs, left, *rights)[0]


def keep_kernel(terms, *refs):
    for left_at, right_at, adds, upper, lower in terms:
        left_ref, right_ref = refs[left_at], refs[right_at]
        half = left_ref.shape[1] // 2
        left = left_ref[:, :half]
        for start, step in chunks(right_ref.shape[1]):
            total = dot_tn(left, right_ref[:, start : start + step])
            for add_at, column in adds:
                total = total + refs[add_at][:, column + start : column + start + step].astype(f32)
            for part, places in ((total[: half // 2], upper), (total[half // 2 :], lower)):
                for first, last, out_at, row, column in places:
                    if first <= start < last:
                        out_ref = refs[out_at]
                        to = column + start - first
                        out_ref[row : row + half // 2, to : to + step] = part.astype(out_ref.dtype)


def keep_grads(args, terms, outs):
    return in_vmem(functools.partial(keep_kernel, terms), "keep_grads", 8, outs, *args)


class Exchange:
    def __init__(self, fsdp):
        self.fsdp = fsdp
        bits = [1 << i for i in range(2, fsdp.bit_length() - 1)]
        self.bits, self.far = bits, []
        for i in range(0, len(bits), 2):
            steps = [0]
            for bit in bits[i : i + 2]:
                steps = steps + [step ^ bit for step in steps]
            self.far.append(steps)
        self.masks = [0]
        for steps in self.far + [[0, 2], [0, 1]]:
            self.masks = [step ^ mask for step in steps for mask in self.masks]

    def flip(self, array, bit):
        return lax.ppermute(array, "fsdp", [(i, i ^ bit) for i in range(self.fsdp)])

    def cross(self, array):
        return lax.ppermute(array, "tp", [(0, 1), (1, 0)])

    def flip_cross(self, array, bit):
        pairs = [(2 * i + j, 2 * (i ^ bit) + 1 - j) for i in range(self.fsdp) for j in range(2)]
        return lax.ppermute(array, ("fsdp", "tp"), pairs)

    def gather_far(self, array):
        for steps in self.far[:-1]:
            array = join([array] + [self.flip(array, step) for step in steps[1:]])
        return [array] + [self.flip(array, step) for step in self.far[-1][1:]]

    def scatter_far(self, array):
        for steps in reversed(self.far):
            size = array.shape[0] // len(steps)
            parts = [array[i * size : (i + 1) * size] for i in range(len(steps))]
            array = parts[0]
            for part, step in zip(parts[1:], steps[1:]):
                array = array + self.flip(part.astype(bf16), step).astype(f32)
        return array

    def halve(self, parts, bit):
        away = self.flip(jnp.concatenate(parts[1::2], axis=0).astype(bf16), bit)
        size = parts[0].shape[0]
        return parts[::2], [away[at : at + size] for at in range(0, away.shape[0], size)]

    def halve_first(self, array):
        size = array.shape[0] >> len(self.bits)
        return self.halve([array[at : at + size] for at in range(0, array.shape[0], size)], self.bits[0])

    def halve_rest(self, keep, away):
        for bit in self.bits[1:]:
            keep, away = self.halve([mine + theirs.astype(f32) for mine, theirs in zip(keep, away)], bit)
        return keep[0], away[0]

    def total_rest(self, array):
        for bit in self.bits[1:]:
            array = array + self.flip(array, bit)
        return array


def gate(values, *others):
    return lax.optimization_barrier((values, others))[0]


def shards(
    tokens,
    lengths,
    cotangent,
    w_query,
    w_key,
    w_value,
    w_output,
    w_inner,
    w_outer,
    bias_query,
    bias_value,
    bias_output,
    norm1_gain,
    norm1_bias,
    bias_inner,
    bias_outer,
    norm2_gain,
    norm2_bias,
):
    fsdp = lax.axis_size("fsdp")
    exchange = Exchange(fsdp)
    rows, model = tokens.shape
    seqs = rows // SEQ
    block = w_query.shape[0]
    width = w_query.shape[1]
    half = model // 2

    here = lax.axis_index("fsdp")
    masks = jnp.repeat(jnp.asarray(exchange.masks, jnp.int32), block)
    inside = jnp.tile(jnp.arange(block, dtype=jnp.int32), fsdp)
    source = (here ^ masks) * block + inside
    place = jnp.arange(model, dtype=jnp.int32)[:, None] == source[None, :]
    place16 = place.astype(bf16)
    lengths_here = lax.dynamic_slice_in_dim(lengths, lax.axis_index("tp") * seqs, seqs, 0)

    zero = jnp.zeros((width,), f32)

    def qkv_bias(biases):
        return jnp.concatenate([biases[:width], zero, biases[width : 2 * width]])

    def inner_bias(biases):
        return biases[2 * width :]

    flip, cross, flip_cross = exchange.flip, exchange.cross, exchange.flip_cross

    shard_attn = jnp.concatenate([w_query, w_key, w_value, w_output.T], axis=1).astype(bf16)
    biases_own = jnp.concatenate([bias_query, bias_value, bias_inner])
    far_attn = exchange.gather_far(shard_attn)
    biases_other = cross(biases_own)
    inputs = dot_nn(tokens, place16).astype(bf16)
    shard_inner, shard_outer = w_inner.astype(bf16), w_outer.T.astype(bf16)
    vectors = jnp.stack([bias_output, norm1_gain, norm1_bias, bias_outer, norm2_gain, norm2_bias, bias_output, bias_output])

    far_attn, shard_inner, shard_outer, biases_other, cotangent, vectors, inputs = gate(
        (far_attn, shard_inner, shard_outer, biases_other, cotangent, vectors, inputs)
    )
    far_attn = join(far_attn)
    near_attn, across_attn = flip(far_attn, 2), cross(far_attn)
    far_inner = exchange.gather_far(shard_inner)
    cotan, vectors = order(cotangent, vectors, place16)

    far_attn, near_attn, across_attn, far_inner, shard_outer, inputs = gate(
        (far_attn, near_attn, across_attn, far_inner, shard_outer, inputs), cotan, vectors
    )
    pair_far_attn, pair_near_attn, corner_attn = flip(far_attn, 1), flip(near_attn, 1), cross(near_attn)
    far_inner = join(far_inner)
    near_inner = flip(far_inner, 2)
    far_outer = exchange.gather_far(shard_outer)
    attn_own = (far_attn, near_attn, pair_far_attn, pair_near_attn)
    proj_own, context_own, lse_own = attend_forward(inputs, attn_own, qkv_bias(biases_own), lengths_here)

    across_attn, corner_attn, far_inner, near_inner, far_outer, context_own = gate(
        (across_attn, corner_attn, far_inner, near_inner, far_outer, context_own)
    )
    pair_across_attn, pair_corner_attn = flip(across_attn, 1), flip(corner_attn, 1)
    across_inner = cross(far_inner)
    far_outer = join(far_outer)
    near_outer = flip(far_outer, 2)
    attn_other = (across_attn, corner_attn, pair_across_attn, pair_corner_attn)
    proj_other, context_other, lse_other = attend_forward(inputs, attn_other, qkv_bias(biases_other), lengths_here)

    far_inner, near_inner, across_inner, far_outer, near_outer, context_other = gate(
        (far_inner, near_inner, across_inner, far_outer, near_outer, context_other)
    )
    pair_far_inner, pair_near_inner = flip(far_inner, 1), flip(near_inner, 1)
    corner_inner = flip(across_inner, 2)
    across_outer = cross(far_outer)
    normal_one, scale_one, normed16 = attention_out(context_own, context_other, attn_own, attn_other, inputs, vectors)
    inner_own = (far_inner, near_inner, pair_far_inner, pair_near_inner)
    hidden_own, slope_own = hidden_parts(normed16, inner_own, inner_bias(biases_own))

    across_inner, corner_inner, far_outer, near_outer, across_outer, normed16, hidden_own = gate(
        (across_inner, corner_inner, far_outer, near_outer, across_outer, normed16, hidden_own)
    )
    corner_outer = cross(near_outer)
    pair_across_inner, pair_corner_inner = flip(across_inner, 1), flip(corner_inner, 1)
    pair_far_outer, pair_near_outer = flip(far_outer, 1), flip(near_outer, 1)
    inner_other = (across_inner, corner_inner, pair_across_inner, pair_corner_inner)
    hidden_other, slope_other = hidden_parts(normed16, inner_other, inner_bias(biases_other))

    across_outer, corner_outer, hidden_other = gate((across_outer, corner_outer, hidden_other))
    pair_across_outer, pair_corner_outer = flip(across_outer, 1), flip(corner_outer, 1)
    outer_own = (far_outer, near_outer, pair_far_outer, pair_near_outer)
    outer_other = (across_outer, corner_outer, pair_across_outer, pair_corner_outer)

    mixed, d_before, d_ffn, sums_two = turn(
        hidden_own, hidden_other, outer_own, outer_other, normal_one, cotan, vectors, place16
    )
    upper = model // 4
    inner_width = bias_inner.shape[0]

    def received(array):
        return array.astype(f32)

    send_outer = send_grads(d_ffn, hidden_own, hidden_other)

    send_outer, d_ffn = gate((send_outer, d_ffn))
    pair_outer = flip(send_outer, 1)
    d_inner_own, inner_sums_own = d_hidden(d_ffn, outer_own, slope_own)

    pair_outer, d_ffn, d_inner_own = gate((pair_outer, d_ffn, d_inner_own))
    part = (upper, inner_width)
    keep_outer, *away_outer = keep_grads(
        (d_ffn, hidden_own, hidden_other, pair_outer),
        (
            (0, 1, ((3, 0),), ((0, inner_width, 4, 0, 0),), ((0, inner_width, 5, 0, 0),)),
            (0, 2, ((3, inner_width),), ((0, inner_width, 6, 0, 0),), ((0, inner_width, 7, 0, 0),)),
        ),
        [(part, f32), (part, bf16), (part, bf16), (part, bf16)],
    )

    keep_outer, away_outer, d_ffn = gate((keep_outer, away_outer, d_ffn))
    ring_outer = (flip(away_outer[0], 2), cross(away_outer[1]), flip_cross(away_outer[2], 2))
    d_inner_other, inner_sums_other = d_hidden(d_ffn, outer_other, slope_other)
    send_inner = send_grads(normed16, d_inner_own, d_inner_other)

    send_inner, d_inner_other, normed16 = gate((send_inner, d_inner_other, normed16))
    pair_inner = flip(send_inner, 1)
    d_summed, d_attn, sums_one = d_attention(
        d_inner_own, d_inner_other, inner_own, inner_other, d_before, normal_one, scale_one, vectors
    )
    send_output = send_grads(d_attn, context_own, context_other)

    send_output, d_attn = gate((send_output, d_attn))
    pair_output = flip(send_output, 1)
    d_context_own, d_context_other = d_context(d_attn, attn_own, attn_other)

    pair_output, pair_inner, d_attn, normed16, d_context_other = gate(
        (pair_output, pair_inner, d_attn, normed16, d_context_other)
    )
    cut = 2 * inner_width // 3
    late = inner_width - cut
    rest = late + width
    args = (normed16, d_attn, d_inner_own, d_inner_other, context_own, context_other, pair_inner, pair_output)
    own_cut, own_low, other_cut, own_rest, other_rest, near_rest = range(8, 14)
    first_keep, first_low, first_away, last_keep, last_cross, last_away = keep_grads(
        args,
        (
            (
                0,
                2,
                ((6, 0),),
                ((0, cut, own_cut, 0, 0), (cut, inner_width, own_rest, 0, 0)),
                ((0, cut, own_low, 0, 0), (cut, inner_width, near_rest, 0, 0)),
            ),
            (
                0,
                3,
                ((6, inner_width),),
                ((0, cut, other_cut, 0, 0), (cut, inner_width, other_rest, 0, 0)),
                ((0, cut, other_cut, upper, 0), (cut, inner_width, near_rest, 0, rest)),
            ),
            (1, 4, ((7, 0),), ((0, width, own_rest, 0, late),), ((0, width, near_rest, 0, late),)),
            (1, 5, ((7, width),), ((0, width, other_rest, 0, late),), ((0, width, near_rest, 0, rest + late),)),
        ),
        [
            ((upper, cut), f32),
            ((upper, cut), f32),
            ((2 * upper, cut), bf16),
            ((upper, rest), f32),
            ((upper, rest), f32),
            ((upper, 2 * rest), bf16),
        ],
    )

    first_keep, first_low, first_away, last_keep, last_cross, last_away, d_context_other, keep_outer, ring_outer = gate(
        (first_keep, first_low, first_away, last_keep, last_cross, last_away, d_context_other, keep_outer, ring_outer)
    )
    first_across, last_near = cross(first_away), flip(last_away, 2)
    for piece in ring_outer:
        keep_outer = keep_outer + received(piece)
    keep_outer, lower_outer = exchange.halve_first(keep_outer)
    d_proj_other, qkv_sums_other = attend_backward(
        proj_other, context_other, d_context_other, lse_other, lengths_here
    )
    send_other = send_grads(inputs, d_proj_other)

    send_other, d_proj_other, first_across, last_near, keep_outer, lower_outer = gate(
        (send_other, d_proj_other, first_across, last_near, keep_outer, lower_outer)
    )
    pair_other = flip(send_other, 1)
    first_near = flip((first_low + received(first_across[upper:])).astype(bf16), 2)
    last_across = cross((last_cross + received(last_near[:, rest:])).astype(bf16))
    keep_outer, lower_outer = exchange.halve_rest(keep_outer, lower_outer)

    pair_other, d_proj_other, qkv_sums_other, sums_one, sums_two = gate(
        (pair_other, d_proj_other, qkv_sums_other, sums_one, sums_two)
    )
    small_other = small_sums(sums_one, sums_two, qkv_sums_other, inner_sums_other, place16)
    triple = 3 * width
    (away_other,) = keep_grads(
        (inputs, d_proj_other, pair_other),
        ((0, 1, ((2, 0),), ((0, triple, 3, 0, 0),), ((0, triple, 3, upper, 0),)),),
        [((2 * upper, triple), bf16)],
    )

    away_other, d_context_own, small_other, first_near, last_across, keep_outer, lower_outer = gate(
        (away_other, d_context_own, small_other, first_near, last_across, keep_outer, lower_outer)
    )
    sum_outer = keep_outer + received(lower_outer)
    across_qkv = cross(away_other)
    across_small = cross(small_other)
    first_keep = first_keep + received(first_across[:upper]) + received(first_near)
    last_keep = last_keep + received(last_near[:, :rest]) + received(last_across)
    keep_mid, lower_mid = exchange.halve_first(jnp.concatenate([first_keep, last_keep], axis=1))
    d_proj_own, qkv_sums_own = attend_backward(proj_own, context_own, d_context_own, lse_own, lengths_here)
    send_own = send_grads(inputs, d_proj_own)
    early = d_inputs(d_summed, d_proj_own, d_proj_other, attn_own, attn_other, place16, 0)

    send_own, d_proj_own, qkv_sums_own, across_small, across_qkv, early, keep_mid, lower_mid = gate(
        (send_own, d_proj_own, qkv_sums_own, across_small, across_qkv, early, keep_mid, lower_mid)
    )
    pair_own = flip(send_own, 1)
    small = across_small + small_sums(sums_one, sums_two, qkv_sums_own, inner_sums_own, place16)
    pair_small = flip(small, 1)
    keep_mid, lower_mid = exchange.halve_rest(keep_mid, lower_mid)

    pair_own, d_proj_own, small, pair_small = gate((pair_own, d_proj_own, small, pair_small))
    small = small + pair_small
    near_small = flip(small, 2)
    keep_qkv, away_qkv = keep_grads(
        (inputs, d_proj_own, pair_own, across_qkv),
        ((0, 1, ((2, 0), (3, 0)), ((0, triple, 4, 0, 0),), ((0, triple, 5, 0, 0),)),),
        [((upper, triple), f32), ((upper, triple), bf16)],
    )

    keep_qkv, away_qkv, small, near_small, early = gate((keep_qkv, away_qkv, small, near_small, early))
    near_qkv = flip(away_qkv, 2)
    small = small + near_small
    pair_small = exchange.flip(small, exchange.bits[0])
    grad_tokens = d_inputs(d_summed, d_proj_own, d_proj_other, attn_own, attn_other, place16, 1, (early,))

    keep_qkv, near_qkv, small, pair_small, grad_tokens, keep_mid, lower_mid = gate(
        (keep_qkv, near_qkv, small, pair_small, grad_tokens, keep_mid, lower_mid)
    )
    sum_mid = keep_mid + received(lower_mid)
    sum_qkv = exchange.scatter_far(keep_qkv + received(near_qkv))
    small = exchange.total_rest(small + pair_small)

    query_bias, value_bias = small[0, :width], small[0, width:]
    rows = inner_width // model
    inner_bias_sum = small[1 : 1 + rows].reshape(-1)
    rest = [small[1 + rows + index] for index in range(6)]

    return (
        mixed,
        grad_tokens,
        sum_qkv[:, :width],
        sum_qkv[:, width : 2 * width],
        sum_qkv[:, 2 * width :],
        sum_mid[:, inner_width:].T,
        sum_mid[:, :inner_width],
        sum_outer.T,
        query_bias,
        value_bias,
        rest[0],
        rest[1],
        rest[2],
        inner_bias_sum,
        rest[3],
        rest[4],
        rest[5],
    )


def solution(mesh):
    both = P(("fsdp", "tp"), None)
    cols, rows = P("fsdp", "tp"), P("tp", "fsdp")
    return jax.shard_map(
        shards,
        mesh=mesh,
        in_specs=(both, P("fsdp"), both, cols, cols, cols, rows, cols, rows)
        + (P("tp"), P("tp"), P(), P(), P(), P("tp"), P(), P(), P()),
        out_specs=(both, both, cols, cols, cols, rows, cols, rows)
        + (P("tp"), P("tp"), P(), P(), P(), P("tp"), P(), P(), P()),
        check_vma=False,
    )
```

```python
import functools

import jax
import jax.numpy as jnp
import numpy as np
from jax import lax
from jax.experimental import pallas as pl
from jax.experimental.pallas import tpu as pltpu
from jax.sharding import PartitionSpec as P

DH = 64
SEQ = 512
PAIR = 2 * DH
norm_eps = 1e-12
masked_score = -1000000000.0
bf16 = jnp.bfloat16
f32 = jnp.float32
TILE = 256
COST = dict(
    attend_forward=39,
    attend_backward=0.02,
    attention_out=12,
    hidden=25.5,
    turn=39,
    d_hidden=10.8,
    d_attention=30,
    d_context=20,
    d_inputs=0.02,
    join=3,
    order=3,
    send_grads=0.02,
    keep_grads=10.5,
)


def cost(micros):
    return pl.CostEstimate(flops=int(micros * 9e8), bytes_accessed=1024, transcendentals=0)


def dot_nn(left, right):
    return lax.dot_general(left, right, (((1,), (0,)), ((), ())), preferred_element_type=f32)


def dot_nt(left, right):
    return lax.dot_general(left, right, (((1,), (1,)), ((), ())), preferred_element_type=f32)


def dot_tn(left, right):
    return lax.dot_general(left, right, (((0,), (0,)), ((), ())), preferred_element_type=f32)


ERF_P = 0.3275911
ERF_A = (0.254829592, -0.284496736, 1.421413741, -1.453152027, 1.061405429)


def gelu_parts(values):
    size = jnp.abs(values)
    t = 1.0 / (1.0 + (ERF_P * 2**-0.5) * size)
    expo = jnp.exp(-0.5 * values * values)
    poly = ERF_A[4]
    for coefficient in ERF_A[3::-1]:
        poly = poly * t + coefficient
    tail = (0.5 * poly) * (t * expo)
    phi = jnp.where(values < 0, tail, 1.0 - tail)
    return values * phi, phi + values * (expo * (2 * np.pi) ** -0.5)


def norm_parts(values):
    centred = values - jnp.mean(values, axis=-1, keepdims=True)
    scale = lax.rsqrt(jnp.mean(centred * centred, axis=-1, keepdims=True) + norm_eps)
    return centred * scale, scale


def norm_pull(grads, gain, normal, scale):
    inner = grads * gain
    return scale * (
        inner
        - jnp.mean(inner, axis=-1, keepdims=True)
        - normal * jnp.mean(inner * normal, axis=-1, keepdims=True)
    )


def fill(ref, column, pieces, start, width):
    part = pieces[0].shape[0]
    step = 32 if part % 32 == 0 else part
    for index, piece in enumerate(pieces):

        def one(at, carry, piece=piece, base=index * part):
            rows = pl.ds(pl.multiple_of(at * step, step), step)
            to = pl.ds(pl.multiple_of(base + at * step, step), step)
            ref[to, column : column + width] = piece[rows, start : start + width]
            return carry

        lax.fori_loop(0, part // step, one, 0)


def head_slice(block, head):
    return block[:, head * DH : (head + 1) * DH]


def live_rows(lengths_ref):
    rows = lax.broadcasted_iota(jnp.int32, (SEQ, 1), 0)
    return rows < lengths_ref[pl.program_id(0)]


def attend_forward_kernel(
    pairs, lengths_ref, inputs_ref, a_ref, b_ref, c_ref, d_ref, shift_ref, qkv_ref, context_ref, lse_ref, weight_ref
):
    live = live_rows(lengths_ref)
    width = pairs * PAIR

    @pl.when(pl.program_id(0) == 0)
    def _():
        fill(weight_ref, 0, (a_ref, b_ref, c_ref, d_ref), 0, 3 * width)

    qkv_ref[...] = (dot_nn(inputs_ref[...], weight_ref[...]) + shift_ref[...]).astype(bf16)

    def one_pair(index, carry):
        at = pl.multiple_of(index * PAIR, PAIR)
        query = qkv_ref[:, pl.ds(at, PAIR)] * jnp.asarray(DH ** (-0.5), bf16)
        keys = qkv_ref[:, pl.ds(width + at, PAIR)]
        values = qkv_ref[:, pl.ds(2 * width + at, PAIR)]
        turned = []
        for head in range(2):
            scores = dot_nt(head_slice(keys, head), head_slice(query, head))
            scores = jnp.where(live, scores, masked_score)
            top = jnp.max(scores, axis=0, keepdims=True)
            expo = jnp.exp(scores - top)
            total = jnp.sum(expo, axis=0, keepdims=True)
            probs = (expo * (1.0 / total)).astype(bf16)
            turned.append(dot_tn(head_slice(values, head), probs))
            lse_ref[0, pl.ds(index * 2 + head, 1), :] = top + jnp.log(total)
        context_ref[:, pl.ds(at, PAIR)] = jnp.concatenate(turned, axis=0).T.astype(bf16)
        return carry

    lax.fori_loop(0, pairs, one_pair, 0)


def attend_forward(inputs, pieces, shift, lengths):
    rows, model = inputs.shape
    part, _ = pieces[0].shape
    triple = shift.shape[0]
    width = triple // 3
    seqs, pairs = rows // SEQ, width // PAIR
    heads = 2 * pairs
    piece_spec = pl.BlockSpec((part, triple), lambda s, n: (0, 0), pipeline_mode=pl.Buffered(1))
    return pl.pallas_call(
        functools.partial(attend_forward_kernel, pairs),
        grid_spec=pltpu.PrefetchScalarGridSpec(
            num_scalar_prefetch=1,
            grid=(seqs,),
            in_specs=[pl.BlockSpec((SEQ, model), lambda s, n: (s, 0))]
            + [piece_spec] * 4
            + [pl.BlockSpec((1, triple), lambda s, n: (0, 0))],
            out_specs=[
                pl.BlockSpec((SEQ, triple), lambda s, n: (s, 0)),
                pl.BlockSpec((SEQ, width), lambda s, n: (s, 0)),
                pl.BlockSpec((1, heads, SEQ), lambda s, n: (s, 0, 0)),
            ],
            scratch_shapes=[pltpu.VMEM((model, triple), bf16)],
        ),
        out_shape=[
            jax.ShapeDtypeStruct((rows, triple), bf16),
            jax.ShapeDtypeStruct((rows, width), bf16),
            jax.ShapeDtypeStruct((seqs, heads, SEQ), f32),
        ],
        compiler_params=pltpu.CompilerParams(vmem_limit_bytes=18 << 20),
        cost_estimate=cost(COST["attend_forward"]),
        name="attend_forward",
    )(lengths, inputs, *pieces, shift[None, :])


def attend_backward_kernel(pairs, lengths_ref, qkv_ref, context_ref, d_context_ref, lse_ref, out_ref, sums_ref):
    live = live_rows(lengths_ref)

    @pl.when(pl.program_id(0) == 0)
    def _():
        sums_ref[...] = jnp.zeros_like(sums_ref)

    width = pairs * PAIR
    scale = DH ** (-0.5)

    def one_pair(index, carry):
        at = pl.multiple_of(index * PAIR, PAIR)
        query = qkv_ref[:, pl.ds(at, PAIR)] * jnp.asarray(scale, bf16)
        keys = qkv_ref[:, pl.ds(width + at, PAIR)]
        values = qkv_ref[:, pl.ds(2 * width + at, PAIR)]
        d_context = d_context_ref[:, pl.ds(at, PAIR)]
        weighed = (context_ref[:, pl.ds(at, PAIR)].astype(f32) * d_context.astype(f32)).T
        d_query, d_key, d_value = [], [], []
        for head in range(2):
            q_h, k_h, v_h = head_slice(query, head), head_slice(keys, head), head_slice(values, head)
            g_h = head_slice(d_context, head)
            row_dot = jnp.sum(weighed[head * DH : (head + 1) * DH], axis=0, keepdims=True)
            scores = jnp.where(live, dot_nt(k_h, q_h), masked_score)
            probs = jnp.exp(scores - lse_ref[0, pl.ds(index * 2 + head, 1), :])
            d_probs = dot_nt(v_h, g_h)
            d_scores = (probs * (d_probs - row_dot)).astype(bf16)
            d_value.append(dot_nn(probs.astype(bf16), g_h))
            d_key.append(dot_nn(d_scores, q_h))
            d_query.append(dot_tn(k_h, d_scores))
        turned = (jnp.concatenate(d_query, axis=0).T * scale).astype(bf16)
        d_value = jnp.concatenate(d_value, axis=1).astype(bf16)
        out_ref[:, pl.ds(at, PAIR)] = turned
        out_ref[:, pl.ds(width + at, PAIR)] = jnp.concatenate(d_key, axis=1).astype(bf16)
        out_ref[:, pl.ds(2 * width + at, PAIR)] = d_value
        sums_ref[0:1, pl.ds(at, PAIR)] += jnp.sum(turned.astype(f32), axis=0, keepdims=True)
        sums_ref[1:2, pl.ds(at, PAIR)] += jnp.sum(d_value.astype(f32), axis=0, keepdims=True)
        return carry

    lax.fori_loop(0, pairs, one_pair, 0)


def attend_backward(qkv, context, d_context, lse, lengths):
    rows, triple = qkv.shape
    width = triple // 3
    seqs, pairs = rows // SEQ, width // PAIR
    heads = 2 * pairs
    return pl.pallas_call(
        functools.partial(attend_backward_kernel, pairs),
        grid_spec=pltpu.PrefetchScalarGridSpec(
            num_scalar_prefetch=1,
            grid=(seqs,),
            in_specs=[
                pl.BlockSpec((SEQ, triple), lambda s, n: (s, 0)),
                pl.BlockSpec((SEQ, width), lambda s, n: (s, 0)),
                pl.BlockSpec((SEQ, width), lambda s, n: (s, 0)),
                pl.BlockSpec((1, heads, SEQ), lambda s, n: (s, 0, 0)),
            ],
            out_specs=[
                pl.BlockSpec((SEQ, triple), lambda s, n: (s, 0)),
                pl.BlockSpec((8, width), lambda s, n: (0, 0)),
            ],
        ),
        out_shape=[jax.ShapeDtypeStruct((rows, triple), bf16), jax.ShapeDtypeStruct((8, width), f32)],
        compiler_params=pltpu.CompilerParams(vmem_limit_bytes=14 << 20),
        cost_estimate=cost(COST["attend_backward"]),
        name="attend_backward",
    )(lengths, qkv, context, d_context, lse)


def in_vmem(kernel, name, limit, outs, *args, scratch=(), aliases=None):
    return pl.pallas_call(
        kernel,
        in_specs=[pl.BlockSpec(memory_space=pltpu.VMEM)] * len(args),
        out_specs=[pl.BlockSpec(memory_space=pltpu.VMEM)] * len(outs),
        out_shape=[jax.ShapeDtypeStruct(*out) for out in outs],
        scratch_shapes=[pltpu.VMEM(shape, bf16) for shape in scratch],
        input_output_aliases=aliases or {},
        compiler_params=pltpu.CompilerParams(vmem_limit_bytes=limit << 20),
        cost_estimate=cost(COST[name]),
        name=name,
    )(*args)


def tiles_of(ref, body):
    def one(index, carry):
        body(pl.ds(pl.multiple_of(index * TILE, TILE), TILE))
        return carry

    lax.fori_loop(0, ref.shape[0] // TILE, one, 0)


def add_sums(ref, row, values):
    ref[row : row + 1, :] += jnp.sum(values, axis=0, keepdims=True)


def side(one, other):
    return jnp.concatenate([one, other], axis=1)


def join_kernel(*refs):
    *pieces, out_ref = refs
    fill(out_ref, 0, pieces, 0, out_ref.shape[1])


def join(arrays):
    if len(arrays) == 1:
        return arrays[0]
    rows, width = arrays[0].shape
    if rows % 16:
        return jnp.concatenate(arrays, axis=0)
    return in_vmem(join_kernel, "join", 8, [((len(arrays) * rows, width), arrays[0].dtype)], *arrays)[0]


def exact_dot(dot, vectors, place):
    parts, left = [], vectors
    for _ in range(3):
        part = left.astype(bf16).astype(f32)
        parts.append(part)
        left = left - part
    count = vectors.shape[0]
    result = dot(jnp.concatenate(parts, axis=0).astype(bf16), place)
    return result[:count] + result[count : 2 * count] + result[2 * count :]


def order_kernel(rows_ref, vectors_ref, place_ref, out_ref, ordered_ref):
    ordered_ref[...] = exact_dot(dot_nn, vectors_ref[...], place_ref[...])

    def body(at):
        out_ref[at] = dot_nn(rows_ref[at], place_ref[...]).astype(bf16)

    tiles_of(rows_ref, body)


def order(rows, vectors, place):
    outs = [(rows.shape, bf16), (vectors.shape, f32)]
    return in_vmem(order_kernel, "order", 8, outs, rows, vectors, place)


def small_kernel(one_ref, two_ref, qkv_ref, inner_ref, place_ref, out_ref):
    whole = exact_dot(dot_nt, jnp.concatenate([one_ref[...], two_ref[...]], axis=0), place_ref[...])
    model = out_ref.shape[1]
    rows = inner_ref.shape[1] // model
    out_ref[...] = jnp.zeros_like(out_ref)
    out_ref[0:1] = side(qkv_ref[0:1], qkv_ref[1:2])
    for index in range(rows):
        out_ref[1 + index : 2 + index] = inner_ref[0:1, index * model : (index + 1) * model]
    out_ref[1 + rows : 4 + rows] = whole[:3]
    out_ref[4 + rows : 7 + rows] = whole[8:11]


def small_sums(one, two, qkv, inner, place):
    return in_vmem(small_kernel, "order", 8, [((16, place.shape[0]), f32)], one, two, qkv, inner, place)[0]


def attention_out_kernel(own_ref, other_ref, *refs):
    pieces, (inputs_ref, vectors_ref, normal_ref, scale_ref, normed_ref, weight_ref) = refs[:8], refs[8:]
    width = own_ref.shape[1]
    fill(weight_ref, 0, pieces[:4], 3 * width, width)
    fill(weight_ref, width, pieces[4:], 3 * width, width)

    def body(at):
        mixed = dot_nt(side(own_ref[at], other_ref[at]), weight_ref[...])
        normal, scale = norm_parts(mixed + vectors_ref[0:1] + inputs_ref[at].astype(f32))
        normal_ref[at] = normal
        scale_ref[at] = scale
        normed_ref[at] = (normal * vectors_ref[1:2] + vectors_ref[2:3]).astype(bf16)

    tiles_of(own_ref, body)


def attention_out(own, other, w_own, w_other, inputs, vectors):
    shape = inputs.shape
    outs = [(shape, f32), ((shape[0], 1), f32), (shape, bf16)]
    args = (own, other, *w_own, *w_other, inputs, vectors)
    return in_vmem(attention_out_kernel, "attention_out", 6, outs, *args, scratch=[(shape[1], shape[1])])


def hidden_kernel(normed_ref, *refs):
    pieces, (shift_ref, hidden_ref, slope_ref, weight_ref) = refs[:4], refs[4:]
    fill(weight_ref, 0, pieces, 0, weight_ref.shape[1])

    def body(at):
        hidden, slope = gelu_parts(dot_nn(normed_ref[at], weight_ref[...]) + shift_ref[...])
        hidden_ref[at] = hidden.astype(bf16)
        slope_ref[at] = slope.astype(bf16)

    tiles_of(normed_ref, body)


def hidden_parts(normed, w, shift):
    rows, model = normed.shape
    shape = (rows, w[0].shape[1])
    outs = [(shape, bf16), (shape, bf16)]
    args = (normed, *w, shift[None, :])
    return in_vmem(hidden_kernel, "hidden", 8, outs, *args, scratch=[(model, shape[1])])


def turn_kernel(own_ref, other_ref, *refs):
    pieces, (normal_one_ref, cotan_ref, vectors_ref, place_ref) = refs[:8], refs[8:12]
    mixed_ref, d_before_ref, d_ffn_ref, sums_ref, w_own_ref, w_other_ref = refs[12:]
    sums_ref[...] = jnp.zeros_like(sums_ref)
    fill(w_own_ref, 0, pieces[:4], 0, w_own_ref.shape[1])
    fill(w_other_ref, 0, pieces[4:], 0, w_other_ref.shape[1])

    def body(at):
        ffn = dot_nt(own_ref[at], w_own_ref[...]) + dot_nt(other_ref[at], w_other_ref[...])
        normed = normal_one_ref[at] * vectors_ref[1:2] + vectors_ref[2:3]
        normal, scale = norm_parts(ffn + vectors_ref[3:4] + normed)
        result = (normal * vectors_ref[4:5] + vectors_ref[5:6]).astype(bf16)
        mixed_ref[at] = dot_nt(result, place_ref[...]).astype(bf16)
        cotan = cotan_ref[at].astype(f32)
        d_before = norm_pull(cotan, vectors_ref[4:5], normal, scale)
        d_before_ref[at] = d_before
        d_ffn_ref[at] = d_before.astype(bf16)
        add_sums(sums_ref, 0, d_before)
        add_sums(sums_ref, 1, cotan * normal)
        add_sums(sums_ref, 2, cotan)

    tiles_of(own_ref, body)


def turn(own, other, w_own, w_other, normal_one, cotan, vectors, place):
    shape = normal_one.shape
    outs = [(shape, bf16), (shape, f32), (shape, bf16), ((8, shape[1]), f32)]
    args = (own, other, *w_own, *w_other, normal_one, cotan, vectors, place)
    scratch = [(shape[1], own.shape[1])] * 2
    return in_vmem(turn_kernel, "turn", 10, outs, *args, scratch=scratch, aliases={11: 2})


def d_hidden_kernel(d_ffn_ref, *refs):
    pieces, (slope_ref, d_inner_ref, sums_ref, weight_ref) = refs[:4], refs[4:]
    sums_ref[...] = jnp.zeros_like(sums_ref)
    fill(weight_ref, 0, pieces, 0, weight_ref.shape[1])

    def body(at):
        d_inner = (dot_nn(d_ffn_ref[at], weight_ref[...]) * slope_ref[at].astype(f32)).astype(bf16)
        d_inner_ref[at] = d_inner
        add_sums(sums_ref, 0, d_inner.astype(f32))

    tiles_of(d_ffn_ref, body)


def d_hidden(d_ffn, w, slope):
    outs = [(slope.shape, bf16), ((8, slope.shape[1]), f32)]
    args = (d_ffn, *w, slope)
    scratch = [(d_ffn.shape[1], slope.shape[1])]
    return in_vmem(d_hidden_kernel, "d_hidden", 8, outs, *args, scratch=scratch, aliases={5: 0})


def d_attention_kernel(own_ref, other_ref, *refs):
    pieces, (d_before_ref, normal_ref, scale_ref, vectors_ref) = refs[:8], refs[8:12]
    d_summed_ref, d_attn_ref, sums_ref, w_own_ref, w_other_ref = refs[12:]
    sums_ref[...] = jnp.zeros_like(sums_ref)
    fill(w_own_ref, 0, pieces[:4], 0, w_own_ref.shape[1])
    fill(w_other_ref, 0, pieces[4:], 0, w_other_ref.shape[1])

    def body(at):
        d_normed = d_before_ref[at] + dot_nt(own_ref[at], w_own_ref[...]) + dot_nt(other_ref[at], w_other_ref[...])
        normal = normal_ref[at]
        d_summed = norm_pull(d_normed, vectors_ref[1:2], normal, scale_ref[at])
        d_summed_ref[at] = d_summed
        d_attn_ref[at] = d_summed.astype(bf16)
        add_sums(sums_ref, 0, d_summed)
        add_sums(sums_ref, 1, d_normed * normal)
        add_sums(sums_ref, 2, d_normed)

    tiles_of(own_ref, body)


def d_attention(own, other, w_own, w_other, d_before, normal, scale, vectors):
    shape = d_before.shape
    outs = [(shape, f32), (shape, bf16), ((8, shape[1]), f32)]
    args = (own, other, *w_own, *w_other, d_before, normal, scale, vectors)
    scratch = [(shape[1], own.shape[1])] * 2
    return in_vmem(d_attention_kernel, "d_attention", 10, outs, *args, scratch=scratch, aliases={10: 0})


def d_context_kernel(d_attn_ref, *refs):
    pieces, (own_ref, other_ref, weight_ref) = refs[:8], refs[8:]
    width = own_ref.shape[1]
    fill(weight_ref, 0, pieces[:4], 3 * width, width)
    fill(weight_ref, width, pieces[4:], 3 * width, width)

    def body(at):
        result = dot_nn(d_attn_ref[at], weight_ref[...]).astype(bf16)
        own_ref[at] = result[:, :width]
        other_ref[at] = result[:, width:]

    tiles_of(d_attn_ref, body)


def d_context(d_attn, w_own, w_other):
    rows, model = d_attn.shape
    outs = [((rows, model // 2), bf16)] * 2
    return in_vmem(d_context_kernel, "d_context", 5, outs, d_attn, *w_own, *w_other, scratch=[(model, model)])


def d_inputs_kernel(d_summed_ref, own_ref, other_ref, *refs):
    pieces, place_ref, (out_ref, weight_ref) = refs[:8], refs[8], refs[-2:]
    triple = own_ref.shape[1]

    @pl.when(pl.program_id(0) == 0)
    def _():
        fill(weight_ref, 0, pieces[:4], 0, triple)
        fill(weight_ref, triple, pieces[4:], 0, triple)

    grads = d_summed_ref[...] + dot_nt(side(own_ref[...], other_ref[...]), weight_ref[...])
    high = grads.astype(bf16)
    low = (grads - high.astype(f32)).astype(bf16)
    out_ref[...] = dot_nt(high, place_ref[...]) + dot_nt(low, place_ref[...])


def d_inputs(d_summed, own, other, w_own, w_other, place, half, earlier=()):
    rows, model = d_summed.shape
    part, triple = w_own[0].shape[0], own.shape[1]
    steps = rows // 2 // TILE

    def tile(width):
        return pl.BlockSpec((TILE, width), lambda i: (i + half * steps, 0))

    def fixed(shape):
        return pl.BlockSpec(shape, lambda i: (0, 0), pipeline_mode=pl.Buffered(1))

    args = (d_summed, own, other, *w_own, *w_other, place)
    return pl.pallas_call(
        d_inputs_kernel,
        grid=(steps,),
        in_specs=[tile(model), tile(triple), tile(triple)]
        + [fixed((part, triple))] * 8
        + [fixed(place.shape)]
        + [pl.BlockSpec(memory_space=pl.ANY)] * len(earlier),
        out_specs=tile(model),
        out_shape=jax.ShapeDtypeStruct((rows, model), f32),
        scratch_shapes=[pltpu.VMEM((model, 2 * triple), bf16)],
        input_output_aliases={len(args): 0} if earlier else {},
        compiler_params=pltpu.CompilerParams(vmem_limit_bytes=18 << 20),
        cost_estimate=cost(COST["d_inputs"]),
        name="d_inputs",
    )(*args, *earlier)


def chunks(width):
    step = next(step for step in (512, 384, 256, 128) if width % step == 0)
    return [(start, step) for start in range(0, width, step)]


def send_kernel(left_ref, *refs):
    *rights, out_ref = refs
    half = left_ref.shape[1] // 2
    left = left_ref[:, half:]
    base = 0
    for right_ref in rights:
        for start, step in chunks(right_ref.shape[1]):
            part = dot_tn(left, right_ref[:, start : start + step])
            out_ref[:, base + start : base + start + step] = part.astype(bf16)
        base += right_ref.shape[1]


def send_grads(left, *rights):
    outs = [((left.shape[1] // 2, sum(right.shape[1] for right in rights)), bf16)]
    return in_vmem(send_kernel, "send_grads", 5, outs, left, *rights)[0]


def keep_kernel(terms, *refs):
    for left_at, right_at, adds, upper, lower in terms:
        left_ref, right_ref = refs[left_at], refs[right_at]
        half = left_ref.shape[1] // 2
        left = left_ref[:, :half]
        for start, step in chunks(right_ref.shape[1]):
            total = dot_tn(left, right_ref[:, start : start + step])
            for add_at, column in adds:
                total = total + refs[add_at][:, column + start : column + start + step].astype(f32)
            for part, places in ((total[: half // 2], upper), (total[half // 2 :], lower)):
                for first, last, out_at, row, column in places:
                    if first <= start < last:
                        out_ref = refs[out_at]
                        to = column + start - first
                        out_ref[row : row + half // 2, to : to + step] = part.astype(out_ref.dtype)


def keep_grads(args, terms, outs):
    return in_vmem(functools.partial(keep_kernel, terms), "keep_grads", 8, outs, *args)


class Exchange:
    def __init__(self, fsdp):
        self.fsdp = fsdp
        bits = [1 << i for i in range(2, fsdp.bit_length() - 1)]
        self.bits, self.far = bits, []
        for i in range(0, len(bits), 2):
            steps = [0]
            for bit in bits[i : i + 2]:
                steps = steps + [step ^ bit for step in steps]
            self.far.append(steps)
        self.masks = [0]
        for steps in self.far + [[0, 2], [0, 1]]:
            self.masks = [step ^ mask for step in steps for mask in self.masks]

    def flip(self, array, bit):
        return lax.ppermute(array, "fsdp", [(i, i ^ bit) for i in range(self.fsdp)])

    def cross(self, array):
        return lax.ppermute(array, "tp", [(0, 1), (1, 0)])

    def flip_cross(self, array, bit):
        pairs = [(2 * i + j, 2 * (i ^ bit) + 1 - j) for i in range(self.fsdp) for j in range(2)]
        return lax.ppermute(array, ("fsdp", "tp"), pairs)

    def gather_far(self, array):
        for steps in self.far[:-1]:
            array = join([array] + [self.flip(array, step) for step in steps[1:]])
        return [array] + [self.flip(array, step) for step in self.far[-1][1:]]

    def scatter_far(self, array):
        for steps in reversed(self.far):
            size = array.shape[0] // len(steps)
            parts = [array[i * size : (i + 1) * size] for i in range(len(steps))]
            array = parts[0]
            for part, step in zip(parts[1:], steps[1:]):
                array = array + self.flip(part.astype(bf16), step).astype(f32)
        return array

    def halve(self, parts, bit):
        away = self.flip(jnp.concatenate(parts[1::2], axis=0).astype(bf16), bit)
        size = parts[0].shape[0]
        return parts[::2], [away[at : at + size] for at in range(0, away.shape[0], size)]

    def halve_first(self, array):
        size = array.shape[0] >> len(self.bits)
        return self.halve([array[at : at + size] for at in range(0, array.shape[0], size)], self.bits[0])

    def halve_rest(self, keep, away):
        for bit in self.bits[1:]:
            keep, away = self.halve([mine + theirs.astype(f32) for mine, theirs in zip(keep, away)], bit)
        return keep[0], away[0]

    def total_rest(self, array):
        for bit in self.bits[1:]:
            array = array + self.flip(array, bit)
        return array


def gate(values, *others):
    return lax.optimization_barrier((values, others))[0]


def shards(
    tokens,
    lengths,
    cotangent,
    w_query,
    w_key,
    w_value,
    w_output,
    w_inner,
    w_outer,
    bias_query,
    bias_value,
    bias_output,
    norm1_gain,
    norm1_bias,
    bias_inner,
    bias_outer,
    norm2_gain,
    norm2_bias,
):
    fsdp = lax.axis_size("fsdp")
    exchange = Exchange(fsdp)
    rows, model = tokens.shape
    seqs = rows // SEQ
    block = w_query.shape[0]
    width = w_query.shape[1]
    half = model // 2

    here = lax.axis_index("fsdp")
    masks = jnp.repeat(jnp.asarray(exchange.masks, jnp.int32), block)
    inside = jnp.tile(jnp.arange(block, dtype=jnp.int32), fsdp)
    source = (here ^ masks) * block + inside
    place = jnp.arange(model, dtype=jnp.int32)[:, None] == source[None, :]
    place16 = place.astype(bf16)
    lengths_here = lax.dynamic_slice_in_dim(lengths, lax.axis_index("tp") * seqs, seqs, 0)

    zero = jnp.zeros((width,), f32)

    def qkv_bias(biases):
        return jnp.concatenate([biases[:width], zero, biases[width : 2 * width]])

    def inner_bias(biases):
        return biases[2 * width :]

    flip, cross, flip_cross = exchange.flip, exchange.cross, exchange.flip_cross

    shard_attn = jnp.concatenate([w_query, w_key, w_value, w_output.T], axis=1).astype(bf16)
    biases_own = jnp.concatenate([bias_query, bias_value, bias_inner])
    far_attn = exchange.gather_far(shard_attn)
    biases_other = cross(biases_own)
    inputs = dot_nn(tokens, place16).astype(bf16)
    shard_inner, shard_outer = w_inner.astype(bf16), w_outer.T.astype(bf16)
    vectors = jnp.stack([bias_output, norm1_gain, norm1_bias, bias_outer, norm2_gain, norm2_bias, bias_output, bias_output])

    far_attn, shard_inner, shard_outer, biases_other, cotangent, vectors, inputs = gate(
        (far_attn, shard_inner, shard_outer, biases_other, cotangent, vectors, inputs)
    )
    far_attn = join(far_attn)
    near_attn, across_attn = flip(far_attn, 2), cross(far_attn)
    far_inner = exchange.gather_far(shard_inner)
    cotan, vectors = order(cotangent, vectors, place16)

    far_attn, near_attn, across_attn, far_inner, shard_outer, inputs = gate(
        (far_attn, near_attn, across_attn, far_inner, shard_outer, inputs), cotan, vectors
    )
    pair_far_attn, pair_near_attn, corner_attn = flip(far_attn, 1), flip(near_attn, 1), cross(near_attn)
    far_inner = join(far_inner)
    near_inner = flip(far_inner, 2)
    far_outer = exchange.gather_far(shard_outer)
    attn_own = (far_attn, near_attn, pair_far_attn, pair_near_attn)
    proj_own, context_own, lse_own = attend_forward(inputs, attn_own, qkv_bias(biases_own), lengths_here)

    across_attn, corner_attn, far_inner, near_inner, far_outer, context_own = gate(
        (across_attn, corner_attn, far_inner, near_inner, far_outer, context_own)
    )
    pair_across_attn, pair_corner_attn = flip(across_attn, 1), flip(corner_attn, 1)
    across_inner = cross(far_inner)
    far_outer = join(far_outer)
    near_outer = flip(far_outer, 2)
    attn_other = (across_attn, corner_attn, pair_across_attn, pair_corner_attn)
    proj_other, context_other, lse_other = attend_forward(inputs, attn_other, qkv_bias(biases_other), lengths_here)

    far_inner, near_inner, across_inner, far_outer, near_outer, context_other = gate(
        (far_inner, near_inner, across_inner, far_outer, near_outer, context_other)
    )
    pair_far_inner, pair_near_inner = flip(far_inner, 1), flip(near_inner, 1)
    corner_inner = flip(across_inner, 2)
    across_outer = cross(far_outer)
    normal_one, scale_one, normed16 = attention_out(context_own, context_other, attn_own, attn_other, inputs, vectors)
    inner_own = (far_inner, near_inner, pair_far_inner, pair_near_inner)
    hidden_own, slope_own = hidden_parts(normed16, inner_own, inner_bias(biases_own))

    across_inner, corner_inner, far_outer, near_outer, across_outer, normed16, hidden_own = gate(
        (across_inner, corner_inner, far_outer, near_outer, across_outer, normed16, hidden_own)
    )
    corner_outer = flip(across_outer, 2)
    pair_across_inner, pair_corner_inner = flip(across_inner, 1), flip(corner_inner, 1)
    pair_far_outer, pair_near_outer = flip(far_outer, 1), flip(near_outer, 1)
    inner_other = (across_inner, corner_inner, pair_across_inner, pair_corner_inner)
    hidden_other, slope_other = hidden_parts(normed16, inner_other, inner_bias(biases_other))

    across_outer, corner_outer, hidden_other = gate((across_outer, corner_outer, hidden_other))
    pair_across_outer, pair_corner_outer = flip(across_outer, 1), flip(corner_outer, 1)
    outer_own = (far_outer, near_outer, pair_far_outer, pair_near_outer)
    outer_other = (across_outer, corner_outer, pair_across_outer, pair_corner_outer)

    mixed, d_before, d_ffn, sums_two = turn(
        hidden_own, hidden_other, outer_own, outer_other, normal_one, cotan, vectors, place16
    )
    upper = model // 4
    inner_width = bias_inner.shape[0]

    def received(array):
        return array.astype(f32)

    send_outer = send_grads(d_ffn, hidden_own, hidden_other)

    send_outer, d_ffn = gate((send_outer, d_ffn))
    pair_outer = flip(send_outer, 1)
    d_inner_own, inner_sums_own = d_hidden(d_ffn, outer_own, slope_own)

    pair_outer, d_ffn, d_inner_own = gate((pair_outer, d_ffn, d_inner_own))
    part = (upper, inner_width)
    keep_outer, *away_outer = keep_grads(
        (d_ffn, hidden_own, hidden_other, pair_outer),
        (
            (0, 1, ((3, 0),), ((0, inner_width, 4, 0, 0),), ((0, inner_width, 5, 0, 0),)),
            (0, 2, ((3, inner_width),), ((0, inner_width, 6, 0, 0),), ((0, inner_width, 7, 0, 0),)),
        ),
        [(part, f32), (part, bf16), (part, bf16), (part, bf16)],
    )

    keep_outer, away_outer, d_ffn = gate((keep_outer, away_outer, d_ffn))
    ring_outer = (flip(away_outer[0], 2), cross(away_outer[1]), flip_cross(away_outer[2], 2))
    d_inner_other, inner_sums_other = d_hidden(d_ffn, outer_other, slope_other)
    send_inner = send_grads(normed16, d_inner_own, d_inner_other)

    send_inner, d_inner_other, normed16 = gate((send_inner, d_inner_other, normed16))
    pair_inner = flip(send_inner, 1)
    d_summed, d_attn, sums_one = d_attention(
        d_inner_own, d_inner_other, inner_own, inner_other, d_before, normal_one, scale_one, vectors
    )
    send_output = send_grads(d_attn, context_own, context_other)

    send_output, d_attn = gate((send_output, d_attn))
    pair_output = flip(send_output, 1)
    d_context_own, d_context_other = d_context(d_attn, attn_own, attn_other)

    pair_output, pair_inner, d_attn, normed16, d_context_other = gate(
        (pair_output, pair_inner, d_attn, normed16, d_context_other)
    )
    cut = 2 * inner_width // 3
    late = inner_width - cut
    rest = late + width
    args = (normed16, d_attn, d_inner_own, d_inner_other, context_own, context_other, pair_inner, pair_output)
    own_cut, own_low, other_cut, own_rest, other_rest, near_rest = range(8, 14)
    first_keep, first_low, first_away, last_keep, last_cross, last_away = keep_grads(
        args,
        (
            (
                0,
                2,
                ((6, 0),),
                ((0, cut, own_cut, 0, 0), (cut, inner_width, own_rest, 0, 0)),
                ((0, cut, own_low, 0, 0), (cut, inner_width, near_rest, 0, 0)),
            ),
            (
                0,
                3,
                ((6, inner_width),),
                ((0, cut, other_cut, 0, 0), (cut, inner_width, other_rest, 0, 0)),
                ((0, cut, other_cut, upper, 0), (cut, inner_width, near_rest, 0, rest)),
            ),
            (1, 4, ((7, 0),), ((0, width, own_rest, 0, late),), ((0, width, near_rest, 0, late),)),
            (1, 5, ((7, width),), ((0, width, other_rest, 0, late),), ((0, width, near_rest, 0, rest + late),)),
        ),
        [
            ((upper, cut), f32),
            ((upper, cut), f32),
            ((2 * upper, cut), bf16),
            ((upper, rest), f32),
            ((upper, rest), f32),
            ((upper, 2 * rest), bf16),
        ],
    )

    first_keep, first_low, first_away, last_keep, last_cross, last_away, d_context_other, keep_outer, ring_outer = gate(
        (first_keep, first_low, first_away, last_keep, last_cross, last_away, d_context_other, keep_outer, ring_outer)
    )
    first_across, last_near = cross(first_away), flip(last_away, 2)
    for piece in ring_outer:
        keep_outer = keep_outer + received(piece)
    keep_outer, lower_outer = exchange.halve_first(keep_outer)
    d_proj_other, qkv_sums_other = attend_backward(
        proj_other, context_other, d_context_other, lse_other, lengths_here
    )
    send_other = send_grads(inputs, d_proj_other)

    send_other, d_proj_other, first_across, last_near, keep_outer, lower_outer = gate(
        (send_other, d_proj_other, first_across, last_near, keep_outer, lower_outer)
    )
    pair_other = flip(send_other, 1)
    first_near = flip((first_low + received(first_across[upper:])).astype(bf16), 2)
    last_across = cross((last_cross + received(last_near[:, rest:])).astype(bf16))
    keep_outer, lower_outer = exchange.halve_rest(keep_outer, lower_outer)

    pair_other, d_proj_other, qkv_sums_other, sums_one, sums_two = gate(
        (pair_other, d_proj_other, qkv_sums_other, sums_one, sums_two)
    )
    small_other = small_sums(sums_one, sums_two, qkv_sums_other, inner_sums_other, place16)
    triple = 3 * width
    (away_other,) = keep_grads(
        (inputs, d_proj_other, pair_other),
        ((0, 1, ((2, 0),), ((0, triple, 3, 0, 0),), ((0, triple, 3, upper, 0),)),),
        [((2 * upper, triple), bf16)],
    )

    away_other, d_context_own, small_other, first_near, last_across, keep_outer, lower_outer = gate(
        (away_other, d_context_own, small_other, first_near, last_across, keep_outer, lower_outer)
    )
    sum_outer = keep_outer + received(lower_outer)
    across_qkv = cross(away_other)
    across_small = cross(small_other)
    first_keep = first_keep + received(first_across[:upper]) + received(first_near)
    last_keep = last_keep + received(last_near[:, :rest]) + received(last_across)
    keep_mid, lower_mid = exchange.halve_first(jnp.concatenate([first_keep, last_keep], axis=1))
    d_proj_own, qkv_sums_own = attend_backward(proj_own, context_own, d_context_own, lse_own, lengths_here)
    send_own = send_grads(inputs, d_proj_own)
    early = d_inputs(d_summed, d_proj_own, d_proj_other, attn_own, attn_other, place16, 0)

    send_own, d_proj_own, qkv_sums_own, across_small, across_qkv, early, keep_mid, lower_mid = gate(
        (send_own, d_proj_own, qkv_sums_own, across_small, across_qkv, early, keep_mid, lower_mid)
    )
    pair_own = flip(send_own, 1)
    small = across_small + small_sums(sums_one, sums_two, qkv_sums_own, inner_sums_own, place16)
    pair_small = flip(small, 1)
    keep_mid, lower_mid = exchange.halve_rest(keep_mid, lower_mid)

    pair_own, d_proj_own, small, pair_small = gate((pair_own, d_proj_own, small, pair_small))
    small = small + pair_small
    near_small = flip(small, 2)
    keep_qkv, away_qkv = keep_grads(
        (inputs, d_proj_own, pair_own, across_qkv),
        ((0, 1, ((2, 0), (3, 0)), ((0, triple, 4, 0, 0),), ((0, triple, 5, 0, 0),)),),
        [((upper, triple), f32), ((upper, triple), bf16)],
    )

    keep_qkv, away_qkv, small, near_small, early = gate((keep_qkv, away_qkv, small, near_small, early))
    near_qkv = flip(away_qkv, 2)
    small = small + near_small
    pair_small = exchange.flip(small, exchange.bits[0])
    grad_tokens = d_inputs(d_summed, d_proj_own, d_proj_other, attn_own, attn_other, place16, 1, (early,))

    keep_qkv, near_qkv, small, pair_small, grad_tokens, keep_mid, lower_mid = gate(
        (keep_qkv, near_qkv, small, pair_small, grad_tokens, keep_mid, lower_mid)
    )
    sum_mid = keep_mid + received(lower_mid)
    sum_qkv = exchange.scatter_far(keep_qkv + received(near_qkv))
    small = exchange.total_rest(small + pair_small)

    query_bias, value_bias = small[0, :width], small[0, width:]
    rows = inner_width // model
    inner_bias_sum = small[1 : 1 + rows].reshape(-1)
    rest = [small[1 + rows + index] for index in range(6)]

    return (
        mixed,
        grad_tokens,
        sum_qkv[:, :width],
        sum_qkv[:, width : 2 * width],
        sum_qkv[:, 2 * width :],
        sum_mid[:, inner_width:].T,
        sum_mid[:, :inner_width],
        sum_outer.T,
        query_bias,
        value_bias,
        rest[0],
        rest[1],
        rest[2],
        inner_bias_sum,
        rest[3],
        rest[4],
        rest[5],
    )


def solution(mesh):
    both = P(("fsdp", "tp"), None)
    cols, rows = P("fsdp", "tp"), P("tp", "fsdp")
    return jax.shard_map(
        shards,
        mesh=mesh,
        in_specs=(both, P("fsdp"), both, cols, cols, cols, rows, cols, rows)
        + (P("tp"), P("tp"), P(), P(), P(), P("tp"), P(), P(), P()),
        out_specs=(both, both, cols, cols, cols, rows, cols, rows)
        + (P("tp"), P("tp"), P(), P(), P(), P("tp"), P(), P(), P()),
        check_vma=False,
    )
```
